32 devices in a mesh: dp: 4 (over y, x), expert: 8 (over z, core).
Axes of the slice: x: 2, y: 2, z: 4, core: 2. Of those that a mesh axis runs over, the one named last changes fastest.
Arguments:
- layer_input: bfloat16 [16384, 1280], P(('dp', 'expert')), may hold values from -6 to 6
- lengths: int32 [32], P(('dp', 'expert')), may hold values from 256 to 512, as said below
- expert_ids: int32 [16384, 7], P(('dp', 'expert')), may hold values from 0 to 14, all different within a row; in each aligned block of 512 rows (0 to 511, 512 to 1023, ...) at most 240 rows name the same one
- norm1: float32 [1280], replicated, may hold values from 0.5 to 1.5
- w_qkv: bfloat16 [1280, 3840], replicated, may hold values from -0.15625 to 0.15625
- w_out: bfloat16 [1280, 1280], replicated, may hold values from -1.25 to 1.25
- norm2: float32 [1280], replicated, may hold values from 0.5 to 1.5
- w_router: bfloat16 [1280, 16], replicated, may hold values from -0.078125 to 0.078125
- w_shared_in: bfloat16 [1280, 1792], replicated, may hold values from -0.15625 to 0.15625
- w_shared_down: bfloat16 [896, 1280], replicated, may hold values from -0.1875 to 0.1875
- w_expert_in: bfloat16 [16, 1280, 1792], P('expert'), may hold values from -0.15625 to 0.15625
- w_expert_down: bfloat16 [16, 896, 1280], P('expert'), may hold values from -1.5 to 1.5
- dout: bfloat16 [16384, 1280], P(('dp', 'expert')), may hold values from -6 to 6
Outputs:
- out: bfloat16 [16384, 1280], P(('dp', 'expert'))
- grad_x: float32 [16384, 1280], P(('dp', 'expert'))
- grad_norm1: float32 [1280], P(('dp', 'expert'))
- grad_qkv: float32 [1280, 3840], P(('dp', 'expert'))
- grad_out: float32 [1280, 1280], P(('dp', 'expert'))
- grad_norm2: float32 [1280], P(('dp', 'expert'))
- grad_router: float32 [1280, 16], P(('dp', 'expert'))
- grad_shared_in: float32 [1280, 1792], P(('dp', 'expert'))
- grad_shared_down: float32 [896, 1280], P(None, ('dp', 'expert'))
- grad_expert_in: float32 [16, 1280, 1792], P('expert', 'dp')
- grad_expert_down: float32 [16, 896, 1280], P('expert', 'dp')
- counts: int32 [16], replicated
The draws below stay inside these ranges and needn't reach their ends.
Inputs may be any that keep to these rules, and one draw needn't show every extreme that they name: `expert_ids`: each row names 7 different routed experts. Among the rows of one sequence no expert is named more than 240 times, a bound that some block reaches. `lengths`: some sequence has exactly 512 live tokens and some exactly half of 512.
All inputs are finite; a program needn't handle non-finite values.
Results may differ from the reference program's by a relative error of at most 0.015.
Values may be sent and summed in bfloat16 or wider, within the bound.
No kernel may reach another device: no remote copies, remote signals or barrier semaphores. Data moves between devices by JAX's collectives and lax.ppermute only.
A program may use at most 384 MiB of HBM per device.

```python
import math
import jax
import jax.numpy as jnp
import numpy as np
from jax import lax

D = 1280
HEADS = 10
HEAD_DIM = 128
FF = 896
TOPK = 7
EXPERTS = 16
ROUTED = 15
SEQ = 512
NSEQ = 32
TOKENS = 16384
CAP = 240


def draw_lengths(key, part):
    first_key, second_key = jax.random.split(key)
    drawn = jax.random.randint(first_key, (NSEQ,), SEQ // 2, SEQ + 1)
    order = jax.random.permutation(second_key, NSEQ)
    drawn = jnp.where(order == 0, SEQ, drawn)
    drawn = jnp.where(order == 1, SEQ // 2, drawn)
    return drawn.astype(jnp.int32)


def block_levels(key, extent, shards, low, high):
    gain, own = 1.0, jax.random.fold_in(key, 6)
    for position, parts in shards:
        steps = jnp.exp(jax.random.uniform(jax.random.fold_in(own, position), (parts,), jnp.float32, low / len(shards), high / len(shards)))
        gain = gain * jnp.repeat(steps, extent[position] // parts).reshape([-1 if axis == position else 1 for axis in range(len(extent))])
    return gain


def deal_out(key, own, number, rows, count, top, reach, skew):
    ranking = jax.random.permutation(key, count)
    crowded, ordinary = load_shares(count, rows * top, reach, skew, True), load_shares(count, rows * top, reach, skew, False)
    places = jnp.arange(count)

    def named(sizes, rotation):
        used = int((sizes > 0).sum())
        fixed = max(1, used // 4)
        moved = fixed + (places - fixed + rotation * (used - fixed)) % max(1, count - fixed)
        return jnp.zeros((count,), jnp.int32).at[ranking[jnp.where(places < fixed, places, moved)]].set(jnp.asarray(sizes, jnp.int32))

    sizes = jnp.where(number % 4 == 0, named(crowded, number // 4), named(ordinary, number - number // 4 - 1))
    mixed = jax.random.permutation(jax.random.fold_in(own, 3), count)
    source_of, receiver = mixed[0:count // 2 * 2:2], mixed[1:count // 2 * 2:2]
    margin = jnp.minimum(sizes[source_of] - 1, reach - sizes[receiver]) // 2
    margin = jnp.where((source_of == ranking[0]) | (receiver == ranking[0]) | (sizes[receiver] == 0), 0, jnp.maximum(margin, 0))
    moved = jax.random.randint(jax.random.fold_in(own, 4), (count // 2,), 0, 1 << 20) % (margin + 1)
    sizes = sizes.at[source_of].add(-moved).at[receiver].add(moved)
    items = jnp.searchsorted(jnp.cumsum(sizes), jnp.arange(rows * top), side="right").astype(jnp.int32)
    table = items.reshape(top, rows).T
    table = table[jax.random.permutation(jax.random.fold_in(own, 1), rows)]
    rotation = jax.random.randint(jax.random.fold_in(own, 2), (rows, 1), 0, top)
    return jnp.take_along_axis(table, (jnp.arange(top)[None, :] + rotation) % top, axis=1)


def load_shares(amount, total, limit, skew, full):
    loads = [(1 << 20) // math.isqrt(standing ** skew) + 1 for standing in range(1, amount + 1)]
    largest = limit if full else min(limit, max(-(-total // amount), total * loads[0] // sum(loads)))
    least = 1 if total - largest >= amount - 1 else 0
    holding, surplus = [largest] + [least] * (amount - 1), total - largest - least * (amount - 1)
    while surplus > 0:
        free = [i for i in range(1, amount) if holding[i] < largest] or [i for i in range(1, amount) if holding[i] < limit]
        pool, budget = sum([loads[i] for i in free]), surplus
        for i in free:
            extra = min(limit - holding[i], max(1, budget * loads[i] // pool), surplus)
            holding[i] = holding[i] + extra
            surplus = surplus - extra
    return np.array(holding)


def bell_draw(stream_key, extent, width, reach, shards=(), kind=jnp.bfloat16):
    array = width * jax.random.normal(stream_key, extent, jnp.float32)
    if shards:
        array = array * block_levels(stream_key, extent, shards, -0.22, 0.18)
    return jnp.clip(array, -reach, reach).astype(kind)


def setup_inputs(seed: int = 0) -> dict:
    arg_keys = jax.random.split(jax.random.key(seed), 14)
    layer_input = bell_draw(arg_keys[0], (TOKENS, D), 1.0, 6.0, ((0, 32),))
    lengths = draw_lengths(jax.random.fold_in(arg_keys[13], 71), 0)
    expert_ids_keys = jax.random.split(jax.random.fold_in(arg_keys[2], 1), TOKENS // SEQ)
    expert_ids_turns = jax.random.permutation(jax.random.fold_in(arg_keys[2], 3), TOKENS // SEQ)
    expert_ids = jax.vmap(lambda own, number: deal_out(jax.random.fold_in(arg_keys[2], 2), own, number, SEQ, ROUTED, TOPK, CAP, 1))(expert_ids_keys, expert_ids_turns).reshape((TOKENS, TOPK))
    norm1 = jnp.clip(1.0 + 0.1 * jax.random.normal(arg_keys[3], (D,), jnp.float32), 0.5, 1.5)
    w_qkv = bell_draw(arg_keys[4], (D, 3 * D), D ** -0.5, 0.15625)
    w_out = bell_draw(arg_keys[5], (D, D), (D // 64) ** -0.5, 1.25)
    norm2 = jnp.clip(1.0 + 0.1 * jax.random.normal(arg_keys[6], (D,), jnp.float32), 0.5, 1.5)
    w_router = bell_draw(arg_keys[7], (D, EXPERTS), (4 * D) ** -0.5, 0.078125)
    w_shared_in = bell_draw(arg_keys[8], (D, 2 * FF), D ** -0.5, 0.15625)
    w_shared_down = bell_draw(arg_keys[9], (FF, D), FF ** -0.5, 0.1875)
    w_expert_in = bell_draw(arg_keys[10], (EXPERTS, D, 2 * FF), D ** -0.5, 0.15625, ((0, 8),))
    w_expert_down = bell_draw(arg_keys[11], (EXPERTS, FF, D), (max(1, 4 * FF // (ROUTED * ROUTED))) ** -0.5, 1.5, ((0, 8),))
    dout = bell_draw(arg_keys[12], (TOKENS, D), 1.0, 6.0, ((0, 32),))
    return {"layer_input": layer_input, "lengths": lengths, "expert_ids": expert_ids, "norm1": norm1, "w_qkv": w_qkv, "w_out": w_out, "norm2": norm2, "w_router": w_router, "w_shared_in": w_shared_in, "w_shared_down": w_shared_down, "w_expert_in": w_expert_in, "w_expert_down": w_expert_down, "dout": dout}


NORM_EPS = 1e-06
MASK_VALUE = -1e+30
HIGHEST_PREC = lax.Precision.HIGHEST

@jax.custom_vjp
def low(v):
    return lax.optimization_barrier(v.astype(jnp.bfloat16)).astype(jnp.float32)

@jax.custom_vjp
def low_back(v):
    return v

def low_keep(v):
    return (low(v), None)

def low_pass(kept, grad):
    return (grad,)

def back_keep(v):
    return (v, None)

def back_low(kept, grad):
    return (low(grad),)
low.defvjp(low_keep, low_pass)
low_back.defvjp(back_keep, back_low)

def silu(values_in):
    return values_in * jax.nn.sigmoid(values_in)

def rms_norm(values_in, gain_vec):
    inverse = lax.rsqrt(lax.optimization_barrier(jnp.mean(values_in * values_in, axis=-1, keepdims=True)) + NORM_EPS)
    return values_in * inverse * gain_vec

def rope_tables(seq_slots, head_width):
    half_dim = head_width // 2
    inv_freq = 1.0 / 10000.0 ** (jnp.arange(half_dim, dtype=jnp.float32) * 2.0 / head_width)
    angles = jnp.arange(seq_slots, dtype=jnp.float32)[:, None] * inv_freq[None, :]
    return (jnp.cos(angles)[:, None, :], jnp.sin(angles)[:, None, :])

def rotate(values_in, cosine, sine_t):
    half_dim = values_in.shape[-1] // 2
    first_half = values_in[..., :half_dim]
    second_half = values_in[..., half_dim:]
    return jnp.concatenate([first_half * cosine - second_half * sine_t, first_half * sine_t + second_half * cosine], axis=-1)

def softmax_rows(scores):
    highest = lax.optimization_barrier(jnp.max(scores, axis=-1, keepdims=True))
    weights_exp = jnp.exp(scores - highest)
    return weights_exp / lax.optimization_barrier(jnp.sum(weights_exp, axis=-1, keepdims=True))

def attend(group_in):
    queries, keys_in, values_in, group_lengths = group_in
    seq_slots = queries.shape[1]
    scores = jnp.einsum('gqhd,gkhd->ghqk', queries, keys_in, precision=HIGHEST_PREC) * queries.shape[-1] ** (-0.5)
    scores = low_back(scores)
    query_pos = jnp.arange(seq_slots, dtype=jnp.int32)[:, None]
    key_pos = jnp.arange(seq_slots, dtype=jnp.int32)[None, :]
    allowed = (key_pos <= query_pos)[None, None] & (key_pos[None, None] < group_lengths[:, None, None, None])
    scores = jnp.where(allowed, scores, MASK_VALUE)
    return jnp.einsum('ghqk,gkhd->gqhd', low(softmax_rows(scores)), values_in, precision=HIGHEST_PREC)

def reference(layer_input, lengths, expert_ids, norm1, w_qkv, w_out, norm2, w_router, w_shared_in, w_shared_down, w_expert_in, w_expert_down, dout):
    num_seqs = lengths.shape[0]
    tokens = num_seqs * SEQ
    positions = jnp.arange(SEQ, dtype=jnp.int32)
    live_mask = positions[None, :] < lengths[:, None]
    live_col = live_mask.reshape(tokens, 1).astype(jnp.float32)
    flat_ids = expert_ids.reshape(num_seqs, SEQ * TOPK)
    live_flat = jnp.repeat(live_mask, TOPK, axis=1)
    pick_table = ((flat_ids[:, :, None] == jnp.arange(EXPERTS, dtype=jnp.int32)[None, None, :]) & live_flat[:, :, None]).astype(jnp.int32)
    slot_rank = lax.optimization_barrier(jnp.sum((jnp.cumsum(pick_table, axis=1) - pick_table) * pick_table, axis=-1))
    counts = lax.optimization_barrier(jnp.sum(pick_table, axis=(0, 1))).astype(jnp.int32)
    seq_index = jnp.arange(num_seqs, dtype=jnp.int32)[:, None]
    per_expert = num_seqs * CAP
    gather_index = jnp.where(live_flat, flat_ids * per_expert + seq_index * CAP + slot_rank, EXPERTS * per_expert).reshape(-1).astype(jnp.int32)
    token_index = (seq_index * SEQ + jnp.arange(SEQ * TOPK, dtype=jnp.int32)[None, :] // TOPK).reshape(-1).astype(jnp.int32)
    source_rows = jnp.full((EXPERTS * per_expert,), tokens, jnp.int32).at[gather_index].set(token_index, mode='drop').reshape(EXPERTS, per_expert)
    cosine, sine_t = rope_tables(SEQ, HEAD_DIM)
    group_size = math.gcd(num_seqs, max(1, 4096 // SEQ))
    group_count = num_seqs // group_size
    router_cols = jnp.arange(EXPERTS, dtype=jnp.int32) < ROUTED

    def forward(x_full, gain_one, weight_qkv, weight_out, gain_two, weight_router, weight_shared_in, weight_shared_down, weight_expert_in, weight_expert_down):
        h1 = low(rms_norm(x_full, gain_one))
        proj_qkv = low_back(jnp.dot(h1, weight_qkv, precision=HIGHEST_PREC))
        proj_qkv = proj_qkv.reshape(group_count, group_size, SEQ, 3, HEADS, HEAD_DIM)
        queries = low(rotate(proj_qkv[..., 0, :, :], cosine, sine_t))
        keys_in = low(rotate(proj_qkv[..., 1, :, :], cosine, sine_t))
        values_in = low(proj_qkv[..., 2, :, :])
        attended = lax.map(jax.checkpoint(attend), (queries, keys_in, values_in, lengths.reshape(group_count, group_size)))
        attended = low(low_back(attended.reshape(tokens, D)))
        branch = low_back(jnp.dot(attended, weight_out, precision=HIGHEST_PREC))
        x_mid = x_full + live_col * branch
        h2_full = rms_norm(x_mid, gain_two)
        h2_low = low(h2_full)
        logits = low_back(jnp.dot(h2_low, weight_router, precision=HIGHEST_PREC))
        logits = jnp.where(router_cols[None, :], logits, MASK_VALUE)
        router_probs = softmax_rows(logits)
        gates = jnp.take_along_axis(router_probs, expert_ids, axis=1)
        shared_gu = low_back(jnp.dot(h2_low, weight_shared_in, precision=HIGHEST_PREC))
        shared_hidden = low(silu(shared_gu[:, :FF]) * shared_gu[:, FF:])
        shared_out = jnp.dot(shared_hidden, weight_shared_down, precision=HIGHEST_PREC)

        def expert_block(item):
            rows_index, weight_in, weight_down = item
            slot_rows = low(low_back(jnp.take(h2_full, rows_index, axis=0, mode='fill', fill_value=0.0)))
            gate_up = low_back(jnp.dot(slot_rows, weight_in, precision=HIGHEST_PREC))
            activation = low(silu(gate_up[:, :FF]) * gate_up[:, FF:])
            return low(low_back(jnp.dot(activation, weight_down, precision=HIGHEST_PREC)))
        expert_out = lax.map(jax.checkpoint(expert_block), (source_rows, weight_expert_in, weight_expert_down))
        picked = jnp.take(expert_out.reshape(-1, D), gather_index, axis=0, mode='fill', fill_value=0.0).reshape(tokens, TOPK, D)
        routed_out = lax.optimization_barrier(jnp.sum(gates[:, :, None] * picked, axis=1))
        return x_mid + live_col * (shared_out + routed_out)
    inputs = (layer_input.astype(jnp.float32), norm1, w_qkv.astype(jnp.float32), w_out.astype(jnp.float32), norm2, w_router.astype(jnp.float32), w_shared_in.astype(jnp.float32), w_shared_down.astype(jnp.float32), w_expert_in.astype(jnp.float32), w_expert_down.astype(jnp.float32))
    result, pullback = jax.vjp(forward, *inputs)
    grads = pullback(dout.astype(jnp.float32))
    return (result.astype(jnp.bfloat16), grads[0], grads[1], grads[2], grads[3], grads[4], grads[5], grads[6], grads[7], grads[8], grads[9], counts)
```

```python
import jax
import jax.numpy as jnp
from jax import lax
from jax.sharding import PartitionSpec as P

HEAD_DIM = 128


NORM_EPS = 1e-06
MASK_VALUE = -1e30
QUERY_BLOCK = 512


def silu_parts(gate_in):
    sigmoid_v = jax.nn.sigmoid(gate_in)
    return (gate_in * sigmoid_v, sigmoid_v * (1.0 + gate_in * (1.0 - sigmoid_v)))


def normalize(values_in, gain_vec):
    inverse = lax.rsqrt(jnp.mean(values_in * values_in, axis=-1, keepdims=True) + NORM_EPS)
    return (values_in * inverse * gain_vec, inverse)


def norm_back(incoming, values_in, inverse, gain_vec):
    scaled = values_in * inverse
    grad_gain = jnp.sum(incoming * scaled, axis=0)
    inner_grad = incoming * gain_vec
    grad_values = inverse * (
        inner_grad - scaled * jnp.mean(inner_grad * scaled, axis=-1, keepdims=True)
    )
    return (grad_values, grad_gain)


def rope_tables(seq_slots, head_width):
    half_dim = head_width // 2
    inv_freq = 1.0 / 10000.0 ** (jnp.arange(half_dim, dtype=jnp.float32) * 2.0 / head_width)
    angles = jnp.arange(seq_slots, dtype=jnp.float32)[:, None] * inv_freq[None, :]
    return (jnp.cos(angles)[:, None, :], jnp.sin(angles)[:, None, :])


def rotate(values_in, cosine, sine_t):
    half_dim = values_in.shape[-1] // 2
    first_half = values_in[..., :half_dim]
    second_half = values_in[..., half_dim:]
    return jnp.concatenate(
        [first_half * cosine - second_half * sine_t, first_half * sine_t + second_half * cosine],
        axis=-1,
    )


def score_block(query_block, keys_in, block_start, seq_length, score_scale):
    raw_scores = (
        jnp.einsum("qhd,khd->hqk", query_block, keys_in, preferred_element_type=jnp.float32)
        * score_scale
    )
    query_pos = block_start + jnp.arange(query_block.shape[0], dtype=jnp.int32)[:, None]
    key_pos = jnp.arange(keys_in.shape[0], dtype=jnp.int32)[None, :]
    allowed = (key_pos <= query_pos) & (key_pos < seq_length)
    return jnp.where(allowed[None], raw_scores, MASK_VALUE)


def attention_forward(queries, keys_in, values_in, seq_length):
    seq_slots, heads, head_width = queries.shape
    block_rows = min(QUERY_BLOCK, seq_slots)
    score_scale = head_width ** (-0.5)

    def one_block(block_index):
        block_start = block_index * block_rows
        scores = score_block(queries, keys_in, block_start, seq_length, score_scale)
        highest = jnp.max(scores, axis=-1, keepdims=True)
        weights_exp = jnp.exp(scores - highest)
        totals = jnp.sum(weights_exp, axis=-1, keepdims=True)
        probs_low = (weights_exp / totals).astype(jnp.bfloat16)
        block_out = jnp.einsum(
            "hqk,khd->qhd", probs_low, values_in, preferred_element_type=jnp.float32
        )
        return (block_out, highest + jnp.log(totals))

    block_outs, log_norm = lax.map(one_block, jnp.arange(seq_slots // block_rows))
    return (block_outs.reshape(seq_slots, heads, head_width), log_norm)


def attention_backward(queries, keys_in, values_in, grad_attended, log_norm, seq_length):
    seq_slots, heads, head_width = queries.shape
    block_rows = min(QUERY_BLOCK, seq_slots)
    score_scale = head_width ** (-0.5)

    def one_step(carried, block_in):
        grad_keys, grad_values = carried
        block_index, block_norm = block_in
        block_start = block_index * block_rows
        scores = score_block(queries, keys_in, block_start, seq_length, score_scale)
        probs = jnp.exp(scores - block_norm)
        grad_probs = jnp.einsum(
            "qhd,khd->hqk", grad_attended, values_in, preferred_element_type=jnp.float32
        )
        row_dot = jnp.sum(grad_probs * probs, axis=-1, keepdims=True)
        grad_scores = (probs * (grad_probs - row_dot)).astype(jnp.bfloat16)
        grad_query = (
            jnp.einsum("hqk,khd->qhd", grad_scores, keys_in, preferred_element_type=jnp.float32)
            * score_scale
        )
        grad_keys = (
            grad_keys
            + jnp.einsum("hqk,qhd->khd", grad_scores, queries, preferred_element_type=jnp.float32)
            * score_scale
        )
        grad_values = grad_values + jnp.einsum(
            "hqk,qhd->khd",
            probs.astype(jnp.bfloat16),
            grad_attended,
            preferred_element_type=jnp.float32,
        )
        return ((grad_keys, grad_values), grad_query)

    zeros_kv = jnp.zeros((seq_slots, heads, head_width), jnp.float32)
    (grad_keys, grad_values), grad_queries = lax.scan(
        one_step, (zeros_kv, zeros_kv), (jnp.arange(seq_slots // block_rows), log_norm)
    )
    return (grad_queries.reshape(seq_slots, heads, head_width), grad_keys, grad_values)


def reduce_experts(grad_in_part, grad_down_part):
    return (
        lax.psum_scatter(
            grad_in_part.astype(jnp.bfloat16), "dp", scatter_dimension=1, tiled=True
        ).astype(jnp.float32),
        lax.psum_scatter(
            grad_down_part.astype(jnp.bfloat16), "dp", scatter_dimension=1, tiled=True
        ).astype(jnp.float32),
    )


def reduce_low(part, dimension):
    return lax.psum_scatter(
        part.astype(jnp.bfloat16), ("dp", "expert"), scatter_dimension=dimension, tiled=True
    ).astype(jnp.float32)


def per_device(
    layer_input,
    lengths,
    expert_ids,
    norm1,
    w_qkv,
    w_out,
    norm2,
    w_router,
    w_shared_in,
    w_shared_down,
    w_expert_in,
    w_expert_down,
    dout,
):
    seq_slots, width = layer_input.shape
    top_k = expert_ids.shape[1]
    experts = w_router.shape[1]
    local_experts = w_expert_in.shape[0]
    hidden_units = w_shared_down.shape[0]
    heads = width // HEAD_DIM
    capacity = (seq_slots * top_k // (experts - 1) // 8 + 1) * 8
    seq_length = lengths[0]
    live_rows = jnp.arange(seq_slots, dtype=jnp.int32) < seq_length
    live_col = live_rows.astype(jnp.float32)[:, None]
    grad_top = dout.astype(jnp.float32)
    grad_branch = live_col * grad_top
    grad_branch_low = grad_branch.astype(jnp.bfloat16)
    cosine, sine_t = rope_tables(seq_slots, HEAD_DIM)
    x_full = layer_input.astype(jnp.float32)
    h1_full, inverse_one = normalize(x_full, norm1)
    h1_low = h1_full.astype(jnp.bfloat16)
    proj_qkv = jnp.dot(h1_low, w_qkv, preferred_element_type=jnp.float32).reshape(
        seq_slots, 3, heads, HEAD_DIM
    )
    queries = rotate(proj_qkv[:, 0], cosine, sine_t).astype(jnp.bfloat16)
    keys_in = rotate(proj_qkv[:, 1], cosine, sine_t).astype(jnp.bfloat16)
    values_in = proj_qkv[:, 2].astype(jnp.bfloat16)
    attended, log_norm = attention_forward(queries, keys_in, values_in, seq_length)
    attended_low = attended.reshape(seq_slots, width).astype(jnp.bfloat16)
    branch = jnp.dot(attended_low, w_out, preferred_element_type=jnp.float32)
    x_mid = x_full + live_col * branch
    h2_full, inverse_two = normalize(x_mid, norm2)
    h2_low = h2_full.astype(jnp.bfloat16)
    logits = jnp.dot(h2_low, w_router, preferred_element_type=jnp.float32)
    router_cols = jnp.arange(experts, dtype=jnp.int32) < experts - 1
    logits = jnp.where(router_cols[None, :], logits, MASK_VALUE)
    highest = jnp.max(logits, axis=-1, keepdims=True)
    weights_exp = jnp.exp(logits - highest)
    router_probs = weights_exp / jnp.sum(weights_exp, axis=-1, keepdims=True)
    shared_gu = jnp.dot(h2_low, w_shared_in, preferred_element_type=jnp.float32)
    shared_act, shared_slope = silu_parts(shared_gu[:, :hidden_units])
    shared_up = shared_gu[:, hidden_units:]
    shared_hidden = (shared_act * shared_up).astype(jnp.bfloat16)
    shared_out = jnp.dot(shared_hidden, w_shared_down, preferred_element_type=jnp.float32)
    slots = jnp.arange(experts, dtype=jnp.int32)
    picked = (
        jnp.any(expert_ids[:, :, None] == slots[None, None, :], axis=1) & live_rows[:, None]
    ).astype(jnp.int32)
    counts = lax.psum(jnp.sum(picked, axis=0), ("dp", "expert"))
    rank = jnp.where(picked > 0, jnp.cumsum(picked, axis=0) - 1, -1)
    rank_all = lax.all_gather(rank.T, "expert", axis=0)
    first_expert = lax.axis_index("expert") * local_experts
    rank_mine = lax.dynamic_slice_in_dim(rank_all, first_expert, local_experts, axis=1)
    grad_all = lax.all_gather(grad_branch_low, "expert", axis=0)
    h2_all = lax.all_gather(h2_low, "expert", axis=0)
    probs_all = lax.all_gather(router_probs.T, "expert", axis=0)
    probs_mine = lax.dynamic_slice_in_dim(probs_all, first_expert, local_experts, axis=1)
    hit = rank_mine[:, :, None, :] == jnp.arange(capacity, dtype=jnp.int32)[None, None, :, None]
    place = hit.astype(jnp.bfloat16)
    slot_gate = jnp.sum(jnp.where(hit, probs_mine[:, :, None, :], 0.0), axis=-1)
    rows_held = jnp.einsum(
        "nsct,ntd->nscd", place, h2_all, preferred_element_type=jnp.float32
    ).astype(jnp.bfloat16)
    grad_rows_in = jnp.einsum("nsct,ntd->nscd", place, grad_all, preferred_element_type=jnp.float32)
    grad_result = (slot_gate[..., None] * grad_rows_in).astype(jnp.bfloat16)
    gate_up = jnp.einsum(
        "nscd,sdf->nscf", rows_held, w_expert_in, preferred_element_type=jnp.float32
    )
    expert_act, expert_slope = silu_parts(gate_up[..., :hidden_units])
    expert_up = gate_up[..., hidden_units:]
    expert_hidden = (expert_act * expert_up).astype(jnp.bfloat16)
    result_rows = (
        jnp.einsum("nscf,sfd->nscd", expert_hidden, w_expert_down, preferred_element_type=jnp.float32)
        .astype(jnp.bfloat16)
        .astype(jnp.float32)
    )
    slot_dot = jnp.sum(result_rows * grad_rows_in, axis=-1)
    routed_part = jnp.einsum(
        "nsct,nscd->ntd",
        place,
        (slot_gate[..., None] * result_rows).astype(jnp.bfloat16),
        preferred_element_type=jnp.float32,
    ).astype(jnp.bfloat16)
    grad_expert_down = jnp.einsum(
        "nscf,nscd->sfd", expert_hidden, grad_result, preferred_element_type=jnp.float32
    )
    grad_expert_hidden = jnp.einsum(
        "nscd,sfd->nscf", grad_result, w_expert_down, preferred_element_type=jnp.float32
    )
    grad_expert_gu = jnp.concatenate(
        [grad_expert_hidden * expert_up * expert_slope, grad_expert_hidden * expert_act], axis=-1
    ).astype(jnp.bfloat16)
    grad_expert_in = jnp.einsum(
        "nscd,nscf->sdf", rows_held, grad_expert_gu, preferred_element_type=jnp.float32
    )
    grad_rows = jnp.einsum(
        "nscf,sdf->nscd", grad_expert_gu, w_expert_in, preferred_element_type=jnp.float32
    ).astype(jnp.bfloat16)
    grad_h2_part = jnp.einsum(
        "nsct,nscd->ntd", place, grad_rows, preferred_element_type=jnp.float32
    ).astype(jnp.bfloat16)
    dot_mine = jnp.sum(jnp.where(hit, slot_dot[..., None], 0.0), axis=2)
    dot_part = lax.dynamic_update_slice_in_dim(
        jnp.zeros((rank_all.shape[0], experts, seq_slots), jnp.float32), dot_mine, first_expert, axis=1
    )
    grad_probs = lax.psum_scatter(dot_part, "expert", scatter_dimension=0, tiled=False).T
    grad_h2_sum = lax.psum_scatter(grad_h2_part, "expert", scatter_dimension=0, tiled=False)
    routed_out = lax.psum_scatter(routed_part, "expert", scatter_dimension=0, tiled=False)
    routed_out = routed_out.astype(jnp.float32)
    result = (x_mid + live_col * (shared_out + routed_out)).astype(jnp.bfloat16)
    grad_shared_down = jnp.dot(shared_hidden.T, grad_branch_low, preferred_element_type=jnp.float32)
    grad_hidden = jnp.dot(grad_branch_low, w_shared_down.T, preferred_element_type=jnp.float32)
    grad_shared_gu = jnp.concatenate(
        [grad_hidden * shared_up * shared_slope, grad_hidden * shared_act], axis=-1
    ).astype(jnp.bfloat16)
    grad_shared_in = jnp.dot(h2_low.T, grad_shared_gu, preferred_element_type=jnp.float32)
    grad_h2 = jnp.dot(grad_shared_gu, w_shared_in.T, preferred_element_type=jnp.float32)
    grad_h2 = grad_h2 + grad_h2_sum.astype(jnp.float32)
    grad_logits = (
        router_probs * (grad_probs - jnp.sum(grad_probs * router_probs, axis=-1, keepdims=True))
    ).astype(jnp.bfloat16)
    grad_router = jnp.dot(h2_low.T, grad_logits, preferred_element_type=jnp.float32)
    grad_h2 = grad_h2 + jnp.dot(grad_logits, w_router.T, preferred_element_type=jnp.float32)
    grad_mid_norm, grad_norm2 = norm_back(grad_h2, x_mid, inverse_two, norm2)
    grad_mid = grad_top + grad_mid_norm
    grad_attn_branch = (live_col * grad_mid).astype(jnp.bfloat16)
    grad_out_weight = jnp.dot(attended_low.T, grad_attn_branch, preferred_element_type=jnp.float32)
    grad_attended = (
        jnp.dot(grad_attn_branch, w_out.T, preferred_element_type=jnp.float32)
        .astype(jnp.bfloat16)
        .reshape(seq_slots, heads, HEAD_DIM)
    )
    grad_queries, grad_keys, grad_values = attention_backward(
        queries, keys_in, values_in, grad_attended, log_norm, seq_length
    )
    grad_proj = (
        jnp.stack(
            [
                rotate(grad_queries, cosine, -sine_t),
                rotate(grad_keys, cosine, -sine_t),
                grad_values,
            ],
            axis=1,
        )
        .astype(jnp.bfloat16)
        .reshape(seq_slots, 3 * width)
    )
    grad_qkv_weight = jnp.dot(h1_low.T, grad_proj, preferred_element_type=jnp.float32)
    grad_h1 = jnp.dot(grad_proj, w_qkv.T, preferred_element_type=jnp.float32)
    grad_in_norm, grad_norm1 = norm_back(grad_h1, x_full, inverse_one, norm1)
    grad_input = grad_mid + grad_in_norm
    expert_in_sum, expert_down_sum = reduce_experts(grad_expert_in, grad_expert_down)
    norm1_sum, qkv_sum, out_sum, norm2_sum, router_sum, shared_in_sum, shared_down_sum = (
        lax.psum_scatter(grad_norm1, ("dp", "expert"), scatter_dimension=0, tiled=True),
        reduce_low(grad_qkv_weight, 0),
        reduce_low(grad_out_weight, 0),
        lax.psum_scatter(grad_norm2, ("dp", "expert"), scatter_dimension=0, tiled=True),
        lax.psum_scatter(grad_router, ("dp", "expert"), scatter_dimension=0, tiled=True),
        reduce_low(grad_shared_in, 0),
        reduce_low(grad_shared_down, 1),
    )
    return (
        result,
        grad_input,
        norm1_sum,
        qkv_sum,
        out_sum,
        norm2_sum,
        router_sum,
        shared_in_sum,
        shared_down_sum,
        expert_in_sum,
        expert_down_sum,
        counts,
    )


def solution(mesh):
    return jax.shard_map(
        per_device,
        mesh=mesh,
        in_specs=(
            P(("dp", "expert"), None),
            P(("dp", "expert")),
            P(("dp", "expert"), None),
            P(),
            P(),
            P(),
            P(),
            P(),
            P(),
            P(),
            P("expert", None, None),
            P("expert", None, None),
            P(("dp", "expert"), None),
        ),
        out_specs=(
            P(("dp", "expert"), None),
            P(("dp", "expert"), None),
            P(("dp", "expert")),
            P(("dp", "expert"), None),
            P(("dp", "expert"), None),
            P(("dp", "expert")),
            P(("dp", "expert"), None),
            P(("dp", "expert"), None),
            P(None, ("dp", "expert")),
            P("expert", "dp", None),
            P("expert", "dp", None),
            P(),
        ),
        check_vma=False,
    )
```

```python
import jax
import jax.numpy as jnp
from jax import lax
from jax.sharding import PartitionSpec as P

HEAD_DIM = 128


NORM_EPS = 1e-06
MASK_VALUE = -1e30
QUERY_BLOCK = 512


def silu_parts(gate_in):
    sigmoid_v = jax.nn.sigmoid(gate_in)
    return (gate_in * sigmoid_v, sigmoid_v * (1.0 + gate_in * (1.0 - sigmoid_v)))


def normalize(values_in, gain_vec):
    inverse = lax.rsqrt(jnp.mean(values_in * values_in, axis=-1, keepdims=True) + NORM_EPS)
    return (values_in * inverse * gain_vec, inverse)


def norm_back(incoming, values_in, inverse, gain_vec):
    scaled = values_in * inverse
    grad_gain = jnp.sum(incoming * scaled, axis=0)
    inner_grad = incoming * gain_vec
    grad_values = inverse * (
        inner_grad - scaled * jnp.mean(inner_grad * scaled, axis=-1, keepdims=True)
    )
    return (grad_values, grad_gain)


def rope_tables(seq_slots, head_width):
    half_dim = head_width // 2
    inv_freq = 1.0 / 10000.0 ** (jnp.arange(half_dim, dtype=jnp.float32) * 2.0 / head_width)
    angles = jnp.arange(seq_slots, dtype=jnp.float32)[:, None] * inv_freq[None, :]
    return (jnp.cos(angles)[:, None, :], jnp.sin(angles)[:, None, :])


def rotate(values_in, cosine, sine_t):
    half_dim = values_in.shape[-1] // 2
    first_half = values_in[..., :half_dim]
    second_half = values_in[..., half_dim:]
    return jnp.concatenate(
        [first_half * cosine - second_half * sine_t, first_half * sine_t + second_half * cosine],
        axis=-1,
    )


def score_block(query_block, keys_in, block_start, seq_length, score_scale):
    raw_scores = (
        jnp.einsum("qhd,khd->hqk", query_block, keys_in, preferred_element_type=jnp.float32)
        * score_scale
    )
    query_pos = block_start + jnp.arange(query_block.shape[0], dtype=jnp.int32)[:, None]
    key_pos = jnp.arange(keys_in.shape[0], dtype=jnp.int32)[None, :]
    allowed = (key_pos <= query_pos) & (key_pos < seq_length)
    return jnp.where(allowed[None], raw_scores, MASK_VALUE)


def attention_forward(queries, keys_in, values_in, seq_length):
    seq_slots, heads, head_width = queries.shape
    block_rows = min(QUERY_BLOCK, seq_slots)
    score_scale = head_width ** (-0.5)

    def one_block(block_index):
        block_start = block_index * block_rows
        scores = score_block(queries, keys_in, block_start, seq_length, score_scale)
        highest = jnp.max(scores, axis=-1, keepdims=True)
        weights_exp = jnp.exp(scores - highest)
        totals = jnp.sum(weights_exp, axis=-1, keepdims=True)
        probs_low = (weights_exp / totals).astype(jnp.bfloat16)
        block_out = jnp.einsum(
            "hqk,khd->qhd", probs_low, values_in, preferred_element_type=jnp.float32
        )
        return (block_out, highest + jnp.log(totals))

    block_outs, log_norm = lax.map(one_block, jnp.arange(seq_slots // block_rows))
    return (block_outs.reshape(seq_slots, heads, head_width), log_norm)


def attention_backward(queries, keys_in, values_in, grad_attended, log_norm, seq_length):
    seq_slots, heads, head_width = queries.shape
    block_rows = min(QUERY_BLOCK, seq_slots)
    score_scale = head_width ** (-0.5)

    def one_step(carried, block_in):
        grad_keys, grad_values = carried
        block_index, block_norm = block_in
        block_start = block_index * block_rows
        scores = score_block(queries, keys_in, block_start, seq_length, score_scale)
        probs = jnp.exp(scores - block_norm)
        grad_probs = jnp.einsum(
            "qhd,khd->hqk", grad_attended, values_in, preferred_element_type=jnp.float32
        )
        row_dot = jnp.sum(grad_probs * probs, axis=-1, keepdims=True)
        grad_scores = (probs * (grad_probs - row_dot)).astype(jnp.bfloat16)
        grad_query = (
            jnp.einsum("hqk,khd->qhd", grad_scores, keys_in, preferred_element_type=jnp.float32)
            * score_scale
        )
        grad_keys = (
            grad_keys
            + jnp.einsum("hqk,qhd->khd", grad_scores, queries, preferred_element_type=jnp.float32)
            * score_scale
        )
        grad_values = grad_values + jnp.einsum(
            "hqk,qhd->khd",
            probs.astype(jnp.bfloat16),
            grad_attended,
            preferred_element_type=jnp.float32,
        )
        return ((grad_keys, grad_values), grad_query)

    zeros_kv = jnp.zeros((seq_slots, heads, head_width), jnp.float32)
    (grad_keys, grad_values), grad_queries = lax.scan(
        one_step, (zeros_kv, zeros_kv), (jnp.arange(seq_slots // block_rows), log_norm)
    )
    return (grad_queries.reshape(seq_slots, heads, head_width), grad_keys, grad_values)


def reduce_experts(grad_in_part, grad_down_part):
    return (
        lax.psum_scatter(
            grad_in_part.astype(jnp.bfloat16), "dp", scatter_dimension=1, tiled=True
        ).astype(jnp.float32),
        lax.psum_scatter(
            grad_down_part.astype(jnp.bfloat16), "dp", scatter_dimension=1, tiled=True
        ).astype(jnp.float32),
    )


def swap_cores(values_in):
    owners = lax.axis_size("expert")
    return lax.ppermute(values_in, "expert", [(i, i ^ 1) for i in range(owners)])


def next_chip(values_in):
    owners = lax.axis_size("expert")
    return lax.ppermute(values_in, "expert", [(i, (i + 2) % owners) for i in range(owners)])


def axis_bits(name):
    return [(name, bit) for bit in range(lax.axis_size(name).bit_length() - 1)]


def scatter_sum(part, order):
    positions = axis_bits("dp")[::-1] + axis_bits("expert")[::-1]
    rows = part.shape[0] >> len(positions)
    terms = [part.reshape((2,) * len(positions) + (rows, part.shape[1]))]
    open_bits = list(positions)

    def total(parts):
        summed = parts[0].astype(jnp.float32)
        for term in parts[1:]:
            summed = summed + term.astype(jnp.float32)
        return summed

    for name, bit in order:
        dim = open_bits.index((name, bit))
        mine = (lax.axis_index(name) >> bit) & 1
        pick = lambda term, index: lax.dynamic_index_in_dim(term, index, dim, keepdims=False)
        away = total([pick(term, 1 - mine) for term in terms]).astype(part.dtype)
        came = lax.ppermute(
            away, name, [(i, i ^ (1 << bit)) for i in range(lax.axis_size(name))]
        )
        terms = [pick(term, mine) for term in terms] + [came]
        open_bits.pop(dim)
    return total(terms)


def scatter_orders():
    core, *line = axis_bits("expert")
    plane = axis_bits("dp")
    return ([core] + plane + line, [core] + plane[::-1] + line)


def scatter_columns(part):
    low_part = part.astype(jnp.bfloat16)
    first, second = scatter_orders()
    half = part.shape[1] // 256 * 128
    return jnp.concatenate(
        [scatter_sum(low_part[:, :half], first), scatter_sum(low_part[:, half:], second)], axis=1
    )


def per_device(
    layer_input,
    lengths,
    expert_ids,
    norm1,
    w_qkv,
    w_out,
    norm2,
    w_router,
    w_shared_in,
    w_shared_down,
    w_expert_in,
    w_expert_down,
    dout,
):
    seq_slots, width = layer_input.shape
    top_k = expert_ids.shape[1]
    experts = w_router.shape[1]
    local_experts = w_expert_in.shape[0]
    hidden_units = w_shared_down.shape[0]
    heads = width // HEAD_DIM
    capacity = (seq_slots * top_k // (experts - 1) // 8 + 1) * 8
    seq_length = lengths[0]
    live_rows = jnp.arange(seq_slots, dtype=jnp.int32) < seq_length
    live_col = live_rows.astype(jnp.float32)[:, None]
    grad_top = dout.astype(jnp.float32)
    grad_branch = live_col * grad_top
    grad_branch_low = grad_branch.astype(jnp.bfloat16)
    cosine, sine_t = rope_tables(seq_slots, HEAD_DIM)
    x_full = layer_input.astype(jnp.float32)
    h1_full, inverse_one = normalize(x_full, norm1)
    h1_low = h1_full.astype(jnp.bfloat16)
    proj_qkv = jnp.dot(h1_low, w_qkv, preferred_element_type=jnp.float32).reshape(
        seq_slots, 3, heads, HEAD_DIM
    )
    queries = rotate(proj_qkv[:, 0], cosine, sine_t).astype(jnp.bfloat16)
    keys_in = rotate(proj_qkv[:, 1], cosine, sine_t).astype(jnp.bfloat16)
    values_in = proj_qkv[:, 2].astype(jnp.bfloat16)
    attended, log_norm = attention_forward(queries, keys_in, values_in, seq_length)
    attended_low = attended.reshape(seq_slots, width).astype(jnp.bfloat16)
    branch = jnp.dot(attended_low, w_out, preferred_element_type=jnp.float32)
    x_mid = x_full + live_col * branch
    h2_full, inverse_two = normalize(x_mid, norm2)
    h2_low = h2_full.astype(jnp.bfloat16)
    logits = jnp.dot(h2_low, w_router, preferred_element_type=jnp.float32)
    router_cols = jnp.arange(experts, dtype=jnp.int32) < experts - 1
    logits = jnp.where(router_cols[None, :], logits, MASK_VALUE)
    highest = jnp.max(logits, axis=-1, keepdims=True)
    weights_exp = jnp.exp(logits - highest)
    router_probs = weights_exp / jnp.sum(weights_exp, axis=-1, keepdims=True)
    shared_gu = jnp.dot(h2_low, w_shared_in, preferred_element_type=jnp.float32)
    shared_act, shared_slope = silu_parts(shared_gu[:, :hidden_units])
    shared_up = shared_gu[:, hidden_units:]
    shared_hidden = (shared_act * shared_up).astype(jnp.bfloat16)
    shared_out = jnp.dot(shared_hidden, w_shared_down, preferred_element_type=jnp.float32)
    slots = jnp.arange(experts, dtype=jnp.int32)
    picked = (
        jnp.any(expert_ids[:, :, None] == slots[None, None, :], axis=1) & live_rows[:, None]
    ).astype(jnp.int32)
    counts_here = jnp.sum(picked, axis=0).astype(jnp.float32)
    rank = jnp.where(picked > 0, jnp.cumsum(picked, axis=0) - 1, -1).T
    first_expert = lax.axis_index("expert") * local_experts
    chips = experts // local_experts // 2
    probs_t = router_probs.T

    def both(block):
        return jnp.stack([block, swap_cores(block)])

    def own_rows(table):
        return lax.dynamic_slice_in_dim(table, first_expert, local_experts, axis=1)

    kept = []
    dot_sum = routed_sum = grad_h2_sum = None
    line_grad, line_rank, line_h2, line_probs = grad_branch_low, rank, h2_low, probs_t
    held = []
    for step in range(chips):
        if step:
            line_grad, line_rank, line_h2, line_probs = (
                next_chip(line_grad),
                next_chip(line_rank),
                next_chip(line_h2),
                next_chip(line_probs),
            )
        hit = (
            own_rows(both(line_rank))[:, :, None, :]
            == jnp.arange(capacity, dtype=jnp.int32)[None, None, :, None]
        )
        place = hit.astype(jnp.bfloat16)
        slot_gate = jnp.sum(
            jnp.where(hit, own_rows(both(line_probs))[:, :, None, :], 0.0), axis=-1
        )
        rows_held = jnp.einsum(
            "nsct,ntd->nscd", place, both(line_h2), preferred_element_type=jnp.float32
        ).astype(jnp.bfloat16)
        grad_rows_in = jnp.einsum(
            "nsct,ntd->nscd", place, both(line_grad), preferred_element_type=jnp.float32
        )
        grad_result = (slot_gate[..., None] * grad_rows_in).astype(jnp.bfloat16)
        gate_up = jnp.einsum(
            "nscd,sdf->nscf", rows_held, w_expert_in, preferred_element_type=jnp.float32
        )
        expert_act, expert_slope = silu_parts(gate_up[..., :hidden_units])
        expert_up = gate_up[..., hidden_units:]
        expert_hidden = (expert_act * expert_up).astype(jnp.bfloat16)
        result_rows = (
            jnp.einsum(
                "nscf,sfd->nscd", expert_hidden, w_expert_down, preferred_element_type=jnp.float32
            )
            .astype(jnp.bfloat16)
            .astype(jnp.float32)
        )
        slot_dot = jnp.sum(result_rows * grad_rows_in, axis=-1)
        routed_part = jnp.einsum(
            "nsct,nscd->ntd",
            place,
            (slot_gate[..., None] * result_rows).astype(jnp.bfloat16),
            preferred_element_type=jnp.float32,
        )
        grad_expert_hidden = jnp.einsum(
            "nscd,sfd->nscf", grad_result, w_expert_down, preferred_element_type=jnp.float32
        )
        grad_expert_gu = jnp.concatenate(
            [grad_expert_hidden * expert_up * expert_slope, grad_expert_hidden * expert_act],
            axis=-1,
        ).astype(jnp.bfloat16)
        grad_rows = jnp.einsum(
            "nscf,sdf->nscd", grad_expert_gu, w_expert_in, preferred_element_type=jnp.float32
        ).astype(jnp.bfloat16)
        grad_h2_part = jnp.einsum(
            "nsct,nscd->ntd", place, grad_rows, preferred_element_type=jnp.float32
        )
        dot_part = lax.dynamic_update_slice_in_dim(
            jnp.zeros((2, experts, seq_slots), jnp.float32),
            jnp.sum(jnp.where(hit, slot_dot[..., None], 0.0), axis=2),
            first_expert,
            axis=1,
        )
        kept.append((rows_held, grad_result, expert_hidden, grad_expert_gu))
        held.append((dot_part, routed_part, grad_h2_part))

    def bring_home(index, dtype):
        travelling = None
        for step in list(range(1, chips)) + [0]:
            part = held[step][index]
            total = part[0] + swap_cores(part[1].astype(dtype)).astype(jnp.float32)
            if travelling is not None:
                total = total + next_chip(travelling).astype(jnp.float32)
            travelling = total.astype(dtype)
        return total

    grad_probs = bring_home(0, jnp.float32).T
    grad_h2_sum = bring_home(2, jnp.bfloat16)
    routed_out = bring_home(1, jnp.bfloat16)
    rows_held, grad_result, expert_hidden, grad_expert_gu = (
        jnp.concatenate(pieces, axis=0) for pieces in zip(*kept)
    )
    grad_expert_down = jnp.einsum(
        "nscf,nscd->sfd", expert_hidden, grad_result, preferred_element_type=jnp.float32
    )
    grad_expert_in = jnp.einsum(
        "nscd,nscf->sdf", rows_held, grad_expert_gu, preferred_element_type=jnp.float32
    )
    result = (x_mid + live_col * (shared_out + routed_out)).astype(jnp.bfloat16)
    grad_shared_down = jnp.dot(grad_branch_low.T, shared_hidden, preferred_element_type=jnp.float32)
    grad_hidden = jnp.dot(grad_branch_low, w_shared_down.T, preferred_element_type=jnp.float32)
    grad_shared_gu = jnp.concatenate(
        [grad_hidden * shared_up * shared_slope, grad_hidden * shared_act], axis=-1
    ).astype(jnp.bfloat16)
    grad_shared_in = jnp.dot(h2_low.T, grad_shared_gu, preferred_element_type=jnp.float32)
    grad_h2 = jnp.dot(grad_shared_gu, w_shared_in.T, preferred_element_type=jnp.float32)
    grad_h2 = grad_h2 + grad_h2_sum
    grad_logits = (
        router_probs * (grad_probs - jnp.sum(grad_probs * router_probs, axis=-1, keepdims=True))
    ).astype(jnp.bfloat16)
    grad_router = jnp.dot(h2_low.T, grad_logits, preferred_element_type=jnp.float32)
    grad_h2 = grad_h2 + jnp.dot(grad_logits, w_router.T, preferred_element_type=jnp.float32)
    grad_mid_norm, grad_norm2 = norm_back(grad_h2, x_mid, inverse_two, norm2)
    grad_mid = grad_top + grad_mid_norm
    grad_attn_branch = (live_col * grad_mid).astype(jnp.bfloat16)
    grad_out_weight = jnp.dot(attended_low.T, grad_attn_branch, preferred_element_type=jnp.float32)
    grad_attended = (
        jnp.dot(grad_attn_branch, w_out.T, preferred_element_type=jnp.float32)
        .astype(jnp.bfloat16)
        .reshape(seq_slots, heads, HEAD_DIM)
    )
    grad_queries, grad_keys, grad_values = attention_backward(
        queries, keys_in, values_in, grad_attended, log_norm, seq_length
    )
    grad_proj = (
        jnp.stack(
            [
                rotate(grad_queries, cosine, -sine_t),
                rotate(grad_keys, cosine, -sine_t),
                grad_values,
            ],
            axis=1,
        )
        .astype(jnp.bfloat16)
        .reshape(seq_slots, 3 * width)
    )
    grad_qkv_weight = jnp.dot(h1_low.T, grad_proj, preferred_element_type=jnp.float32)
    grad_h1 = jnp.dot(grad_proj, w_qkv.T, preferred_element_type=jnp.float32)
    grad_in_norm, grad_norm1 = norm_back(grad_h1, x_full, inverse_one, norm1)
    grad_input = grad_mid + grad_in_norm
    expert_in_sum, expert_down_sum = reduce_experts(grad_expert_in, grad_expert_down)
    shared_sum = scatter_columns(jnp.concatenate([grad_shared_in, grad_shared_down], axis=1))
    shared_in_sum = shared_sum[:, : 2 * hidden_units]
    shared_down_sum = shared_sum[:, 2 * hidden_units :].T
    out_sum = scatter_columns(grad_out_weight)
    qkv_sum = scatter_columns(grad_qkv_weight)
    small_sum = scatter_sum(
        jnp.concatenate(
            [
                grad_router,
                jnp.broadcast_to(counts_here[None, :], (width, experts)),
                grad_norm1[:, None],
                grad_norm2[:, None],
            ],
            axis=1,
        ),
        scatter_orders()[0],
    )
    router_sum = small_sum[:, :experts]
    counts = small_sum[0, experts : 2 * experts].astype(jnp.int32)
    norm1_sum = small_sum[:, 2 * experts]
    norm2_sum = small_sum[:, 2 * experts + 1]
    return (
        result,
        grad_input,
        norm1_sum,
        qkv_sum,
        out_sum,
        norm2_sum,
        router_sum,
        shared_in_sum,
        shared_down_sum,
        expert_in_sum,
        expert_down_sum,
        counts,
    )


def solution(mesh):
    return jax.shard_map(
        per_device,
        mesh=mesh,
        in_specs=(
            P(("dp", "expert"), None),
            P(("dp", "expert")),
            P(("dp", "expert"), None),
            P(),
            P(),
            P(),
            P(),
            P(),
            P(),
            P(),
            P("expert", None, None),
            P("expert", None, None),
            P(("dp", "expert"), None),
        ),
        out_specs=(
            P(("dp", "expert"), None),
            P(("dp", "expert"), None),
            P(("dp", "expert")),
            P(("dp", "expert"), None),
            P(("dp", "expert"), None),
            P(("dp", "expert")),
            P(("dp", "expert"), None),
            P(("dp", "expert"), None),
            P(None, ("dp", "expert")),
            P("expert", "dp", None),
            P("expert", "dp", None),
            P(),
        ),
        check_vma=False,
    )
```

```python
import jax
import jax.numpy as jnp
from jax import lax
from jax.experimental import pallas as pl
from jax.experimental.pallas import tpu as pltpu
from jax.sharding import PartitionSpec as P

HEAD_DIM = 128
NORM_EPS = 1e-06
MASK_VALUE = -1e30
NT = (((1,), (1,)), ((), ()))
TN = (((0,), (0,)), ((), ()))

def turn(values_in, cosine, signed_sine):
    return values_in * cosine + pltpu.roll(values_in, HEAD_DIM // 2, 1) * signed_sine

def block_scores(q, k, start, seq_length):
    s = lax.dot_general(q, k, NT, preferred_element_type=jnp.float32) * HEAD_DIM ** (-0.5)
    query_pos = start + lax.broadcasted_iota(jnp.int32, s.shape, 0)
    key_pos = lax.broadcasted_iota(jnp.int32, s.shape, 1)
    return jnp.where((key_pos <= query_pos) & (key_pos < seq_length), s, MASK_VALUE)

def attention_kernel(length_ref, x, norm1, wq, wk, wv, cosine, sine, w_out, norm2, h1, q_o, k_o, v_o, att, lse, x_mid, h2):
    f32, bf16 = jnp.float32, jnp.bfloat16
    p = pl.program_id(0)
    tokens = x.shape[0]
    seq_length = length_ref[0]
    span = min(256, tokens)

    @pl.when(p == 0)
    def _():
        xf = x[...].astype(f32)
        inverse = lax.rsqrt(jnp.mean(xf * xf, axis=-1, keepdims=True) + NORM_EPS)
        h1[...] = (xf * inverse * norm1[...]).astype(bf16)
        lse[...] = jnp.zeros_like(lse)

    for w, o in ((wq, q_o), (wk, k_o), (wv, v_o)):
        full = jnp.dot(h1[...], w[...], preferred_element_type=f32)
        for j in (0, 1):
            part = full[:, j * HEAD_DIM:(j + 1) * HEAD_DIM]
            if w is not wv:
                part = turn(part, cosine[...], sine[...])
            o[:, pl.ds(j * HEAD_DIM, HEAD_DIM)] = part.astype(bf16)
    lane = lax.broadcasted_iota(jnp.int32, (span, lse.shape[1]), 1)
    for j in (0, 1):
        cols = pl.ds(j * HEAD_DIM, HEAD_DIM)
        for start in range(0, tokens, span):
            rows = pl.ds(start, span)
            seen = pl.ds(0, start + span)
            s = block_scores(q_o[rows, cols], k_o[seen, cols], start, seq_length)
            high = jnp.max(s, axis=-1, keepdims=True)
            ex = jnp.exp(s - high)
            total = jnp.sum(ex, axis=-1, keepdims=True)
            low = (ex / total).astype(bf16)
            out = jnp.dot(low, v_o[seen, cols], preferred_element_type=f32)
            att[rows, pl.ds(pl.multiple_of(p * 2 * HEAD_DIM + j * HEAD_DIM, HEAD_DIM), HEAD_DIM)] = out.astype(bf16)
            lse[rows, :] = jnp.where(lane == 2 * p + j, high + jnp.log(total), lse[rows, :])

    @pl.when(p == pl.num_programs(0) - 1)
    def _():
        branch = jnp.dot(att[...], w_out[...], preferred_element_type=f32)
        live = lax.broadcasted_iota(jnp.int32, (tokens, 1), 0) < seq_length
        mid = x[...].astype(f32) + jnp.where(live, branch, 0.0)
        x_mid[...] = mid
        inverse = lax.rsqrt(jnp.mean(mid * mid, axis=-1, keepdims=True) + NORM_EPS)
        h2[...] = (mid * inverse * norm2[...]).astype(bf16)

def whole(a):
    return pl.BlockSpec(a.shape, lambda p: (0,) * len(a.shape), pipeline_mode=pl.Buffered(1))

def attention_forward(lengths, x, norm1, w_qkv, cosine, sine, w_out, norm2):
    tokens, width = x.shape
    pairs = width // (2 * HEAD_DIM)
    f32, bf16 = jnp.float32, jnp.bfloat16
    wide = 2 * HEAD_DIM
    col = lambda k: pl.BlockSpec((width, wide), lambda p, k=k: (0, k * pairs + p))
    head = pl.BlockSpec((tokens, wide), lambda p: (0, p))
    full = pl.BlockSpec((tokens, width), lambda p: (0, 0))
    sd = jax.ShapeDtypeStruct
    return pl.pallas_call(
        attention_kernel, grid=(pairs,),
        in_specs=[pl.BlockSpec(memory_space=pltpu.SMEM), whole(x), whole(norm1), col(0), col(1), col(2), whole(cosine), whole(sine), whole(w_out), whole(norm2)],
        out_specs=[full, head, head, head, full, pl.BlockSpec((tokens, 128), lambda p: (0, 0)), full, full],
        out_shape=[sd((tokens, width), bf16)] * 5 + [sd((tokens, 128), f32), sd((tokens, width), f32), sd((tokens, width), bf16)],
        compiler_params=pltpu.CompilerParams(vmem_limit_bytes=48 * 2**20),
        cost_estimate=pl.CostEstimate(flops=0, bytes_accessed=0, transcendentals=0),
        name="attention_forward",
    )(lengths, x, norm1, w_qkv, w_qkv, w_qkv, cosine, sine, w_out, norm2)

def attention_back_kernel(rows, extra, carried, length_ref, core_ref, da, w_out, q, k, v, lse, cosine, sine, h1, att, wq, wk, wv, *rest):
    f32, bf16 = jnp.float32, jnp.bfloat16
    dh1_in = None
    if carried:
        dh1_in, *rest = rest
    if extra:
        x, gain, grad_mid, small, *rest = rest
    *grads, dh1, dk_s, dv_s, dproj = rest
    p = pl.program_id(0)
    pair = length_ref[1] + p
    tokens, width = da.shape
    seq_length = length_ref[0]
    span = min(256, tokens)
    scale = HEAD_DIM ** (-0.5)
    mine = core_ref[0] == 0
    wide = 2 * HEAD_DIM
    do_full = lax.dot_general(da[...], w_out[...], NT, preferred_element_type=f32).astype(bf16)
    lane = lax.broadcasted_iota(jnp.int32, (span, lse.shape[1]), 1)
    back_sine = -sine[...]
    for j in (0, 1):
        cols = pl.ds(j * HEAD_DIM, HEAD_DIM)
        do_head = do_full[:, j * HEAD_DIM : (j + 1) * HEAD_DIM]
        for start in range(tokens - span, -1, -span):
            r = pl.ds(start, span)
            seen = pl.ds(0, start + span)
            s = block_scores(q[r, cols], k[seen, cols], start, seq_length)
            norm = jnp.sum(jnp.where(lane == 2 * pair + j, lse[r, :], 0.0), axis=1, keepdims=True)
            probs = jnp.exp(s - norm)
            do = do_head[start : start + span]
            dp = lax.dot_general(do, v[seen, cols], NT, preferred_element_type=f32)
            row = jnp.sum(dp * probs, axis=1, keepdims=True)
            ds = (probs * (dp - row)).astype(bf16)
            dq = jnp.dot(ds, k[seen, cols], preferred_element_type=f32) * scale
            dproj[r, pl.ds(j * HEAD_DIM, HEAD_DIM)] = turn(
                dq, cosine[r, :], back_sine[start : start + span]
            ).astype(bf16)
            dk = lax.dot_general(ds, q[r, cols], TN, preferred_element_type=f32) * scale
            dv = lax.dot_general(probs.astype(bf16), do, TN, preferred_element_type=f32)
            if start == tokens - span:
                dk_s[seen, :] = dk
                dv_s[seen, :] = dv
            else:
                dk_s[seen, :] += dk
                dv_s[seen, :] += dv
        dproj[:, pl.ds(wide + j * HEAD_DIM, HEAD_DIM)] = turn(dk_s[...], cosine[...], back_sine).astype(bf16)
        dproj[:, pl.ds(2 * wide + j * HEAD_DIM, HEAD_DIM)] = dv_s[...].astype(bf16)
    total = jnp.where(p == 0, dh1_in[...] if carried else 0.0, dh1[...])
    for i, w in enumerate((wq, wk, wv)):
        part = dproj[:, pl.ds(i * wide, wide)]
        grad = lax.dot_general(h1[...], part, TN, preferred_element_type=f32)
        store_grad(grad, pl.ds(i * wide, wide), rows, mine, grads)
        total += lax.dot_general(part, w[...], NT, preferred_element_type=f32)
    part = da[:, pl.ds(pl.multiple_of(pair * wide, wide), wide)]
    grad = lax.dot_general(att[...], part, TN, preferred_element_type=f32)
    store_grad(grad, pl.ds(3 * wide, wide), rows, mine, grads)
    dh1[...] = total
    if not extra:
        return

    @pl.when(p < pl.num_programs(0) - 1)
    def _():
        store_grad(jnp.zeros(small.shape, f32), pl.ds(4 * wide, small.shape[1]), rows, mine, grads)

    @pl.when(p == pl.num_programs(0) - 1)
    def _():
        full = x[...].astype(f32)
        inverse = lax.rsqrt(jnp.mean(full * full, axis=-1, keepdims=True) + NORM_EPS)
        scaled = full * inverse
        inner = total * gain[...]
        dh1[...] = grad_mid[...] + inverse * (
            inner - scaled * jnp.mean(inner * scaled, axis=-1, keepdims=True)
        )
        column = lax.broadcasted_iota(jnp.int32, (tokens, small.shape[1]), 1)
        grad = small[...] + lax.dot_general(
            total * scaled, jnp.where(column == extra + 1, 1.0, 0.0), TN,
            precision=lax.Precision.HIGHEST, preferred_element_type=f32,
        )
        store_grad(grad, pl.ds(4 * wide, small.shape[1]), rows, mine, grads)


def attention_backward(lengths, core, da, w_out, q, k, v, lse, cosine, sine, h1, att, w_qkv, dh1_in, first, count, rows, tail):
    tokens, width = da.shape
    pairs = width // (2 * HEAD_DIM)
    wide = 2 * HEAD_DIM
    f32, bf16 = jnp.float32, jnp.bfloat16
    col = lambda k: pl.BlockSpec((width, wide), lambda p, k=k: (0, k * pairs + first + p))
    head = pl.BlockSpec((tokens, wide), lambda p: (0, first + p))
    sd = jax.ShapeDtypeStruct
    smem = pl.BlockSpec(memory_space=pltpu.SMEM)
    n = width // 2 if rows else width
    extra, tail_args = tail if tail else (0, ())
    columns = 4 * wide + (tail_args[-1].shape[1] if extra else 0)
    grads = [sd((n, count * columns), bf16)] * (2 if rows else 1)
    carried = dh1_in is not None
    tail_args = ((dh1_in,) if carried else ()) + tuple(tail_args)
    whole_args = (da, lse, cosine, sine, h1, att) + tail_args
    spec = {id(a): whole(a) for a in whole_args}
    return pl.pallas_call(
        lambda *r: attention_back_kernel(rows, extra, carried, *r),
        grid=(count,),
        in_specs=[smem, smem, spec[id(da)], pl.BlockSpec((wide, width), lambda p: (first + p, 0)), head, head, head]
        + [spec[id(a)] for a in (lse, cosine, sine, h1, att)]
        + [col(0), col(1), col(2)]
        + [spec[id(a)] for a in tail_args],
        out_specs=[pl.BlockSpec((n, columns), lambda p: (0, p))] * len(grads)
        + [pl.BlockSpec((tokens, width), lambda p: (0, 0))],
        out_shape=grads + [sd((tokens, width), f32)],
        scratch_shapes=[pltpu.VMEM((tokens, HEAD_DIM), f32), pltpu.VMEM((tokens, HEAD_DIM), f32), pltpu.VMEM((tokens, 3 * wide), bf16)],
        compiler_params=pltpu.CompilerParams(vmem_limit_bytes=48 * 2**20),
        cost_estimate=pl.CostEstimate(flops=0, bytes_accessed=0, transcendentals=0),
        name="attention_backward",
    )(
        jnp.concatenate([lengths, jnp.full((1,), first, jnp.int32)]), core, da, w_out, q, k, v,
        lse, cosine, sine, h1, att, w_qkv, w_qkv, w_qkv, *tail_args,
    )


def expert_kernel(cap, tokens, hidden, last_slot, *refs):
    (first_ref, h2a, h2b, cba, cbb, wr, w_in, w_down) = refs[:8]
    (dra, drb, outa, outb, rows_o, dy_o, act_o, dgu_o, gu, cbrow, oh, gy, drs, probs, dots) = refs[-15:]
    f32, bf16 = jnp.float32, jnp.bfloat16
    e = pl.program_id(0)
    experts = wr.shape[0]
    width = wr.shape[1]
    mine = first_ref[0] + e
    table_rows = probs.shape[1]

    @pl.when(e == 0)
    def _():
        for src, h2 in ((0, h2a), (1, h2b)):
            logits = lax.dot_general(wr[...], h2[...], (((1,), (1,)), ((), ())), preferred_element_type=f32)
            row = lax.broadcasted_iota(jnp.int32, logits.shape, 0)
            logits = jnp.where(row < experts - 1, logits, MASK_VALUE)
            ex = jnp.exp(logits - jnp.max(logits, axis=0, keepdims=True))
            probs[src] = ex / jnp.sum(ex, axis=0, keepdims=True)
            dots[src] = jnp.zeros_like(probs[src])

    gates = []
    masks = []
    for src, h2, cb in ((0, h2a, cba), (1, h2b, cbb)):
        row_id = lax.broadcasted_iota(jnp.int32, (table_rows, tokens), 0)
        table = cb[pl.ds(tokens, table_rows), pl.ds(0, tokens)].astype(f32)
        rank = jnp.sum(jnp.where(row_id == mine, table, 0.0), axis=0, keepdims=True)
        prob = jnp.sum(jnp.where(row_id == mine, probs[src], 0.0), axis=0, keepdims=True)
        hit = lax.broadcasted_iota(jnp.int32, (cap, tokens), 0).astype(f32) == rank
        masks.append(hit)
        gates.append(jnp.sum(jnp.where(hit, prob, 0.0), axis=1, keepdims=True))
        onehot = jnp.where(hit, 1.0, 0.0).astype(bf16)
        oh[src, pl.ds(e * cap, cap), :] = onehot
        half = pl.ds(src * cap, cap)
        @pl.loop(0, width // 256, unroll=True)
        def _(i):
            t = pl.ds(pl.multiple_of(i * 256, 256), 256)
            rows_o[0, half, t] = jnp.dot(onehot, h2[:, t], preferred_element_type=f32).astype(bf16)
            cbrow[half, t] = jnp.dot(onehot, cb[pl.ds(0, tokens), t], preferred_element_type=f32).astype(bf16)
    gate = jnp.concatenate(gates, axis=0)

    @pl.loop(0, 2 * hidden // 256, unroll=True)
    def _(i):
        t = pl.ds(pl.multiple_of(i * 256, 256), 256)
        gu[:, t] = jnp.dot(rows_o[0], w_in[0, :, t], preferred_element_type=f32)

    @pl.loop(0, hidden // 128, unroll=True)
    def _(i):
        ta = pl.ds(pl.multiple_of(i * 128, 128), 128)
        tb = pl.ds(pl.multiple_of(hidden + i * 128, 128), 128)
        a = gu[:, ta]
        b = gu[:, tb]
        sig = jax.nn.sigmoid(a)
        silu = a * sig
        act_o[0, :, ta] = (silu * b).astype(bf16)
        gu[:, ta] = b * (sig * (1.0 + a * (1.0 - sig)))
        gu[:, tb] = silu

    def down(i, dot):
        t = pl.ds(pl.multiple_of(i * 256, 256), 256)
        y = jnp.dot(act_o[0], w_down[0, :, t], preferred_element_type=f32).astype(bf16).astype(f32)
        c = cbrow[:, t].astype(f32)
        gyt = (gate * y).astype(bf16)
        for src in (0, 1):
            gy[src, pl.ds(e * cap, cap), t] = gyt[src * cap:(src + 1) * cap]
        dy_o[0, :, t] = (gate * c).astype(bf16)
        return dot + jnp.sum(y * c, axis=1, keepdims=True)
    dot = lax.fori_loop(0, width // 256, down, jnp.zeros((2 * cap, 1), f32), unroll=True)
    for src in (0, 1):
        back = jnp.sum(jnp.where(masks[src], dot[src * cap:(src + 1) * cap], 0.0), axis=0, keepdims=True)
        row_id = lax.broadcasted_iota(jnp.int32, (table_rows, tokens), 0)
        dots[src] += jnp.where(row_id == mine, back, 0.0)

    for start in range(0, hidden, 256):
        n = min(256, hidden - start)
        dact = lax.dot_general(dy_o[0], w_down[0, pl.ds(start, n), :], (((1,), (1,)), ((), ())), preferred_element_type=f32)
        dgu_o[0, :, pl.ds(start, n)] = (dact * gu[:, pl.ds(start, n)]).astype(bf16)
        dgu_o[0, :, pl.ds(hidden + start, n)] = (dact * gu[:, pl.ds(hidden + start, n)]).astype(bf16)

    @pl.loop(0, width // 256, unroll=True)
    def _(i):
        t = pl.ds(pl.multiple_of(i * 256, 256), 256)
        dr = lax.dot_general(dgu_o[0], w_in[0, t, :], (((1,), (1,)), ((), ())), preferred_element_type=f32).astype(bf16)
        for src in (0, 1):
            drs[src, pl.ds(e * cap, cap), t] = dr[src * cap:(src + 1) * cap]

    @pl.when(e == pl.num_programs(0) - 1)
    def _():
        for src, dro, outo in ((0, dra, outa), (1, drb, outb)):
            @pl.loop(0, width // 256, unroll=True)
            def _(i):
                t = pl.ds(pl.multiple_of(i * 256, 256), 256)
                dims = (((0,), (0,)), ((), ()))
                outo[:, t] = lax.dot_general(oh[src], gy[src, :, t], dims, preferred_element_type=f32).astype(bf16)
                dro[pl.ds(0, tokens), t] = lax.dot_general(oh[src], drs[src, :, t], dims, preferred_element_type=f32).astype(bf16)
            hi = dots[src].astype(bf16)
            lo = (dots[src] - hi.astype(f32)).astype(bf16)
            pad = jnp.zeros((2 * table_rows, width - tokens), bf16)
            dro[pl.ds(tokens, table_rows), pl.ds(0, tokens)] = hi
            dro[pl.ds(tokens + table_rows, table_rows), pl.ds(0, tokens)] = lo
            dro[pl.ds(tokens, 2 * table_rows), pl.ds(tokens, width - tokens)] = pad

def expert_step(first, h2a, h2b, cba, cbb, wr, w_in, w_down, step, steps, cap, kept):
    tokens, width = h2a.shape
    local, _, hidden2 = w_in.shape
    hidden = hidden2 // 2
    table_rows = cba.shape[0] - tokens
    bf16, f32 = jnp.bfloat16, jnp.float32
    whole = lambda a: pl.BlockSpec(a.shape, lambda e: (0,) * a.ndim, pipeline_mode=pl.Buffered(1))
    ins = [pl.BlockSpec(memory_space=pltpu.SMEM)] + [whole(a) for a in (h2a, h2b, cba, cbb, wr)]
    ins += [pl.BlockSpec((1,) + w_in.shape[1:], lambda e: (e, 0, 0)), pl.BlockSpec((1,) + w_down.shape[1:], lambda e: (e, 0, 0))]
    kept_shapes = [jax.ShapeDtypeStruct((local, steps * 2 * cap, n), bf16) for n in (width, width, hidden, 2 * hidden)]
    sums = [jax.ShapeDtypeStruct((tokens + 2 * table_rows, width), bf16)] * 2 + [jax.ShapeDtypeStruct((tokens, width), bf16)] * 2
    args = [first, h2a, h2b, cba, cbb, wr, w_in, w_down]
    alias = {}
    if kept is not None:
        ins += [pl.BlockSpec(memory_space=pl.ANY)] * 4
        alias = {len(args) + i: 4 + i for i in range(4)}
        args += list(kept)
    outs = [pl.BlockSpec(s.shape, lambda e: (0, 0)) for s in sums]
    outs += [pl.BlockSpec((1, 2 * cap, s.shape[2]), lambda e: (e, step, 0)) for s in kept_shapes]
    rows = 2 * cap
    flops = 2 * local * rows * (2 * (3 * width * hidden) + 4 * tokens * width)
    res = pl.pallas_call(
        lambda *r: expert_kernel(cap, tokens, hidden, None, *r),
        grid=(local,),
        in_specs=ins, out_specs=outs, out_shape=sums + kept_shapes,
        scratch_shapes=[pltpu.VMEM((rows, 2 * hidden), f32), pltpu.VMEM((rows, width), bf16), pltpu.VMEM((2, local * cap, tokens), bf16),
                        pltpu.VMEM((2, local * cap, width), bf16), pltpu.VMEM((2, local * cap, width), bf16),
                        pltpu.VMEM((2, table_rows, tokens), f32), pltpu.VMEM((2, table_rows, tokens), f32)],
        input_output_aliases=alias,
        compiler_params=pltpu.CompilerParams(vmem_limit_bytes=60 * 2**20),
        cost_estimate=pl.CostEstimate(flops=0, bytes_accessed=0, transcendentals=0),
        name="expert_step",
    )(*args)
    return res[:4], res[4:]


def token_kernel(length_ref, ids, dout, rows_o):
    f32, bf16 = jnp.float32, jnp.bfloat16
    tokens = dout.shape[0]
    table_rows = rows_o.shape[0] - tokens
    live = lax.broadcasted_iota(jnp.int32, (tokens, 1), 0) < length_ref[0]
    rows_o[pl.ds(0, tokens), :] = jnp.where(live, dout[...].astype(f32), 0.0).astype(bf16)
    lane = lax.broadcasted_iota(jnp.int32, (tokens, 128), 1)
    picked = jnp.zeros((tokens, 128), f32)
    for k in range(ids.shape[1]):
        picked = jnp.where(lane == ids[:, k:k + 1], 1.0, picked)
    picked = jnp.where(live, picked, 0.0).astype(bf16)
    earlier = lax.broadcasted_iota(jnp.int32, (tokens, tokens), 0)
    later = lax.broadcasted_iota(jnp.int32, (tokens, tokens), 1)
    before = jnp.where(earlier < later, 1.0, 0.0).astype(bf16)
    same = jnp.where(earlier == later, 1.0, 0.0).astype(bf16)
    rank = lax.dot_general(picked, before, TN, preferred_element_type=f32)
    hit = lax.dot_general(picked, same, TN, preferred_element_type=f32)
    table = jnp.where(hit > 0.5, rank, -1.0)[:table_rows].astype(bf16)
    rows_o[pl.ds(tokens, table_rows), pl.ds(0, tokens)] = table
    rows_o[pl.ds(tokens, table_rows), pl.ds(tokens, dout.shape[1] - tokens)] = jnp.zeros(
        (table_rows, dout.shape[1] - tokens), bf16
    )


def token_rows(lengths, expert_ids, dout, experts):
    return pl.pallas_call(
        token_kernel,
        in_specs=[
            pl.BlockSpec(memory_space=pltpu.SMEM),
            pl.BlockSpec(memory_space=pltpu.VMEM),
            pl.BlockSpec(memory_space=pltpu.VMEM),
        ],
        out_specs=pl.BlockSpec(memory_space=pltpu.VMEM),
        out_shape=jax.ShapeDtypeStruct((dout.shape[0] + experts, dout.shape[1]), jnp.bfloat16),
        cost_estimate=pl.CostEstimate(flops=0, bytes_accessed=0, transcendentals=0),
        name="token_rows",
    )(lengths, expert_ids, dout)


def store_grad(grad, cols, rows, mine, outs):
    low = jnp.bfloat16
    if not rows:
        outs[0][:, cols] = grad.astype(low)
        return
    for c in range(grad.shape[0] // (2 * rows)):
        first = grad[2 * c * rows : (2 * c + 1) * rows]
        second = grad[(2 * c + 1) * rows : (2 * c + 2) * rows]
        outs[0][pl.ds(c * rows, rows), cols] = jnp.where(mine, first, second).astype(low)
        outs[1][pl.ds(c * rows, rows), cols] = jnp.where(mine, second, first).astype(low)


def shared_kernel(rows, experts, core_ref, h2, cb, w_in, w_down, w_router, shared_out, grad_h2, probs, *rest):
    f32, bf16 = jnp.float32, jnp.bfloat16
    *grads, gu, hs, dgu = rest
    tokens, width = h2.shape
    hidden = w_down.shape[0]
    mine = core_ref[0] == 0
    own = pl.ds(0, tokens)

    logits = jnp.dot(h2[...], w_router[...], preferred_element_type=f32)
    column = lax.broadcasted_iota(jnp.int32, logits.shape, 1)
    logits = jnp.where(column < experts - 1, logits, MASK_VALUE)
    ex = jnp.exp(logits - jnp.max(logits, axis=1, keepdims=True))
    probs[...] = ex / jnp.sum(ex, axis=1, keepdims=True)
    for start in range(0, 2 * hidden, 256):
        t = pl.ds(start, 256)
        gu[:, t] = jnp.dot(h2[...], w_in[:, t], preferred_element_type=f32)
    for start in range(0, hidden, 128):
        ta, tb = pl.ds(start, 128), pl.ds(hidden + start, 128)
        a, b = gu[:, ta], gu[:, tb]
        sig = jax.nn.sigmoid(a)
        silu = a * sig
        hs[:, ta] = (silu * b).astype(bf16)
        gu[:, ta] = b * (sig * (1.0 + a * (1.0 - sig)))
        gu[:, tb] = silu
    for start in range(0, hidden, 256):
        n = min(256, hidden - start)
        dhs = lax.dot_general(cb[own, :], w_down[pl.ds(start, n), :], NT, preferred_element_type=f32)
        for t in (pl.ds(start, n), pl.ds(hidden + start, n)):
            dgu[:, t] = (dhs * gu[:, t]).astype(bf16)
    for start in range(0, width, 256):
        t = pl.ds(start, 256)
        shared_out[:, t] = jnp.dot(hs[...], w_down[:, t], preferred_element_type=f32)
        grad_h2[:, t] = lax.dot_general(dgu[...], w_in[t, :], NT, preferred_element_type=f32)
    for start in range(0, 2 * hidden, 256):
        t = pl.ds(start, 256)
        grad = lax.dot_general(h2[...], dgu[:, t], TN, preferred_element_type=f32)
        store_grad(grad, t, rows, mine, grads)
    for start in range(0, hidden, 256):
        n = min(256, hidden - start)
        grad = lax.dot_general(cb[own, :], hs[:, pl.ds(start, n)], TN, preferred_element_type=f32)
        store_grad(grad, pl.ds(2 * hidden + start, n), rows, mine, grads)


def shared_expert(core, h2, cb, w_in, w_down, w_router, rows, experts):
    tokens, width = h2.shape
    hidden = w_down.shape[0]
    f32, bf16 = jnp.float32, jnp.bfloat16
    sd = jax.ShapeDtypeStruct
    vmem = pl.BlockSpec(memory_space=pltpu.VMEM)
    grads = [sd((width // 2, 3 * hidden), bf16)] * 2 if rows else [sd((width, 3 * hidden), bf16)]
    outs = [sd((tokens, width), f32), sd((tokens, width), f32), sd((tokens, w_router.shape[1]), f32)] + grads
    return pl.pallas_call(
        lambda *r: shared_kernel(rows, experts, *r),
        in_specs=[pl.BlockSpec(memory_space=pltpu.SMEM)] + [vmem] * 5,
        out_specs=[vmem] * len(outs),
        out_shape=outs,
        scratch_shapes=[pltpu.VMEM((tokens, 2 * hidden), f32), pltpu.VMEM((tokens, hidden), bf16), pltpu.VMEM((tokens, 2 * hidden), bf16)],
        compiler_params=pltpu.CompilerParams(vmem_limit_bytes=48 * 2**20),
        cost_estimate=pl.CostEstimate(flops=0, bytes_accessed=0, transcendentals=0),
        name="shared_expert",
    )(core, h2, cb, w_in, w_down, w_router)


def middle_kernel(experts, length_ref, home_a, home_b, home_c, grad_shared, probs, h2, w_router, x_mid, dout, gain, grad_mid, da, small):
    f32, bf16 = jnp.float32, jnp.bfloat16
    tokens = x_mid.shape[0]
    own, table = pl.ds(0, tokens), pl.ds(tokens, 2 * experts)
    total = lambda r, c: home_a[r, c].astype(f32) + home_b[r, c].astype(f32) + home_c[r, c].astype(f32)
    dots = total(table, own)
    dots = dots[:experts] + dots[experts:]
    grad_probs = jnp.concatenate([dots, jnp.zeros((128 - experts, tokens), f32)], axis=0).T
    p = probs[...]
    low = (p * (grad_probs - jnp.sum(grad_probs * p, axis=1, keepdims=True))).astype(bf16)
    incoming = total(own, slice(None)) + grad_shared[...]
    incoming += lax.dot_general(low, w_router[...], NT, preferred_element_type=f32)
    mid = x_mid[...]
    inverse = lax.rsqrt(jnp.mean(mid * mid, axis=-1, keepdims=True) + NORM_EPS)
    scaled = mid * inverse
    column = lax.broadcasted_iota(jnp.int32, (tokens, 128), 1)
    small[...] = lax.dot_general(h2[...], low, TN, preferred_element_type=f32) + lax.dot_general(
        incoming * scaled, jnp.where(column == experts, 1.0, 0.0), TN,
        precision=lax.Precision.HIGHEST, preferred_element_type=f32,
    )
    inner = incoming * gain[...]
    back = inverse * (inner - scaled * jnp.mean(inner * scaled, axis=-1, keepdims=True))
    grad = dout[...].astype(f32) + back
    grad_mid[...] = grad
    live = lax.broadcasted_iota(jnp.int32, (tokens, 1), 0) < length_ref[0]
    da[...] = jnp.where(live, grad, 0.0).astype(bf16)


def middle_back(lengths, home, grad_shared, probs, h2, w_router, x_mid, dout, gain, experts):
    tokens, width = x_mid.shape
    f32 = jnp.float32
    sd = jax.ShapeDtypeStruct
    vmem = pl.BlockSpec(memory_space=pltpu.VMEM)
    return pl.pallas_call(
        lambda *r: middle_kernel(experts, *r),
        in_specs=[pl.BlockSpec(memory_space=pltpu.SMEM)] + [vmem] * 10,
        out_specs=[vmem] * 3,
        out_shape=[sd((tokens, width), f32), sd((tokens, width), jnp.bfloat16), sd((width, 128), f32)],
        compiler_params=pltpu.CompilerParams(vmem_limit_bytes=48 * 2**20),
        cost_estimate=pl.CostEstimate(flops=0, bytes_accessed=0, transcendentals=0),
        name="middle_back",
    )(lengths, *home, grad_shared, probs, h2, w_router, x_mid, dout, gain)


def weight_grad_kernel(parts, bit, index_ref, lhs, rhs, keep, away):
    f32, bf16 = jnp.float32, jnp.bfloat16
    grad = lax.dot_general(lhs[0], rhs[0], TN, preferred_element_type=f32)
    mine = ((index_ref[0] >> bit) & 1) == 0
    rows = grad.shape[0] // parts
    at = 0
    for c in range(parts):
        if (c >> bit) & 1:
            continue
        other = c | (1 << bit)
        first = grad[c * rows : (c + 1) * rows]
        second = grad[other * rows : (other + 1) * rows]
        keep[pl.ds(at, rows), :] = jnp.where(mine, first, second).astype(bf16)
        away[pl.ds(at, rows), :] = jnp.where(mine, second, first).astype(bf16)
        at += rows


def weight_grad(index, lhs, rhs, expert, parts, bit):
    _, rows, m = lhs.shape
    n = rhs.shape[2]
    return pl.pallas_call(
        lambda *r: weight_grad_kernel(parts, bit, *r),
        grid=(n // 256,),
        in_specs=[
            pl.BlockSpec(memory_space=pltpu.SMEM),
            pl.BlockSpec((1, rows, m), lambda i: (expert, 0, 0)),
            pl.BlockSpec((1, rows, 256), lambda i: (expert, 0, i)),
        ],
        out_specs=[pl.BlockSpec((m // 2, 256), lambda i: (0, i))] * 2,
        out_shape=[jax.ShapeDtypeStruct((m // 2, n), jnp.bfloat16)] * 2,
        compiler_params=pltpu.CompilerParams(vmem_limit_bytes=48 * 2**20),
        cost_estimate=pl.CostEstimate(flops=0, bytes_accessed=0, transcendentals=0),
        name="weight_grad",
    )(index, lhs, rhs)


def rope_tables(seq_slots):
    half_dim = HEAD_DIM // 2
    inv_freq = 1.0 / 10000.0 ** (jnp.arange(half_dim, dtype=jnp.float32) * 2.0 / HEAD_DIM)
    angles = jnp.arange(seq_slots, dtype=jnp.float32)[:, None] * inv_freq[None, :]
    cosine, sine = jnp.cos(angles), jnp.sin(angles)
    return jnp.concatenate([cosine, cosine], axis=1), jnp.concatenate([-sine, sine], axis=1)


def swap_cores(values_in):
    owners = lax.axis_size("expert")
    return lax.ppermute(values_in, "expert", [(i, i ^ 1) for i in range(owners)])


def next_chip(values_in):
    owners = lax.axis_size("expert")
    return lax.ppermute(values_in, "expert", [(i, (i + 2) % owners) for i in range(owners)])


def axis_bits(name):
    return [(name, bit) for bit in range(lax.axis_size(name).bit_length() - 1)]


def row_bits():
    return axis_bits("dp")[::-1] + axis_bits("expert")[::-1]


def sum_terms(parts):
    summed = parts[0].astype(jnp.float32)
    for term in parts[1:]:
        summed = summed + term.astype(jnp.float32)
    return summed


def after(values_in, *earlier):
    return lax.optimization_barrier((values_in, earlier))[0]


class Scatter:
    def __init__(self, terms, open_bits, order):
        self.terms, self.open_bits, self.order = list(terms), list(open_bits), list(order)

    def advance(self, *earlier):
        name, bit = self.order.pop(0)
        dim = self.open_bits.index((name, bit))
        mine = (lax.axis_index(name) >> bit) & 1
        terms = after(self.terms, *earlier) if earlier else self.terms
        pick = lambda term, index: lax.dynamic_index_in_dim(term, index, dim, keepdims=False)
        away = sum_terms([pick(term, 1 - mine) for term in terms]).astype(terms[0].dtype)
        came = lax.ppermute(
            away, name, [(i, i ^ (1 << bit)) for i in range(lax.axis_size(name))]
        )
        self.terms = [pick(term, mine) for term in terms] + [came]
        self.open_bits.pop(dim)
        return away

    def finish(self):
        while self.order:
            self.advance()
        return sum_terms(self.terms)


def split_rows(part, bits):
    rows = part.shape[0] >> len(bits)
    return part.reshape((2,) * len(bits) + (rows, part.shape[1]))


def scatter_orders():
    core, *line = axis_bits("expert")
    plane = axis_bits("dp")
    return ([core] + plane + line, [core] + plane[::-1] + line, [core] + plane + line)


def per_device(
    layer_input,
    lengths,
    expert_ids,
    norm1,
    w_qkv,
    w_out,
    norm2,
    w_router,
    w_shared_in,
    w_shared_down,
    w_expert_in,
    w_expert_down,
    dout,
):
    seq_slots, width = layer_input.shape
    top_k = expert_ids.shape[1]
    experts = w_router.shape[1]
    local_experts = w_expert_in.shape[0]
    hidden_units = w_shared_down.shape[0]
    capacity = (seq_slots * top_k // (experts - 1) // 8 + 1) * 8
    live_col = (jnp.arange(seq_slots, dtype=jnp.int32) < lengths[0]).astype(jnp.float32)[:, None]
    cosine, sine = rope_tables(seq_slots)

    bits = row_bits()
    rows = width >> len(bits)
    rows = rows if rows % 8 == 0 else 0
    core = (lax.axis_index("expert") & 1).astype(jnp.int32)[None]
    orders = scatter_orders()
    chips = experts // local_experts // 2
    first_expert = (lax.axis_index("expert") * local_experts).astype(jnp.int32)[None]
    router_t = w_router.T

    def start_scatter(grads, order):
        if rows:
            terms = [split_rows(grads[0], bits[:-1]), split_rows(swap_cores(grads[1]), bits[:-1])]
            return Scatter(terms, bits[:-1], order[1:])
        return Scatter([split_rows(grads[0], bits)], bits, order)

    def run_step(step, h2_pair, grad_pair, kept, *earlier):
        sums, kept = expert_step(
            first_expert, after(h2_pair[0], *earlier), h2_pair[1], grad_pair[0], grad_pair[1],
            router_t, w_expert_in, w_expert_down, step, chips, capacity, kept,
        )
        parts.append(sums)
        return kept, sums[0]

    parts = []
    router_wide = jnp.pad(w_router, ((0, 0), (0, 128 - experts)))
    grad_table = token_rows(lengths, expert_ids, dout, experts)
    grad_here = (grad_table, swap_cores(grad_table))
    grad_next = next_chip(grad_table)
    counts_here = jnp.sum((grad_table[seq_slots:, :seq_slots] >= 0).astype(jnp.int32), axis=1)
    places = jnp.minimum(jnp.arange(width >> len(bits), dtype=jnp.int32), 30)
    digits = ((counts_here[None, :] >> places[:, None]) & 1).astype(jnp.float32)
    small_columns = -(-(2 * experts + 2) // 128) * 128
    digits = jnp.pad(
        jnp.tile(digits, (1 << len(bits), 1)),
        ((0, 0), (experts + 2, small_columns - 2 * experts - 2)),
    )
    h1_low, queries, keys_in, values_in, attended_low, log_norm, x_mid, h2_low = attention_forward(
        lengths, after(layer_input, grad_table), norm1[None, :], w_qkv, cosine, sine, w_out,
        norm2[None, :],
    )
    h2_here = (h2_low, swap_cores(h2_low))
    h2_next = next_chip(h2_low)
    grad_next = after(grad_next, h2_low)
    grad_other = swap_cores(grad_next)
    grad_ahead = next_chip(grad_next)
    kept, done = run_step(0, h2_here, grad_here, None, grad_next)
    shared_out, grad_shared, router_probs, *shared_grads = shared_expert(
        core, after(h2_low, done), grad_table, w_shared_in, w_shared_down, router_wide, rows, experts
    )
    shared_scatter = start_scatter(after(shared_grads, h2_next, grad_ahead), orders[0])
    fence = shared_out
    shared_away = []
    swapped = [swap_cores(after(parts[0][3], fence, h2_next, grad_ahead))]
    travelling = None
    for step in range(1, chips):
        h2_next, grad_next = after(h2_next, fence), after(grad_next, fence)
        pair_h2 = (h2_next, swap_cores(h2_next))
        pair_grad = (grad_next, grad_other)
        earlier = [] if travelling is None else [travelling]
        earlier += shared_away
        if step + 1 < chips:
            h2_next = next_chip(h2_next)
            grad_next = after(grad_ahead, fence)
            grad_other = swap_cores(grad_next)
            if step + 2 < chips:
                grad_ahead = next_chip(grad_next)
        kept, fence = run_step(step, pair_h2, pair_grad, kept, *earlier)
        mine, theirs = parts[step][:2]
        if step + 1 < chips:
            theirs = after(theirs, h2_next, grad_ahead)
        theirs = after(theirs, *swapped)
        swapped.append(swap_cores(after(parts[step][3], theirs)))
        if shared_away:
            theirs = after(theirs, shared_scatter.terms[-1])
        if travelling is None:
            total = mine.astype(jnp.float32) + swap_cores(theirs).astype(jnp.float32)
        else:
            came = next_chip(travelling)
            total = (
                mine.astype(jnp.float32)
                + swap_cores(after(theirs, came)).astype(jnp.float32)
                + came.astype(jnp.float32)
            )
        travelling = total.astype(mine.dtype)
        if shared_scatter.order[0][0] == "dp":
            shared_away = [shared_scatter.advance(fence)]

    home_hop = next_chip(travelling)
    rows_held, grad_result, expert_hidden, grad_expert_gu = kept

    plane = axis_bits("dp")
    plane_index = lax.axis_index("dp").astype(jnp.int32)[None]

    def expert_grads(lhs, rhs, expert):
        order = plane if expert % 2 == 0 else plane[::-1]
        return order, weight_grad(
            plane_index, lhs, rhs, expert, 1 << len(plane), order[0][1]
        )

    def plane_scatter(order, grads, *earlier):
        name, bit = order[0]
        keep, away = after(grads, *earlier)
        came = lax.ppermute(
            away, name, [(i, i ^ (1 << bit)) for i in range(lax.axis_size(name))]
        )
        open_bits = [place for place in plane[::-1] if place != order[0]]
        terms = [split_rows(piece, open_bits) for piece in (keep, came)]
        return Scatter(terms, open_bits, order[1:])

    fence = [travelling, shared_scatter.terms[-1]]
    down_parts, in_parts = [], []
    for i in range(local_experts):
        down_parts.append(
            expert_grads(after(expert_hidden, *fence), grad_result, i)
        )
        fence = down_parts[-1][1]
    down_scatters = [plane_scatter(*part, *fence) for part in down_parts]
    fence = list(fence) + [shared_scatter.advance(*fence)]
    for i in range(local_experts):
        in_parts.append(expert_grads(after(rows_held, *fence), grad_expert_gu, i))
        fence = in_parts[-1][1]
    there = [home_hop, swapped[-1], shared_scatter.terms[-1]] + [scatter.terms[-1] for scatter in down_scatters]
    in_scatters = [plane_scatter(*part, *there, *fence) for part in in_parts]
    fence = list(fence) + there + [shared_scatter.advance(*there)]

    mine, theirs = parts[0][:2]
    home = after((mine, swap_cores(theirs), home_hop), *fence)
    grad_mid, grad_attn_branch, small = middle_back(
        lengths, home, grad_shared, router_probs, h2_low, router_wide, x_mid, dout, norm2[None, :],
        experts,
    )
    small = digits + jnp.pad(small, ((0, 0), (0, small_columns - 128)))
    out_order = list(range(1, chips)) + [0]

    def add_routed(index, came, *earlier):
        mine, theirs = after((parts[out_order[index]][2], swapped[out_order[index]]), *earlier)
        total = mine.astype(jnp.float32) + theirs.astype(jnp.float32)
        return total if came is None else total + came.astype(jnp.float32)

    out_hop = next_chip(add_routed(0, None, *fence).astype(jnp.bfloat16))

    pairs = width // (2 * HEAD_DIM)
    half = (pairs - 1) // 2
    cuts = (0, pairs - 2 * half, pairs - half, pairs)
    running = None
    scatters, pending = [], []
    fence = (grad_attn_branch,)
    column_orders = (orders[0], orders[0], orders[1])
    for index, (first, last) in enumerate(zip(cuts[:-1], cuts[1:])):
        tail = None
        if last == pairs:
            tail = (experts, (layer_input, norm1[None, :], grad_mid, small))
        *grads, running = attention_backward(
            lengths, core, after(grad_attn_branch, *fence), w_out, queries, keys_in, values_in,
            log_norm, cosine, sine, h1_low, attended_low, w_qkv, running, first, last - first, rows,
            tail,
        )
        fence = [running]
        if index == 0:
            scatters.append(start_scatter(grads, column_orders[0]))
        elif index == 1:
            landed = [scatter.terms[-1] for scatter in in_scatters]
            landed += [running, out_hop, shared_scatter.terms[-1]]
            scatters.append(start_scatter(after(grads, *landed), column_orders[1]))
            fence = [scatters[0].advance(*landed)]
            routed = add_routed(1, out_hop, *fence).astype(jnp.bfloat16)
            out_hop = next_chip(routed)
            fence.append(routed)
        else:
            landed = [running, out_hop, scatters[0].terms[-1]]
            scatters.append(start_scatter(after(grads, *landed), column_orders[2]))
    grad_input = running
    first_cols, second_cols, third_cols = scatters
    fence = second_cols.advance(*landed)
    hops = 2
    rest = [third_cols, first_cols, None, second_cols, third_cols, first_cols] + in_scatters
    rest += down_scatters + [second_cols, third_cols, first_cols, second_cols, third_cols]
    for scatter in rest:
        if scatter is not None:
            if scatter.order:
                fence = scatter.advance(fence)
        elif hops < chips:
            routed = add_routed(hops, out_hop, fence)
            hops, fence = hops + 1, routed
            if hops < chips:
                out_hop = next_chip(routed.astype(jnp.bfloat16))
    while hops < chips:
        routed = add_routed(hops, out_hop, fence)
        out_hop = next_chip(routed.astype(jnp.bfloat16))
        hops += 1
    result = (x_mid + live_col * (shared_out + routed)).astype(jnp.bfloat16)
    shared_sum = shared_scatter.finish()
    expert_in_sum = jnp.stack([scatter.finish() for scatter in in_scatters])
    expert_down_sum = jnp.stack([scatter.finish() for scatter in down_scatters])
    pieces = []
    for scatter, first, last in zip(scatters, cuts[:-1], cuts[1:]):
        piece = scatter.finish().reshape(width >> len(bits), last - first, -1)
        small_sum = piece[:, -1, 8 * HEAD_DIM :]
        piece = piece[:, :, : 8 * HEAD_DIM].reshape(-1, last - first, 4, 2 * HEAD_DIM)
        pieces.append(piece.transpose(0, 2, 1, 3).reshape(piece.shape[0], 4, -1))
    pieces = jnp.concatenate(pieces, axis=2)
    counts = jnp.sum(
        small_sum[:, experts + 2 : 2 * experts + 2] * (1 << places).astype(jnp.float32)[:, None],
        axis=0,
    )
    return (
        result,
        grad_input,
        small_sum[:, experts + 1],
        pieces[:, :3].reshape(-1, 3 * width),
        pieces[:, 3],
        small_sum[:, experts],
        small_sum[:, :experts],
        shared_sum[:, : 2 * hidden_units],
        shared_sum[:, 2 * hidden_units :].T,
        expert_in_sum,
        expert_down_sum,
        counts.astype(jnp.int32),
    )


def solution(mesh):
    return jax.shard_map(
        per_device,
        mesh=mesh,
        in_specs=(
            P(("dp", "expert"), None),
            P(("dp", "expert")),
            P(("dp", "expert"), None),
            P(),
            P(),
            P(),
            P(),
            P(),
            P(),
            P(),
            P("expert", None, None),
            P("expert", None, None),
            P(("dp", "expert"), None),
        ),
        out_specs=(
            P(("dp", "expert"), None),
            P(("dp", "expert"), None),
            P(("dp", "expert")),
            P(("dp", "expert"), None),
            P(("dp", "expert"), None),
            P(("dp", "expert")),
            P(("dp", "expert"), None),
            P(("dp", "expert"), None),
            P(None, ("dp", "expert")),
            P("expert", "dp", None),
            P("expert", "dp", None),
            P(),
        ),
        check_vma=False,
    )
```

```python
import jax
import jax.numpy as jnp
from jax import lax
from jax.experimental import pallas as pl
from jax.experimental.pallas import tpu as pltpu
from jax.sharding import PartitionSpec as P

HEAD_DIM = 128
NORM_EPS = 1e-06
MASK_VALUE = -1e30
NT = (((1,), (1,)), ((), ()))
TN = (((0,), (0,)), ((), ()))

def turn(values_in, cosine, signed_sine):
    return values_in * cosine + pltpu.roll(values_in, HEAD_DIM // 2, 1) * signed_sine

def block_scores(q, k, start, seq_length):
    s = lax.dot_general(q, k, NT, preferred_element_type=jnp.float32) * HEAD_DIM ** (-0.5)
    query_pos = start + lax.broadcasted_iota(jnp.int32, s.shape, 0)
    key_pos = lax.broadcasted_iota(jnp.int32, s.shape, 1)
    return jnp.where((key_pos <= query_pos) & (key_pos < seq_length), s, MASK_VALUE)

def attention_kernel(length_ref, x, norm1, wq, wk, wv, cosine, sine, w_out, norm2, h1, q_o, k_o, v_o, att, lse, x_mid, h2):
    f32, bf16 = jnp.float32, jnp.bfloat16
    p = pl.program_id(0)
    tokens = x.shape[0]
    seq_length = length_ref[0]
    span = min(256, tokens)

    @pl.when(p == 0)
    def _():
        xf = x[...].astype(f32)
        inverse = lax.rsqrt(jnp.mean(xf * xf, axis=-1, keepdims=True) + NORM_EPS)
        h1[...] = (xf * inverse * norm1[...]).astype(bf16)
        lse[...] = jnp.zeros_like(lse)

    for w, o in ((wq, q_o), (wk, k_o), (wv, v_o)):
        full = jnp.dot(h1[...], w[...], preferred_element_type=f32)
        for j in (0, 1):
            part = full[:, j * HEAD_DIM:(j + 1) * HEAD_DIM]
            if w is not wv:
                part = turn(part, cosine[...], sine[...])
            o[:, pl.ds(j * HEAD_DIM, HEAD_DIM)] = part.astype(bf16)
    lane = lax.broadcasted_iota(jnp.int32, (span, lse.shape[1]), 1)
    for j in (0, 1):
        cols = pl.ds(j * HEAD_DIM, HEAD_DIM)
        for start in range(0, tokens, span):
            rows = pl.ds(start, span)
            seen = pl.ds(0, start + span)
            s = block_scores(q_o[rows, cols], k_o[seen, cols], start, seq_length)
            high = jnp.max(s, axis=-1, keepdims=True)
            ex = jnp.exp(s - high)
            total = jnp.sum(ex, axis=-1, keepdims=True)
            low = (ex / total).astype(bf16)
            out = jnp.dot(low, v_o[seen, cols], preferred_element_type=f32)
            att[rows, pl.ds(pl.multiple_of(p * 2 * HEAD_DIM + j * HEAD_DIM, HEAD_DIM), HEAD_DIM)] = out.astype(bf16)
            lse[rows, :] = jnp.where(lane == 2 * p + j, high + jnp.log(total), lse[rows, :])

    @pl.when(p == pl.num_programs(0) - 1)
    def _():
        branch = jnp.dot(att[...], w_out[...], preferred_element_type=f32)
        live = lax.broadcasted_iota(jnp.int32, (tokens, 1), 0) < seq_length
        mid = x[...].astype(f32) + jnp.where(live, branch, 0.0)
        x_mid[...] = mid
        inverse = lax.rsqrt(jnp.mean(mid * mid, axis=-1, keepdims=True) + NORM_EPS)
        h2[...] = (mid * inverse * norm2[...]).astype(bf16)

def whole(a):
    return pl.BlockSpec(a.shape, lambda p: (0,) * len(a.shape), pipeline_mode=pl.Buffered(1))

def attention_forward(lengths, x, norm1, w_qkv, cosine, sine, w_out, norm2):
    tokens, width = x.shape
    pairs = width // (2 * HEAD_DIM)
    f32, bf16 = jnp.float32, jnp.bfloat16
    wide = 2 * HEAD_DIM
    col = lambda k: pl.BlockSpec((width, wide), lambda p, k=k: (0, k * pairs + p))
    head = pl.BlockSpec((tokens, wide), lambda p: (0, p))
    full = pl.BlockSpec((tokens, width), lambda p: (0, 0))
    sd = jax.ShapeDtypeStruct
    return pl.pallas_call(
        attention_kernel, grid=(pairs,),
        in_specs=[pl.BlockSpec(memory_space=pltpu.SMEM), whole(x), whole(norm1), col(0), col(1), col(2), whole(cosine), whole(sine), whole(w_out), whole(norm2)],
        out_specs=[full, head, head, head, full, pl.BlockSpec((tokens, 128), lambda p: (0, 0)), full, full],
        out_shape=[pltpu.HBM((tokens, width), bf16)] * 5 + [pltpu.HBM((tokens, 128), f32), pltpu.HBM((tokens, width), f32), pltpu.HBM((tokens, width), bf16)],
        compiler_params=pltpu.CompilerParams(vmem_limit_bytes=48 * 2**20),
        cost_estimate=pl.CostEstimate(flops=0, bytes_accessed=0, transcendentals=0),
        name="attention_forward",
    )(lengths, x, norm1, w_qkv, w_qkv, w_qkv, cosine, sine, w_out, norm2)

def attention_back_kernel(rows, extra, carried, length_ref, core_ref, da, w_out, q, k, v, lse, cosine, sine, h1, att, wq, wk, wv, *rest):
    f32, bf16 = jnp.float32, jnp.bfloat16
    dh1_in = None
    if carried:
        dh1_in, *rest = rest
    if extra:
        x, gain, grad_mid, small, *rest = rest
    *grads, dh1, dk_s, dv_s, dproj = rest
    p = pl.program_id(0)
    pair = length_ref[1] + p
    tokens, width = da.shape
    seq_length = length_ref[0]
    span = min(256, tokens)
    scale = HEAD_DIM ** (-0.5)
    mine = core_ref[0] == 0
    wide = 2 * HEAD_DIM
    do_full = lax.dot_general(da[...], w_out[...], NT, preferred_element_type=f32).astype(bf16)
    lane = lax.broadcasted_iota(jnp.int32, (span, lse.shape[1]), 1)
    back_sine = -sine[...]
    for j in (0, 1):
        cols = pl.ds(j * HEAD_DIM, HEAD_DIM)
        do_head = do_full[:, j * HEAD_DIM : (j + 1) * HEAD_DIM]
        for start in range(tokens - span, -1, -span):
            r = pl.ds(start, span)
            seen = pl.ds(0, start + span)
            s = block_scores(q[r, cols], k[seen, cols], start, seq_length)
            norm = jnp.sum(jnp.where(lane == 2 * pair + j, lse[r, :], 0.0), axis=1, keepdims=True)
            probs = jnp.exp(s - norm)
            do = do_head[start : start + span]
            dp = lax.dot_general(do, v[seen, cols], NT, preferred_element_type=f32)
            row = jnp.sum(dp * probs, axis=1, keepdims=True)
            ds = (probs * (dp - row)).astype(bf16)
            dq = jnp.dot(ds, k[seen, cols], preferred_element_type=f32) * scale
            dproj[r, pl.ds(j * HEAD_DIM, HEAD_DIM)] = turn(
                dq, cosine[r, :], back_sine[start : start + span]
            ).astype(bf16)
            dk = lax.dot_general(ds, q[r, cols], TN, preferred_element_type=f32) * scale
            dv = lax.dot_general(probs.astype(bf16), do, TN, preferred_element_type=f32)
            if start == tokens - span:
                dk_s[seen, :] = dk
                dv_s[seen, :] = dv
            else:
                dk_s[seen, :] += dk
                dv_s[seen, :] += dv
        dproj[:, pl.ds(wide + j * HEAD_DIM, HEAD_DIM)] = turn(dk_s[...], cosine[...], back_sine).astype(bf16)
        dproj[:, pl.ds(2 * wide + j * HEAD_DIM, HEAD_DIM)] = dv_s[...].astype(bf16)
    total = jnp.where(p == 0, dh1_in[...] if carried else 0.0, dh1[...])
    for i, w in enumerate((wq, wk, wv)):
        part = dproj[:, pl.ds(i * wide, wide)]
        grad = lax.dot_general(h1[...], part, TN, preferred_element_type=f32)
        store_grad(grad, pl.ds(i * wide, wide), rows, mine, grads)
        total += lax.dot_general(part, w[...], NT, preferred_element_type=f32)
    part = da[:, pl.ds(pl.multiple_of(pair * wide, wide), wide)]
    grad = lax.dot_general(att[...], part, TN, preferred_element_type=f32)
    store_grad(grad, pl.ds(3 * wide, wide), rows, mine, grads)
    dh1[...] = total
    if not extra:
        return

    @pl.when(p < pl.num_programs(0) - 1)
    def _():
        store_grad(jnp.zeros(small.shape, f32), pl.ds(4 * wide, small.shape[1]), rows, mine, grads)

    @pl.when(p == pl.num_programs(0) - 1)
    def _():
        full = x[...].astype(f32)
        inverse = lax.rsqrt(jnp.mean(full * full, axis=-1, keepdims=True) + NORM_EPS)
        scaled = full * inverse
        inner = total * gain[...]
        dh1[...] = grad_mid[...] + inverse * (
            inner - scaled * jnp.mean(inner * scaled, axis=-1, keepdims=True)
        )
        column = lax.broadcasted_iota(jnp.int32, (tokens, small.shape[1]), 1)
        grad = small[...] + lax.dot_general(
            total * scaled, jnp.where(column == extra + 1, 1.0, 0.0), TN,
            precision=lax.Precision.HIGHEST, preferred_element_type=f32,
        )
        store_grad(grad, pl.ds(4 * wide, small.shape[1]), rows, mine, grads)


def attention_backward(lengths, core, da, w_out, q, k, v, lse, cosine, sine, h1, att, w_qkv, dh1_in, first, count, rows, tail):
    tokens, width = da.shape
    pairs = width // (2 * HEAD_DIM)
    wide = 2 * HEAD_DIM
    f32, bf16 = jnp.float32, jnp.bfloat16
    col = lambda k: pl.BlockSpec((width, wide), lambda p, k=k: (0, k * pairs + first + p))
    head = pl.BlockSpec((tokens, wide), lambda p: (0, first + p))
    sd = jax.ShapeDtypeStruct
    smem = pl.BlockSpec(memory_space=pltpu.SMEM)
    n = width // 2 if rows else width
    extra, tail_args = tail if tail else (0, ())
    columns = 4 * wide + (tail_args[-1].shape[1] if extra else 0)
    grads = [sd((n, count * columns), bf16)] * (2 if rows else 1)
    carried = dh1_in is not None
    tail_args = ((dh1_in,) if carried else ()) + tuple(tail_args)
    whole_args = (da, lse, cosine, sine, h1, att) + tail_args
    spec = {id(a): whole(a) for a in whole_args}
    return pl.pallas_call(
        lambda *r: attention_back_kernel(rows, extra, carried, *r),
        grid=(count,),
        in_specs=[smem, smem, spec[id(da)], pl.BlockSpec((wide, width), lambda p: (first + p, 0)), head, head, head]
        + [spec[id(a)] for a in (lse, cosine, sine, h1, att)]
        + [col(0), col(1), col(2)]
        + [spec[id(a)] for a in tail_args],
        out_specs=[pl.BlockSpec((n, columns), lambda p: (0, p))] * len(grads)
        + [pl.BlockSpec((tokens, width), lambda p: (0, 0))],
        out_shape=grads + [sd((tokens, width), f32)],
        scratch_shapes=[pltpu.VMEM((tokens, HEAD_DIM), f32), pltpu.VMEM((tokens, HEAD_DIM), f32), pltpu.VMEM((tokens, 3 * wide), bf16)],
        compiler_params=pltpu.CompilerParams(vmem_limit_bytes=48 * 2**20),
        cost_estimate=pl.CostEstimate(flops=0, bytes_accessed=0, transcendentals=0),
        name="attention_backward",
    )(
        jnp.concatenate([lengths, jnp.full((1,), first, jnp.int32)]), core, da, w_out, q, k, v,
        lse, cosine, sine, h1, att, w_qkv, w_qkv, w_qkv, *tail_args,
    )


def expert_kernel(cap, tokens, hidden, last_slot, *refs):
    (first_ref, h2a, h2b, cba, cbb, wr, w_in, w_down) = refs[:8]
    (dra, drb, outa, outb, rows_o, dy_o, act_o, dgu_o, gu, cbrow, oh, gy, drs, probs, dots) = refs[-15:]
    f32, bf16 = jnp.float32, jnp.bfloat16
    e = pl.program_id(0)
    experts = wr.shape[0]
    width = wr.shape[1]
    mine = first_ref[0] + e
    table_rows = probs.shape[1]

    @pl.when(e == 0)
    def _():
        for src, h2 in ((0, h2a), (1, h2b)):
            logits = lax.dot_general(wr[...], h2[...], (((1,), (1,)), ((), ())), preferred_element_type=f32)
            row = lax.broadcasted_iota(jnp.int32, logits.shape, 0)
            logits = jnp.where(row < experts - 1, logits, MASK_VALUE)
            ex = jnp.exp(logits - jnp.max(logits, axis=0, keepdims=True))
            probs[src] = ex / jnp.sum(ex, axis=0, keepdims=True)
            dots[src] = jnp.zeros_like(probs[src])

    gates = []
    masks = []
    for src, h2, cb in ((0, h2a, cba), (1, h2b, cbb)):
        row_id = lax.broadcasted_iota(jnp.int32, (table_rows, tokens), 0)
        table = cb[pl.ds(tokens, table_rows), pl.ds(0, tokens)].astype(f32)
        rank = jnp.sum(jnp.where(row_id == mine, table, 0.0), axis=0, keepdims=True)
        prob = jnp.sum(jnp.where(row_id == mine, probs[src], 0.0), axis=0, keepdims=True)
        hit = lax.broadcasted_iota(jnp.int32, (cap, tokens), 0).astype(f32) == rank
        masks.append(hit)
        gates.append(jnp.sum(jnp.where(hit, prob, 0.0), axis=1, keepdims=True))
        onehot = jnp.where(hit, 1.0, 0.0).astype(bf16)
        oh[src, pl.ds(e * cap, cap), :] = onehot
        half = pl.ds(src * cap, cap)
        @pl.loop(0, width // 256, unroll=True)
        def _(i):
            t = pl.ds(pl.multiple_of(i * 256, 256), 256)
            rows_o[0, half, t] = jnp.dot(onehot, h2[:, t], preferred_element_type=f32).astype(bf16)
            cbrow[half, t] = jnp.dot(onehot, cb[pl.ds(0, tokens), t], preferred_element_type=f32).astype(bf16)
    gate = jnp.concatenate(gates, axis=0)

    @pl.loop(0, 2 * hidden // 256, unroll=True)
    def _(i):
        t = pl.ds(pl.multiple_of(i * 256, 256), 256)
        gu[:, t] = jnp.dot(rows_o[0], w_in[0, :, t], preferred_element_type=f32)

    @pl.loop(0, hidden // 128, unroll=True)
    def _(i):
        ta = pl.ds(pl.multiple_of(i * 128, 128), 128)
        tb = pl.ds(pl.multiple_of(hidden + i * 128, 128), 128)
        a = gu[:, ta]
        b = gu[:, tb]
        sig = jax.nn.sigmoid(a)
        silu = a * sig
        act_o[0, :, ta] = (silu * b).astype(bf16)
        gu[:, ta] = b * (sig * (1.0 + a * (1.0 - sig)))
        gu[:, tb] = silu

    def down(i, dot):
        t = pl.ds(pl.multiple_of(i * 256, 256), 256)
        y = jnp.dot(act_o[0], w_down[0, :, t], preferred_element_type=f32).astype(bf16).astype(f32)
        c = cbrow[:, t].astype(f32)
        gyt = (gate * y).astype(bf16)
        for src in (0, 1):
            gy[src, pl.ds(e * cap, cap), t] = gyt[src * cap:(src + 1) * cap]
        dy_o[0, :, t] = (gate * c).astype(bf16)
        return dot + jnp.sum(y * c, axis=1, keepdims=True)
    dot = lax.fori_loop(0, width // 256, down, jnp.zeros((2 * cap, 1), f32), unroll=True)
    for src in (0, 1):
        back = jnp.sum(jnp.where(masks[src], dot[src * cap:(src + 1) * cap], 0.0), axis=0, keepdims=True)
        row_id = lax.broadcasted_iota(jnp.int32, (table_rows, tokens), 0)
        dots[src] += jnp.where(row_id == mine, back, 0.0)

    for start in range(0, hidden, 256):
        n = min(256, hidden - start)
        dact = lax.dot_general(dy_o[0], w_down[0, pl.ds(start, n), :], (((1,), (1,)), ((), ())), preferred_element_type=f32)
        dgu_o[0, :, pl.ds(start, n)] = (dact * gu[:, pl.ds(start, n)]).astype(bf16)
        dgu_o[0, :, pl.ds(hidden + start, n)] = (dact * gu[:, pl.ds(hidden + start, n)]).astype(bf16)

    @pl.loop(0, width // 256, unroll=True)
    def _(i):
        t = pl.ds(pl.multiple_of(i * 256, 256), 256)
        dr = lax.dot_general(dgu_o[0], w_in[0, t, :], (((1,), (1,)), ((), ())), preferred_element_type=f32).astype(bf16)
        for src in (0, 1):
            drs[src, pl.ds(e * cap, cap), t] = dr[src * cap:(src + 1) * cap]

    @pl.when(e == pl.num_programs(0) - 1)
    def _():
        for src, dro, outo in ((0, dra, outa), (1, drb, outb)):
            @pl.loop(0, width // 256, unroll=True)
            def _(i):
                t = pl.ds(pl.multiple_of(i * 256, 256), 256)
                dims = (((0,), (0,)), ((), ()))
                outo[:, t] = lax.dot_general(oh[src], gy[src, :, t], dims, preferred_element_type=f32).astype(bf16)
                dro[pl.ds(0, tokens), t] = lax.dot_general(oh[src], drs[src, :, t], dims, preferred_element_type=f32).astype(bf16)
            hi = dots[src].astype(bf16)
            lo = (dots[src] - hi.astype(f32)).astype(bf16)
            pad = jnp.zeros((2 * table_rows, width - tokens), bf16)
            dro[pl.ds(tokens, table_rows), pl.ds(0, tokens)] = hi
            dro[pl.ds(tokens + table_rows, table_rows), pl.ds(0, tokens)] = lo
            dro[pl.ds(tokens, 2 * table_rows), pl.ds(tokens, width - tokens)] = pad

def expert_step(first, h2a, h2b, cba, cbb, wr, w_in, w_down, step, steps, cap, kept):
    tokens, width = h2a.shape
    local, _, hidden2 = w_in.shape
    hidden = hidden2 // 2
    table_rows = cba.shape[0] - tokens
    bf16, f32 = jnp.bfloat16, jnp.float32
    whole = lambda a: pl.BlockSpec(a.shape, lambda e: (0,) * a.ndim, pipeline_mode=pl.Buffered(1))
    ins = [pl.BlockSpec(memory_space=pltpu.SMEM)] + [whole(a) for a in (h2a, h2b, cba, cbb, wr)]
    ins += [pl.BlockSpec((1,) + w_in.shape[1:], lambda e: (e, 0, 0)), pl.BlockSpec((1,) + w_down.shape[1:], lambda e: (e, 0, 0))]
    kept_shapes = [jax.ShapeDtypeStruct((local, steps * 2 * cap, n), bf16) for n in (width, width, hidden, 2 * hidden)]
    sums = [jax.ShapeDtypeStruct((tokens + 2 * table_rows, width), bf16)] * 2 + [jax.ShapeDtypeStruct((tokens, width), bf16)] * 2
    args = [first, h2a, h2b, cba, cbb, wr, w_in, w_down]
    alias = {}
    if kept is not None:
        ins += [pl.BlockSpec(memory_space=pl.ANY)] * 4
        alias = {len(args) + i: 4 + i for i in range(4)}
        args += list(kept)
    outs = [pl.BlockSpec(s.shape, lambda e: (0, 0), pipeline_mode=pl.Buffered(1)) for s in sums]
    outs += [pl.BlockSpec((1, 2 * cap, s.shape[2]), lambda e: (e, step, 0)) for s in kept_shapes]
    rows = 2 * cap
    flops = 2 * local * rows * (2 * (3 * width * hidden) + 4 * tokens * width)
    res = pl.pallas_call(
        lambda *r: expert_kernel(cap, tokens, hidden, None, *r),
        grid=(local,),
        in_specs=ins, out_specs=outs, out_shape=[pltpu.HBM(x.shape, x.dtype) for x in sums + kept_shapes],
        scratch_shapes=[pltpu.VMEM((rows, 2 * hidden), f32), pltpu.VMEM((rows, width), bf16), pltpu.VMEM((2, local * cap, tokens), bf16),
                        pltpu.VMEM((2, local * cap, width), bf16), pltpu.VMEM((2, local * cap, width), bf16),
                        pltpu.VMEM((2, table_rows, tokens), f32), pltpu.VMEM((2, table_rows, tokens), f32)],
        input_output_aliases=alias,
        compiler_params=pltpu.CompilerParams(vmem_limit_bytes=50 * 2**20),
        cost_estimate=pl.CostEstimate(flops=0, bytes_accessed=0, transcendentals=0),
        name="expert_step",
    )(*args)
    return res[:4], res[4:]


def token_kernel(length_ref, ids, dout, rows_o):
    f32, bf16 = jnp.float32, jnp.bfloat16
    tokens = dout.shape[0]
    table_rows = rows_o.shape[0] - tokens
    live = lax.broadcasted_iota(jnp.int32, (tokens, 1), 0) < length_ref[0]
    rows_o[pl.ds(0, tokens), :] = jnp.where(live, dout[...].astype(f32), 0.0).astype(bf16)
    lane = lax.broadcasted_iota(jnp.int32, (tokens, 128), 1)
    picked = jnp.zeros((tokens, 128), f32)
    for k in range(ids.shape[1]):
        picked = jnp.where(lane == ids[:, k:k + 1], 1.0, picked)
    picked = jnp.where(live, picked, 0.0).astype(bf16)
    earlier = lax.broadcasted_iota(jnp.int32, (tokens, tokens), 0)
    later = lax.broadcasted_iota(jnp.int32, (tokens, tokens), 1)
    before = jnp.where(earlier < later, 1.0, 0.0).astype(bf16)
    same = jnp.where(earlier == later, 1.0, 0.0).astype(bf16)
    rank = lax.dot_general(picked, before, TN, preferred_element_type=f32)
    hit = lax.dot_general(picked, same, TN, preferred_element_type=f32)
    table = jnp.where(hit > 0.5, rank, -1.0)[:table_rows].astype(bf16)
    rows_o[pl.ds(tokens, table_rows), pl.ds(0, tokens)] = table
    rows_o[pl.ds(tokens, table_rows), pl.ds(tokens, dout.shape[1] - tokens)] = jnp.zeros(
        (table_rows, dout.shape[1] - tokens), bf16
    )


def token_rows(lengths, expert_ids, dout, experts):
    return pl.pallas_call(
        token_kernel,
        in_specs=[
            pl.BlockSpec(memory_space=pltpu.SMEM),
            pl.BlockSpec(memory_space=pltpu.VMEM),
            pl.BlockSpec(memory_space=pltpu.VMEM),
        ],
        out_specs=pl.BlockSpec(memory_space=pltpu.VMEM),
        out_shape=jax.ShapeDtypeStruct((dout.shape[0] + experts, dout.shape[1]), jnp.bfloat16),
        cost_estimate=pl.CostEstimate(flops=0, bytes_accessed=0, transcendentals=0),
        name="token_rows",
    )(lengths, expert_ids, dout)


def store_grad(grad, cols, rows, mine, outs):
    low = jnp.bfloat16
    if not rows:
        outs[0][:, cols] = grad.astype(low)
        return
    for c in range(grad.shape[0] // (2 * rows)):
        first = grad[2 * c * rows : (2 * c + 1) * rows]
        second = grad[(2 * c + 1) * rows : (2 * c + 2) * rows]
        outs[0][pl.ds(c * rows, rows), cols] = jnp.where(mine, first, second).astype(low)
        outs[1][pl.ds(c * rows, rows), cols] = jnp.where(mine, second, first).astype(low)


def shared_kernel(rows, experts, core_ref, h2, cb, w_in, w_down, w_router, shared_out, grad_h2, probs, *rest):
    f32, bf16 = jnp.float32, jnp.bfloat16
    *grads, gu, hs, dgu = rest
    tokens, width = h2.shape
    hidden = w_down.shape[0]
    mine = core_ref[0] == 0
    own = pl.ds(0, tokens)

    logits = jnp.dot(h2[...], w_router[...], preferred_element_type=f32)
    column = lax.broadcasted_iota(jnp.int32, logits.shape, 1)
    logits = jnp.where(column < experts - 1, logits, MASK_VALUE)
    ex = jnp.exp(logits - jnp.max(logits, axis=1, keepdims=True))
    probs[...] = ex / jnp.sum(ex, axis=1, keepdims=True)
    for start in range(0, 2 * hidden, 256):
        t = pl.ds(start, 256)
        gu[:, t] = jnp.dot(h2[...], w_in[:, t], preferred_element_type=f32)
    for start in range(0, hidden, 128):
        ta, tb = pl.ds(start, 128), pl.ds(hidden + start, 128)
        a, b = gu[:, ta], gu[:, tb]
        sig = jax.nn.sigmoid(a)
        silu = a * sig
        hs[:, ta] = (silu * b).astype(bf16)
        gu[:, ta] = b * (sig * (1.0 + a * (1.0 - sig)))
        gu[:, tb] = silu
    for start in range(0, hidden, 256):
        n = min(256, hidden - start)
        dhs = lax.dot_general(cb[own, :], w_down[pl.ds(start, n), :], NT, preferred_element_type=f32)
        for t in (pl.ds(start, n), pl.ds(hidden + start, n)):
            dgu[:, t] = (dhs * gu[:, t]).astype(bf16)
    for start in range(0, width, 256):
        t = pl.ds(start, 256)
        shared_out[:, t] = jnp.dot(hs[...], w_down[:, t], preferred_element_type=f32)
        grad_h2[:, t] = lax.dot_general(dgu[...], w_in[t, :], NT, preferred_element_type=f32)
    for start in range(0, 2 * hidden, 256):
        t = pl.ds(start, 256)
        grad = lax.dot_general(h2[...], dgu[:, t], TN, preferred_element_type=f32)
        store_grad(grad, t, rows, mine, grads)
    for start in range(0, hidden, 256):
        n = min(256, hidden - start)
        grad = lax.dot_general(cb[own, :], hs[:, pl.ds(start, n)], TN, preferred_element_type=f32)
        store_grad(grad, pl.ds(2 * hidden + start, n), rows, mine, grads)


def shared_expert(core, h2, cb, w_in, w_down, w_router, rows, experts):
    tokens, width = h2.shape
    hidden = w_down.shape[0]
    f32, bf16 = jnp.float32, jnp.bfloat16
    sd = jax.ShapeDtypeStruct
    vmem = pl.BlockSpec(memory_space=pltpu.VMEM)
    grads = [sd((width // 2, 3 * hidden), bf16)] * 2 if rows else [sd((width, 3 * hidden), bf16)]
    outs = [sd((tokens, width), f32), sd((tokens, width), f32), sd((tokens, w_router.shape[1]), f32)] + grads
    return pl.pallas_call(
        lambda *r: shared_kernel(rows, experts, *r),
        in_specs=[pl.BlockSpec(memory_space=pltpu.SMEM)] + [vmem] * 5,
        out_specs=[vmem] * len(outs),
        out_shape=outs,
        scratch_shapes=[pltpu.VMEM((tokens, 2 * hidden), f32), pltpu.VMEM((tokens, hidden), bf16), pltpu.VMEM((tokens, 2 * hidden), bf16)],
        compiler_params=pltpu.CompilerParams(vmem_limit_bytes=48 * 2**20),
        cost_estimate=pl.CostEstimate(flops=0, bytes_accessed=0, transcendentals=0),
        name="shared_expert",
    )(core, h2, cb, w_in, w_down, w_router)


def middle_kernel(experts, length_ref, home_a, home_b, home_c, grad_shared, probs, h2, w_router, x_mid, dout, gain, grad_mid, da, small):
    f32, bf16 = jnp.float32, jnp.bfloat16
    tokens = x_mid.shape[0]
    own, table = pl.ds(0, tokens), pl.ds(tokens, 2 * experts)
    total = lambda r, c: home_a[r, c].astype(f32) + home_b[r, c].astype(f32) + home_c[r, c].astype(f32)
    dots = total(table, own)
    dots = dots[:experts] + dots[experts:]
    grad_probs = jnp.concatenate([dots, jnp.zeros((128 - experts, tokens), f32)], axis=0).T
    p = probs[...]
    low = (p * (grad_probs - jnp.sum(grad_probs * p, axis=1, keepdims=True))).astype(bf16)
    incoming = total(own, slice(None)) + grad_shared[...]
    incoming += lax.dot_general(low, w_router[...], NT, preferred_element_type=f32)
    mid = x_mid[...]
    inverse = lax.rsqrt(jnp.mean(mid * mid, axis=-1, keepdims=True) + NORM_EPS)
    scaled = mid * inverse
    column = lax.broadcasted_iota(jnp.int32, (tokens, 128), 1)
    small[...] = lax.dot_general(h2[...], low, TN, preferred_element_type=f32) + lax.dot_general(
        incoming * scaled, jnp.where(column == experts, 1.0, 0.0), TN,
        precision=lax.Precision.HIGHEST, preferred_element_type=f32,
    )
    inner = incoming * gain[...]
    back = inverse * (inner - scaled * jnp.mean(inner * scaled, axis=-1, keepdims=True))
    grad = dout[...].astype(f32) + back
    grad_mid[...] = grad
    live = lax.broadcasted_iota(jnp.int32, (tokens, 1), 0) < length_ref[0]
    da[...] = jnp.where(live, grad, 0.0).astype(bf16)


def middle_back(lengths, home, grad_shared, probs, h2, w_router, x_mid, dout, gain, experts):
    tokens, width = x_mid.shape
    f32 = jnp.float32
    sd = jax.ShapeDtypeStruct
    vmem = pl.BlockSpec(memory_space=pltpu.VMEM)
    return pl.pallas_call(
        lambda *r: middle_kernel(experts, *r),
        in_specs=[pl.BlockSpec(memory_space=pltpu.SMEM)] + [vmem] * 10,
        out_specs=[vmem] * 3,
        out_shape=[sd((tokens, width), f32), sd((tokens, width), jnp.bfloat16), sd((width, 128), f32)],
        compiler_params=pltpu.CompilerParams(vmem_limit_bytes=48 * 2**20),
        cost_estimate=pl.CostEstimate(flops=0, bytes_accessed=0, transcendentals=0),
        name="middle_back",
    )(lengths, *home, grad_shared, probs, h2, w_router, x_mid, dout, gain)


def weight_grad_kernel(parts, bit, index_ref, lhs, rhs, keep, away):
    f32, bf16 = jnp.float32, jnp.bfloat16
    grad = lax.dot_general(lhs[0], rhs[0], TN, preferred_element_type=f32)
    mine = ((index_ref[0] >> bit) & 1) == 0
    rows = grad.shape[0] // parts
    at = 0
    for c in range(parts):
        if (c >> bit) & 1:
            continue
        other = c | (1 << bit)
        first = grad[c * rows : (c + 1) * rows]
        second = grad[other * rows : (other + 1) * rows]
        keep[pl.ds(at, rows), :] = jnp.where(mine, first, second).astype(bf16)
        away[pl.ds(at, rows), :] = jnp.where(mine, second, first).astype(bf16)
        at += rows


def weight_grad(index, lhs, rhs, expert, parts, bit):
    _, rows, m = lhs.shape
    n = rhs.shape[2]
    tile = 256
    return pl.pallas_call(
        lambda *r: weight_grad_kernel(parts, bit, *r),
        grid=(n // tile,),
        in_specs=[
            pl.BlockSpec(memory_space=pltpu.SMEM),
            pl.BlockSpec((1, rows, m), lambda i: (expert, 0, 0)),
            pl.BlockSpec((1, rows, tile), lambda i: (expert, 0, i)),
        ],
        out_specs=[pl.BlockSpec((m // 2, tile), lambda i: (0, i))] * 2,
        out_shape=[jax.ShapeDtypeStruct((m // 2, n), jnp.bfloat16)] * 2,
        compiler_params=pltpu.CompilerParams(vmem_limit_bytes=48 * 2**20),
        cost_estimate=pl.CostEstimate(flops=0, bytes_accessed=0, transcendentals=0),
        name="weight_grad",
    )(index, lhs, rhs)


def rope_tables(seq_slots):
    half_dim = HEAD_DIM // 2
    inv_freq = 1.0 / 10000.0 ** (jnp.arange(half_dim, dtype=jnp.float32) * 2.0 / HEAD_DIM)
    angles = jnp.arange(seq_slots, dtype=jnp.float32)[:, None] * inv_freq[None, :]
    cosine, sine = jnp.cos(angles), jnp.sin(angles)
    return jnp.concatenate([cosine, cosine], axis=1), jnp.concatenate([-sine, sine], axis=1)


def swap_cores(values_in):
    owners = lax.axis_size("expert")
    return lax.ppermute(values_in, "expert", [(i, i ^ 1) for i in range(owners)])


def next_chip(values_in):
    owners = lax.axis_size("expert")
    return lax.ppermute(values_in, "expert", [(i, (i + 2) % owners) for i in range(owners)])


def axis_bits(name):
    return [(name, bit) for bit in range(lax.axis_size(name).bit_length() - 1)]


def row_bits():
    return axis_bits("dp")[::-1] + axis_bits("expert")[::-1]


def sum_terms(parts):
    summed = parts[0].astype(jnp.float32)
    for term in parts[1:]:
        summed = summed + term.astype(jnp.float32)
    return summed


def after(values_in, *earlier):
    return lax.optimization_barrier((values_in, earlier))[0]


def picked(term, choices):
    for dim, index in choices:
        term = lax.dynamic_index_in_dim(term, index, dim, keepdims=False)
    return term


class Scatter:
    def __init__(self, terms, open_bits, order):
        self.terms, self.choices = list(terms), [[] for _ in terms]
        self.open_bits, self.order = list(open_bits), list(order)

    def advance(self, *earlier):
        name, bit = self.order.pop(0)
        dim = self.open_bits.index((name, bit))
        mine = (lax.axis_index(name) >> bit) & 1
        terms = after(self.terms, *earlier) if earlier else self.terms
        away = sum_terms(
            [picked(term, made + [(dim, 1 - mine)]) for term, made in zip(terms, self.choices)]
        ).astype(terms[0].dtype)
        came = lax.ppermute(
            away, name, [(i, i ^ (1 << bit)) for i in range(lax.axis_size(name))]
        )
        self.choices = [made + [(dim, mine)] for made in self.choices] + [[]]
        self.terms.append(came)
        self.open_bits.pop(dim)
        return away

    def finish(self):
        while self.order:
            self.advance()
        return sum_terms([picked(term, made) for term, made in zip(self.terms, self.choices)])


def split_rows(part, bits):
    rows = part.shape[0] >> len(bits)
    return part.reshape((2,) * len(bits) + (rows, part.shape[1]))


def scatter_orders():
    core, *line = axis_bits("expert")
    plane = axis_bits("dp")
    return ([core] + plane + line, [core] + plane[::-1] + line, [core] + plane + line)


def per_device(
    layer_input,
    lengths,
    expert_ids,
    norm1,
    w_qkv,
    w_out,
    norm2,
    w_router,
    w_shared_in,
    w_shared_down,
    w_expert_in,
    w_expert_down,
    dout,
):
    seq_slots, width = layer_input.shape
    top_k = expert_ids.shape[1]
    experts = w_router.shape[1]
    local_experts = w_expert_in.shape[0]
    hidden_units = w_shared_down.shape[0]
    capacity = (seq_slots * top_k // (experts - 1) // 8 + 1) * 8
    live_col = (jnp.arange(seq_slots, dtype=jnp.int32) < lengths[0]).astype(jnp.float32)[:, None]
    cosine, sine = rope_tables(seq_slots)

    bits = row_bits()
    rows = width >> len(bits)
    rows = rows if rows % 8 == 0 else 0
    core = (lax.axis_index("expert") & 1).astype(jnp.int32)[None]
    orders = scatter_orders()
    chips = experts // local_experts // 2
    first_expert = (lax.axis_index("expert") * local_experts).astype(jnp.int32)[None]
    router_t = w_router.T

    def start_scatter(grads, order):
        if rows:
            terms = [split_rows(grads[0], bits[:-1]), split_rows(swap_cores(grads[1]), bits[:-1])]
            return Scatter(terms, bits[:-1], order[1:])
        return Scatter([split_rows(grads[0], bits)], bits, order)

    def run_step(step, h2_pair, grad_pair, kept, *earlier):
        sums, kept = expert_step(
            first_expert, after(h2_pair[0], *earlier), h2_pair[1], grad_pair[0], grad_pair[1],
            router_t, w_expert_in, w_expert_down, step, chips, capacity, kept,
        )
        parts.append(sums)
        return kept, sums[0]

    parts = []
    router_wide = jnp.pad(w_router, ((0, 0), (0, 128 - experts)))
    grad_table = token_rows(lengths, expert_ids, dout, experts)
    grad_here = (grad_table, swap_cores(grad_table))
    grad_next = next_chip(grad_table)
    counts_here = jnp.sum((grad_table[seq_slots:, :seq_slots] >= 0).astype(jnp.int32), axis=1)
    places = jnp.minimum(jnp.arange(width >> len(bits), dtype=jnp.int32), 30)
    digits = ((counts_here[None, :] >> places[:, None]) & 1).astype(jnp.float32)
    small_columns = -(-(2 * experts + 2) // 128) * 128
    digits = jnp.pad(
        jnp.tile(digits, (1 << len(bits), 1)),
        ((0, 0), (experts + 2, small_columns - 2 * experts - 2)),
    )
    h1_low, queries, keys_in, values_in, attended_low, log_norm, x_mid, h2_low = attention_forward(
        lengths, after(layer_input, grad_table), norm1[None, :], w_qkv, cosine, sine, w_out,
        norm2[None, :],
    )
    h2_here = (h2_low, swap_cores(h2_low))
    h2_next = next_chip(h2_low)
    grad_next = after(grad_next, h2_low)
    grad_other = swap_cores(grad_next)
    grad_ahead = next_chip(grad_next)
    kept, done = run_step(0, h2_here, grad_here, None, grad_next)
    shared_out, grad_shared, router_probs, *shared_grads = shared_expert(
        core, after(h2_low, done), grad_table, w_shared_in, w_shared_down, router_wide, rows, experts
    )
    fence = shared_out
    shared_away = []
    swapped = []
    shared_scatter = None
    travelling = None
    for step in range(1, chips):
        h2_next, grad_next = after(h2_next, fence), after(grad_next, fence)
        pair_h2 = (h2_next, swap_cores(h2_next))
        pair_grad = (grad_next, grad_other)
        if shared_scatter is None:
            ready = (fence, grad_ahead, pair_h2[1], grad_other)
            shared_scatter = start_scatter(after(shared_grads, *ready), orders[0])
            swapped.append(swap_cores(after(parts[0][3], *ready)))
        earlier = [] if travelling is None else [travelling]
        earlier += shared_away
        if step + 1 < chips:
            h2_next = next_chip(h2_next)
            grad_next = after(grad_ahead, fence)
            grad_other = swap_cores(grad_next)
            if step + 2 < chips:
                grad_ahead = next_chip(grad_next)
        kept, fence = run_step(step, pair_h2, pair_grad, kept, *earlier)
        mine, theirs = parts[step][:2]
        if step + 1 < chips:
            theirs = after(theirs, h2_next, grad_ahead)
        theirs = after(theirs, *swapped)
        if step == 2:
            first_routed = parts[1][2].astype(jnp.float32) + swapped[1].astype(jnp.float32)
            first_routed = first_routed.astype(jnp.bfloat16)
            theirs = after(theirs, first_routed)
        swapped.append(swap_cores(after(parts[step][3], theirs)))
        if shared_away:
            theirs = after(theirs, shared_scatter.terms[-1])
        if shared_scatter.order[0][0] == "dp":
            shared_away = [shared_scatter.advance(fence)]
            theirs = after(theirs, *shared_away)
        if travelling is None:
            total = mine.astype(jnp.float32) + swap_cores(theirs).astype(jnp.float32)
        else:
            came = next_chip(travelling)
            total = (
                mine.astype(jnp.float32)
                + swap_cores(after(theirs, came)).astype(jnp.float32)
                + came.astype(jnp.float32)
            )
        travelling = total.astype(mine.dtype)

    home_hop = next_chip(travelling)
    rows_held, grad_result, expert_hidden, grad_expert_gu = kept

    plane = axis_bits("dp")
    plane_index = lax.axis_index("dp").astype(jnp.int32)[None]

    def expert_grads(lhs, rhs, expert):
        order = plane if expert % 2 == 0 else plane[::-1]
        return order, weight_grad(
            plane_index, lhs, rhs, expert, 1 << len(plane), order[0][1]
        )

    def plane_scatter(order, grads, *earlier):
        name, bit = order[0]
        keep, away = after(grads, *earlier) if earlier else grads
        came = lax.ppermute(
            away, name, [(i, i ^ (1 << bit)) for i in range(lax.axis_size(name))]
        )
        open_bits = [place for place in plane[::-1] if place != order[0]]
        terms = [split_rows(piece, open_bits) for piece in (keep, came)]
        return Scatter(terms, open_bits, order[1:])

    fence = [travelling, shared_scatter.terms[-1]]
    down_parts, in_parts = [], []
    for i in range(local_experts):
        down_parts.append(expert_grads(after(expert_hidden, *fence), grad_result, i))
        fence = down_parts[-1][1]
    down_scatters = [plane_scatter(*part) for part in down_parts]
    for i in range(local_experts):
        in_parts.append(expert_grads(after(rows_held, *fence), grad_expert_gu, i))
        fence = in_parts[-1][1]

    mine, theirs = parts[0][:2]
    own_home = (mine, swap_cores(after(theirs, travelling)))
    out_order = list(range(1, chips)) + [0]

    def add_routed(index, came, *earlier):
        mine, theirs = after((parts[out_order[index]][2], swapped[out_order[index]]), *earlier)
        total = mine.astype(jnp.float32) + theirs.astype(jnp.float32)
        return total if came is None else total + came.astype(jnp.float32)

    routed = first_routed if chips > 2 else add_routed(0, None, travelling).astype(jnp.bfloat16)
    landed = list(fence) + [home_hop, own_home[1], swapped[-1], routed]
    landed += [scatter.terms[-1] for scatter in down_scatters]
    in_scatters = [plane_scatter(*part, *landed) for part in in_parts]
    out_hop = next_chip(after(routed, *landed))
    fence = landed
    for scatter in down_scatters:
        fence = [scatter.advance(*fence)]
    home = after((*own_home, home_hop), *fence)
    grad_mid, grad_attn_branch, small = middle_back(
        lengths, home, grad_shared, router_probs, h2_low, router_wide, x_mid, dout, norm2[None, :],
        experts,
    )
    small = digits + jnp.pad(small, ((0, 0), (0, small_columns - 128)))

    pairs = width // (2 * HEAD_DIM)
    half = (pairs - 1) // 2
    cuts = (0, half, 2 * half, pairs)
    running = None
    columns = []
    fence = [grad_attn_branch]
    for index, (first, last) in enumerate(zip(cuts[:-1], cuts[1:])):
        tail = None
        if last == pairs:
            tail = (experts, (layer_input, norm1[None, :], grad_mid, small))
        *grads, running = attention_backward(
            lengths, core, after(grad_attn_branch, *fence), w_out, queries, keys_in, values_in,
            log_norm, cosine, sine, h1_low, attended_low, w_qkv, running, first, last - first, rows,
            tail,
        )
        fence = [running]
        columns.append(grads)
        if index == 0:
            routed = add_routed(1, out_hop, running).astype(jnp.bfloat16)
            out_hop = next_chip(routed)
            fence.append(routed)
    grad_input = running
    landed = [running, out_hop]
    landed += [scatter.terms[-1] for scatter in in_scatters + down_scatters]
    scatters = []
    for grads, order in zip(columns, orders):
        scatters.append(start_scatter(after(grads, *landed), order))
    fence = landed
    hops = 2
    first_cols, second_cols, third_cols = scatters
    plan = [first_cols, second_cols, None, third_cols, shared_scatter]
    plan += [first_cols, second_cols, third_cols, shared_scatter, None]
    plan += [first_cols, second_cols, third_cols] + in_scatters
    plan += [first_cols, second_cols, third_cols]
    for scatter in plan:
        if scatter is not None:
            if scatter.order:
                fence = [scatter.advance(*fence)]
        elif hops < chips:
            routed = add_routed(hops, out_hop, *fence)
            hops += 1
            if hops < chips:
                out_hop = next_chip(routed.astype(jnp.bfloat16))
            fence = [routed]
    for hops in range(hops, chips):
        routed = add_routed(hops, out_hop, *fence)
        out_hop = next_chip(routed.astype(jnp.bfloat16))
    for scatter in down_scatters + in_scatters:
        scatter.terms = after(scatter.terms, *fence)
    result = (x_mid + live_col * (shared_out + routed)).astype(jnp.bfloat16)
    shared_sum = shared_scatter.finish()
    expert_in_sum = jnp.stack([scatter.finish() for scatter in in_scatters])
    expert_down_sum = jnp.stack([scatter.finish() for scatter in down_scatters])
    wide = 2 * HEAD_DIM
    blocks = []
    for scatter, first, last in zip(scatters, cuts[:-1], cuts[1:]):
        piece = scatter.finish()
        step = piece.shape[1] // (last - first)
        blocks += [piece[:, at * step : (at + 1) * step] for at in range(last - first)]
    small_sum = blocks[-1][:, 4 * wide :]
    qkv_sum, out_sum = (
        jnp.concatenate(
            [block[:, k * wide : (k + 1) * wide] for k in kinds for block in blocks], axis=1
        )
        for kinds in ((0, 1, 2), (3,))
    )
    counts = jnp.sum(
        small_sum[:, experts + 2 : 2 * experts + 2] * (1 << places).astype(jnp.float32)[:, None],
        axis=0,
    )
    return (
        result,
        grad_input,
        small_sum[:, experts + 1],
        qkv_sum,
        out_sum,
        small_sum[:, experts],
        small_sum[:, :experts],
        shared_sum[:, : 2 * hidden_units],
        shared_sum[:, 2 * hidden_units :].T,
        expert_in_sum,
        expert_down_sum,
        counts.astype(jnp.int32),
    )


def solution(mesh):
    return jax.shard_map(
        per_device,
        mesh=mesh,
        in_specs=(
            P(("dp", "expert"), None),
            P(("dp", "expert")),
            P(("dp", "expert"), None),
            P(),
            P(),
            P(),
            P(),
            P(),
            P(),
            P(),
            P("expert", None, None),
            P("expert", None, None),
            P(("dp", "expert"), None),
        ),
        out_specs=(
            P(("dp", "expert"), None),
            P(("dp", "expert"), None),
            P(("dp", "expert")),
            P(("dp", "expert"), None),
            P(("dp", "expert"), None),
            P(("dp", "expert")),
            P(("dp", "expert"), None),
            P(("dp", "expert"), None),
            P(None, ("dp", "expert")),
            P("expert", "dp", None),
            P("expert", "dp", None),
            P(),
        ),
        check_vma=False,
    )
```

```python
import jax
import jax.numpy as jnp
from jax import lax
from jax.experimental import pallas as pl
from jax.experimental.pallas import tpu as pltpu
from jax.sharding import PartitionSpec as P

HEAD_DIM = 128
NORM_EPS = 1e-06
MASK_VALUE = -1e30
NT = (((1,), (1,)), ((), ()))
TN = (((0,), (0,)), ((), ()))

def turn(values_in, cosine, signed_sine):
    return values_in * cosine + pltpu.roll(values_in, HEAD_DIM // 2, 1) * signed_sine

def block_scores(q, k, start, seq_length):
    s = lax.dot_general(q, k, NT, preferred_element_type=jnp.float32) * HEAD_DIM ** (-0.5)
    query_pos = start + lax.broadcasted_iota(jnp.int32, s.shape, 0)
    key_pos = lax.broadcasted_iota(jnp.int32, s.shape, 1)
    return jnp.where((key_pos <= query_pos) & (key_pos < seq_length), s, MASK_VALUE)

def attention_kernel(length_ref, x, norm1, wq, wk, wv, cosine, sine, w_out, norm2, h1, q_o, k_o, v_o, att, lse, x_mid, h2):
    f32, bf16 = jnp.float32, jnp.bfloat16
    p = pl.program_id(0)
    tokens = x.shape[0]
    seq_length = length_ref[0]
    span = min(256, tokens)

    @pl.when(p == 0)
    def _():
        xf = x[...].astype(f32)
        inverse = lax.rsqrt(jnp.mean(xf * xf, axis=-1, keepdims=True) + NORM_EPS)
        h1[...] = (xf * inverse * norm1[...]).astype(bf16)
        lse[...] = jnp.zeros_like(lse)

    for w, o in ((wq, q_o), (wk, k_o), (wv, v_o)):
        full = jnp.dot(h1[...], w[...], preferred_element_type=f32)
        for j in (0, 1):
            part = full[:, j * HEAD_DIM:(j + 1) * HEAD_DIM]
            if w is not wv:
                part = turn(part, cosine[...], sine[...])
            o[:, pl.ds(j * HEAD_DIM, HEAD_DIM)] = part.astype(bf16)
    lane = lax.broadcasted_iota(jnp.int32, (span, lse.shape[1]), 1)
    for j in (0, 1):
        cols = pl.ds(j * HEAD_DIM, HEAD_DIM)
        for start in range(0, tokens, span):
            rows = pl.ds(start, span)
            seen = pl.ds(0, start + span)
            s = block_scores(q_o[rows, cols], k_o[seen, cols], start, seq_length)
            high = jnp.max(s, axis=-1, keepdims=True)
            ex = jnp.exp(s - high)
            total = jnp.sum(ex, axis=-1, keepdims=True)
            low = (ex / total).astype(bf16)
            out = jnp.dot(low, v_o[seen, cols], preferred_element_type=f32)
            att[rows, pl.ds(pl.multiple_of(p * 2 * HEAD_DIM + j * HEAD_DIM, HEAD_DIM), HEAD_DIM)] = out.astype(bf16)
            lse[rows, :] = jnp.where(lane == 2 * p + j, high + jnp.log(total), lse[rows, :])

    @pl.when(p == pl.num_programs(0) - 1)
    def _():
        branch = jnp.dot(att[...], w_out[...], preferred_element_type=f32)
        live = lax.broadcasted_iota(jnp.int32, (tokens, 1), 0) < seq_length
        mid = x[...].astype(f32) + jnp.where(live, branch, 0.0)
        x_mid[...] = mid
        inverse = lax.rsqrt(jnp.mean(mid * mid, axis=-1, keepdims=True) + NORM_EPS)
        h2[...] = (mid * inverse * norm2[...]).astype(bf16)

def whole(a):
    return pl.BlockSpec(a.shape, lambda p: (0,) * len(a.shape), pipeline_mode=pl.Buffered(1))

def attention_forward(lengths, x, norm1, w_qkv, cosine, sine, w_out, norm2):
    tokens, width = x.shape
    pairs = width // (2 * HEAD_DIM)
    f32, bf16 = jnp.float32, jnp.bfloat16
    wide = 2 * HEAD_DIM
    col = lambda k: pl.BlockSpec((width, wide), lambda p, k=k: (0, k * pairs + p))
    head = pl.BlockSpec((tokens, wide), lambda p: (0, p))
    full = pl.BlockSpec((tokens, width), lambda p: (0, 0))
    sd = jax.ShapeDtypeStruct
    return pl.pallas_call(
        attention_kernel, grid=(pairs,),
        in_specs=[pl.BlockSpec(memory_space=pltpu.SMEM), whole(x), whole(norm1), col(0), col(1), col(2), whole(cosine), whole(sine), whole(w_out), whole(norm2)],
        out_specs=[full, head, head, head, full, pl.BlockSpec((tokens, 128), lambda p: (0, 0)), full, full],
        out_shape=[pltpu.HBM((tokens, width), bf16)] * 5 + [pltpu.HBM((tokens, 128), f32), pltpu.HBM((tokens, width), f32), pltpu.HBM((tokens, width), bf16)],
        compiler_params=pltpu.CompilerParams(vmem_limit_bytes=48 * 2**20),
        cost_estimate=pl.CostEstimate(flops=0, bytes_accessed=0, transcendentals=0),
        name="attention_forward",
    )(lengths, x, norm1, w_qkv, w_qkv, w_qkv, cosine, sine, w_out, norm2)

def attention_back_kernel(rows, extra, carried, length_ref, core_ref, da, w_out, q, k, v, lse, cosine, sine, h1, att, wq, wk, wv, *rest):
    f32, bf16 = jnp.float32, jnp.bfloat16
    dh1_in = None
    if carried:
        dh1_in, *rest = rest
    if extra:
        x, gain, grad_mid, small, *rest = rest
    *grads, dh1, dk_s, dv_s, dproj = rest
    p = pl.program_id(0)
    pair = length_ref[1] + p
    tokens, width = da.shape
    seq_length = length_ref[0]
    span = min(256, tokens)
    scale = HEAD_DIM ** (-0.5)
    mine = core_ref[0] == 0
    wide = 2 * HEAD_DIM
    do_full = lax.dot_general(da[...], w_out[...], NT, preferred_element_type=f32).astype(bf16)
    lane = lax.broadcasted_iota(jnp.int32, (span, lse.shape[1]), 1)
    back_sine = -sine[...]
    for j in (0, 1):
        cols = pl.ds(j * HEAD_DIM, HEAD_DIM)
        do_head = do_full[:, j * HEAD_DIM : (j + 1) * HEAD_DIM]
        for start in range(tokens - span, -1, -span):
            r = pl.ds(start, span)
            seen = pl.ds(0, start + span)
            s = block_scores(q[r, cols], k[seen, cols], start, seq_length)
            norm = jnp.sum(jnp.where(lane == 2 * pair + j, lse[r, :], 0.0), axis=1, keepdims=True)
            probs = jnp.exp(s - norm)
            do = do_head[start : start + span]
            dp = lax.dot_general(do, v[seen, cols], NT, preferred_element_type=f32)
            row = jnp.sum(dp * probs, axis=1, keepdims=True)
            ds = (probs * (dp - row)).astype(bf16)
            dq = jnp.dot(ds, k[seen, cols], preferred_element_type=f32) * scale
            dproj[r, pl.ds(j * HEAD_DIM, HEAD_DIM)] = turn(
                dq, cosine[r, :], back_sine[start : start + span]
            ).astype(bf16)
            dk = lax.dot_general(ds, q[r, cols], TN, preferred_element_type=f32) * scale
            dv = lax.dot_general(probs.astype(bf16), do, TN, preferred_element_type=f32)
            if start == tokens - span:
                dk_s[seen, :] = dk
                dv_s[seen, :] = dv
            else:
                dk_s[seen, :] += dk
                dv_s[seen, :] += dv
        dproj[:, pl.ds(wide + j * HEAD_DIM, HEAD_DIM)] = turn(dk_s[...], cosine[...], back_sine).astype(bf16)
        dproj[:, pl.ds(2 * wide + j * HEAD_DIM, HEAD_DIM)] = dv_s[...].astype(bf16)
    total = jnp.where(p == 0, dh1_in[...] if carried else 0.0, dh1[...])
    for i, w in enumerate((wq, wk, wv)):
        part = dproj[:, pl.ds(i * wide, wide)]
        grad = lax.dot_general(h1[...], part, TN, preferred_element_type=f32)
        store_grad(grad, pl.ds(i * wide, wide), rows, mine, grads)
        total += lax.dot_general(part, w[...], NT, preferred_element_type=f32)
    part = da[:, pl.ds(pl.multiple_of(pair * wide, wide), wide)]
    grad = lax.dot_general(att[...], part, TN, preferred_element_type=f32)
    store_grad(grad, pl.ds(3 * wide, wide), rows, mine, grads)
    dh1[...] = total
    if not extra:
        return

    @pl.when(p < pl.num_programs(0) - 1)
    def _():
        store_grad(jnp.zeros(small.shape, f32), pl.ds(4 * wide, small.shape[1]), rows, mine, grads)

    @pl.when(p == pl.num_programs(0) - 1)
    def _():
        full = x[...].astype(f32)
        inverse = lax.rsqrt(jnp.mean(full * full, axis=-1, keepdims=True) + NORM_EPS)
        scaled = full * inverse
        inner = total * gain[...]
        dh1[...] = grad_mid[...] + inverse * (
            inner - scaled * jnp.mean(inner * scaled, axis=-1, keepdims=True)
        )
        column = lax.broadcasted_iota(jnp.int32, (tokens, small.shape[1]), 1)
        grad = small[...] + lax.dot_general(
            total * scaled, jnp.where(column == extra + 1, 1.0, 0.0), TN,
            precision=lax.Precision.HIGHEST, preferred_element_type=f32,
        )
        store_grad(grad, pl.ds(4 * wide, small.shape[1]), rows, mine, grads)


def attention_backward(lengths, core, da, w_out, q, k, v, lse, cosine, sine, h1, att, w_qkv, dh1_in, first, count, rows, tail):
    tokens, width = da.shape
    pairs = width // (2 * HEAD_DIM)
    wide = 2 * HEAD_DIM
    f32, bf16 = jnp.float32, jnp.bfloat16
    col = lambda k: pl.BlockSpec((width, wide), lambda p, k=k: (0, k * pairs + first + p))
    head = pl.BlockSpec((tokens, wide), lambda p: (0, first + p))
    sd = jax.ShapeDtypeStruct
    smem = pl.BlockSpec(memory_space=pltpu.SMEM)
    n = width // 2 if rows else width
    extra, tail_args = tail if tail else (0, ())
    columns = 4 * wide + (tail_args[-1].shape[1] if extra else 0)
    grads = [sd((n, count * columns), bf16)] * (2 if rows else 1)
    carried = dh1_in is not None
    tail_args = ((dh1_in,) if carried else ()) + tuple(tail_args)
    whole_args = (da, lse, cosine, sine, h1, att) + tail_args
    spec = {id(a): whole(a) for a in whole_args}
    *held, h1_held, att_held = (
        pltpu.with_memory_space_constraint(a, pltpu.HBM) for a in (q, k, v, h1, att)
    )
    return pl.pallas_call(
        lambda *r: attention_back_kernel(rows, extra, carried, *r),
        grid=(count,),
        in_specs=[smem, smem, spec[id(da)], pl.BlockSpec((wide, width), lambda p: (first + p, 0)), head, head, head]
        + [spec[id(a)] for a in (lse, cosine, sine, h1, att)]
        + [col(0), col(1), col(2)]
        + [spec[id(a)] for a in tail_args],
        out_specs=[pl.BlockSpec((n, columns), lambda p: (0, p))] * len(grads)
        + [pl.BlockSpec((tokens, width), lambda p: (0, 0))],
        out_shape=grads + [sd((tokens, width), f32)],
        scratch_shapes=[pltpu.VMEM((tokens, HEAD_DIM), f32), pltpu.VMEM((tokens, HEAD_DIM), f32), pltpu.VMEM((tokens, 3 * wide), bf16)],
        compiler_params=pltpu.CompilerParams(vmem_limit_bytes=48 * 2**20),
        cost_estimate=pl.CostEstimate(flops=0, bytes_accessed=0, transcendentals=0),
        name="attention_backward",
    )(
        jnp.concatenate([lengths, jnp.full((1,), first, jnp.int32)]), core, da, w_out, *held,
        lse, cosine, sine, h1_held, att_held, w_qkv, w_qkv, w_qkv, *tail_args,
    )


def expert_kernel(cap, tokens, hidden, last_slot, *refs):
    (first_ref, h2a, h2b, cba, cbb, wr, w_in, w_down) = refs[:8]
    (dra, drb, outa, outb, rows_o, dy_o, act_o, dgu_o, gu, cbrow, oh, gy, drs, probs, dots) = refs[-15:]
    f32, bf16 = jnp.float32, jnp.bfloat16
    e = pl.program_id(0)
    experts = wr.shape[0]
    width = wr.shape[1]
    mine = first_ref[0] + e
    table_rows = probs.shape[1]

    @pl.when(e == 0)
    def _():
        for src, h2 in ((0, h2a), (1, h2b)):
            logits = lax.dot_general(wr[...], h2[...], (((1,), (1,)), ((), ())), preferred_element_type=f32)
            row = lax.broadcasted_iota(jnp.int32, logits.shape, 0)
            logits = jnp.where(row < experts - 1, logits, MASK_VALUE)
            ex = jnp.exp(logits - jnp.max(logits, axis=0, keepdims=True))
            probs[src] = ex / jnp.sum(ex, axis=0, keepdims=True)
            dots[src] = jnp.zeros_like(probs[src])

    gates = []
    masks = []
    for src, h2, cb in ((0, h2a, cba), (1, h2b, cbb)):
        row_id = lax.broadcasted_iota(jnp.int32, (table_rows, tokens), 0)
        table = cb[pl.ds(tokens, table_rows), pl.ds(0, tokens)].astype(f32)
        rank = jnp.sum(jnp.where(row_id == mine, table, 0.0), axis=0, keepdims=True)
        prob = jnp.sum(jnp.where(row_id == mine, probs[src], 0.0), axis=0, keepdims=True)
        hit = lax.broadcasted_iota(jnp.int32, (cap, tokens), 0).astype(f32) == rank
        masks.append(hit)
        gates.append(jnp.sum(jnp.where(hit, prob, 0.0), axis=1, keepdims=True))
        onehot = jnp.where(hit, 1.0, 0.0).astype(bf16)
        oh[src, pl.ds(e * cap, cap), :] = onehot
        half = pl.ds(src * cap, cap)
        @pl.loop(0, width // 256, unroll=True)
        def _(i):
            t = pl.ds(pl.multiple_of(i * 256, 256), 256)
            rows_o[0, half, t] = jnp.dot(onehot, h2[:, t], preferred_element_type=f32).astype(bf16)
            cbrow[half, t] = jnp.dot(onehot, cb[pl.ds(0, tokens), t], preferred_element_type=f32).astype(bf16)
    gate = jnp.concatenate(gates, axis=0)

    @pl.loop(0, 2 * hidden // 256, unroll=True)
    def _(i):
        t = pl.ds(pl.multiple_of(i * 256, 256), 256)
        gu[:, t] = jnp.dot(rows_o[0], w_in[0, :, t], preferred_element_type=f32)

    @pl.loop(0, hidden // 128, unroll=True)
    def _(i):
        ta = pl.ds(pl.multiple_of(i * 128, 128), 128)
        tb = pl.ds(pl.multiple_of(hidden + i * 128, 128), 128)
        a = gu[:, ta]
        b = gu[:, tb]
        sig = jax.nn.sigmoid(a)
        silu = a * sig
        act_o[0, :, ta] = (silu * b).astype(bf16)
        gu[:, ta] = b * (sig * (1.0 + a * (1.0 - sig)))
        gu[:, tb] = silu

    def down(i, dot):
        t = pl.ds(pl.multiple_of(i * 256, 256), 256)
        y = jnp.dot(act_o[0], w_down[0, :, t], preferred_element_type=f32).astype(bf16).astype(f32)
        c = cbrow[:, t].astype(f32)
        gyt = (gate * y).astype(bf16)
        for src in (0, 1):
            gy[src, pl.ds(e * cap, cap), t] = gyt[src * cap:(src + 1) * cap]
        dy_o[0, :, t] = (gate * c).astype(bf16)
        return dot + jnp.sum(y * c, axis=1, keepdims=True)
    dot = lax.fori_loop(0, width // 256, down, jnp.zeros((2 * cap, 1), f32), unroll=True)
    for src in (0, 1):
        back = jnp.sum(jnp.where(masks[src], dot[src * cap:(src + 1) * cap], 0.0), axis=0, keepdims=True)
        row_id = lax.broadcasted_iota(jnp.int32, (table_rows, tokens), 0)
        dots[src] += jnp.where(row_id == mine, back, 0.0)

    for start in range(0, hidden, 256):
        n = min(256, hidden - start)
        dact = lax.dot_general(dy_o[0], w_down[0, pl.ds(start, n), :], (((1,), (1,)), ((), ())), preferred_element_type=f32)
        dgu_o[0, :, pl.ds(start, n)] = (dact * gu[:, pl.ds(start, n)]).astype(bf16)
        dgu_o[0, :, pl.ds(hidden + start, n)] = (dact * gu[:, pl.ds(hidden + start, n)]).astype(bf16)

    @pl.loop(0, width // 256, unroll=True)
    def _(i):
        t = pl.ds(pl.multiple_of(i * 256, 256), 256)
        dr = lax.dot_general(dgu_o[0], w_in[0, t, :], (((1,), (1,)), ((), ())), preferred_element_type=f32).astype(bf16)
        for src in (0, 1):
            drs[src, pl.ds(e * cap, cap), t] = dr[src * cap:(src + 1) * cap]

    @pl.when(e == pl.num_programs(0) - 1)
    def _():
        for src, dro, outo in ((0, dra, outa), (1, drb, outb)):
            @pl.loop(0, width // 256, unroll=True)
            def _(i):
                t = pl.ds(pl.multiple_of(i * 256, 256), 256)
                dims = (((0,), (0,)), ((), ()))
                outo[:, t] = lax.dot_general(oh[src], gy[src, :, t], dims, preferred_element_type=f32).astype(bf16)
                dro[pl.ds(0, tokens), t] = lax.dot_general(oh[src], drs[src, :, t], dims, preferred_element_type=f32).astype(bf16)
            hi = dots[src].astype(bf16)
            lo = (dots[src] - hi.astype(f32)).astype(bf16)
            pad = jnp.zeros((2 * table_rows, width - tokens), bf16)
            dro[pl.ds(tokens, table_rows), pl.ds(0, tokens)] = hi
            dro[pl.ds(tokens + table_rows, table_rows), pl.ds(0, tokens)] = lo
            dro[pl.ds(tokens, 2 * table_rows), pl.ds(tokens, width - tokens)] = pad

def expert_step(first, h2a, h2b, cba, cbb, wr, w_in, w_down, step, steps, cap, kept):
    tokens, width = h2a.shape
    local, _, hidden2 = w_in.shape
    hidden = hidden2 // 2
    table_rows = cba.shape[0] - tokens
    bf16, f32 = jnp.bfloat16, jnp.float32
    whole = lambda a: pl.BlockSpec(a.shape, lambda e: (0,) * a.ndim, pipeline_mode=pl.Buffered(1))
    ins = [pl.BlockSpec(memory_space=pltpu.SMEM)] + [whole(a) for a in (h2a, h2b, cba, cbb, wr)]
    ins += [pl.BlockSpec((1,) + w_in.shape[1:], lambda e: (e, 0, 0)), pl.BlockSpec((1,) + w_down.shape[1:], lambda e: (e, 0, 0))]
    kept_shapes = [jax.ShapeDtypeStruct((local, steps * 2 * cap, n), bf16) for n in (width, width, hidden, 2 * hidden)]
    sums = [jax.ShapeDtypeStruct((tokens + 2 * table_rows, width), bf16)] * 2 + [jax.ShapeDtypeStruct((tokens, width), bf16)] * 2
    args = [first, h2a, h2b, cba, cbb, wr, w_in, w_down]
    alias = {}
    if kept is not None:
        ins += [pl.BlockSpec(memory_space=pl.ANY)] * 4
        alias = {len(args) + i: 4 + i for i in range(4)}
        args += list(kept)
    outs = [pl.BlockSpec(s.shape, lambda e: (0, 0), pipeline_mode=pl.Buffered(1)) for s in sums]
    outs += [pl.BlockSpec((1, 2 * cap, s.shape[2]), lambda e: (e, step, 0)) for s in kept_shapes]
    rows = 2 * cap
    flops = 2 * local * rows * (2 * (3 * width * hidden) + 4 * tokens * width)
    res = pl.pallas_call(
        lambda *r: expert_kernel(cap, tokens, hidden, None, *r),
        grid=(local,),
        in_specs=ins, out_specs=outs, out_shape=[pltpu.HBM(x.shape, x.dtype) for x in sums + kept_shapes],
        scratch_shapes=[pltpu.VMEM((rows, 2 * hidden), f32), pltpu.VMEM((rows, width), bf16), pltpu.VMEM((2, local * cap, tokens), bf16),
                        pltpu.VMEM((2, local * cap, width), bf16), pltpu.VMEM((2, local * cap, width), bf16),
                        pltpu.VMEM((2, table_rows, tokens), f32), pltpu.VMEM((2, table_rows, tokens), f32)],
        input_output_aliases=alias,
        compiler_params=pltpu.CompilerParams(vmem_limit_bytes=50 * 2**20),
        cost_estimate=pl.CostEstimate(flops=0, bytes_accessed=0, transcendentals=0),
        name="expert_step",
    )(*args)
    return res[:4], res[4:]


def token_kernel(length_ref, ids, dout, rows_o):
    f32, bf16 = jnp.float32, jnp.bfloat16
    tokens = dout.shape[0]
    table_rows = rows_o.shape[0] - tokens
    live = lax.broadcasted_iota(jnp.int32, (tokens, 1), 0) < length_ref[0]
    rows_o[pl.ds(0, tokens), :] = jnp.where(live, dout[...].astype(f32), 0.0).astype(bf16)
    lane = lax.broadcasted_iota(jnp.int32, (tokens, 128), 1)
    picked = jnp.zeros((tokens, 128), f32)
    for k in range(ids.shape[1]):
        picked = jnp.where(lane == ids[:, k:k + 1], 1.0, picked)
    picked = jnp.where(live, picked, 0.0).astype(bf16)
    earlier = lax.broadcasted_iota(jnp.int32, (tokens, tokens), 0)
    later = lax.broadcasted_iota(jnp.int32, (tokens, tokens), 1)
    before = jnp.where(earlier < later, 1.0, 0.0).astype(bf16)
    same = jnp.where(earlier == later, 1.0, 0.0).astype(bf16)
    rank = lax.dot_general(picked, before, TN, preferred_element_type=f32)
    hit = lax.dot_general(picked, same, TN, preferred_element_type=f32)
    table = jnp.where(hit > 0.5, rank, -1.0)[:table_rows].astype(bf16)
    rows_o[pl.ds(tokens, table_rows), pl.ds(0, tokens)] = table
    rows_o[pl.ds(tokens, table_rows), pl.ds(tokens, dout.shape[1] - tokens)] = jnp.zeros(
        (table_rows, dout.shape[1] - tokens), bf16
    )


def token_rows(lengths, expert_ids, dout, experts):
    return pl.pallas_call(
        token_kernel,
        in_specs=[
            pl.BlockSpec(memory_space=pltpu.SMEM),
            pl.BlockSpec(memory_space=pltpu.VMEM),
            pl.BlockSpec(memory_space=pltpu.VMEM),
        ],
        out_specs=pl.BlockSpec(memory_space=pltpu.VMEM),
        out_shape=jax.ShapeDtypeStruct((dout.shape[0] + experts, dout.shape[1]), jnp.bfloat16),
        cost_estimate=pl.CostEstimate(flops=0, bytes_accessed=0, transcendentals=0),
        name="token_rows",
    )(lengths, expert_ids, dout)


def store_grad(grad, cols, rows, mine, outs):
    low = jnp.bfloat16
    if not rows:
        outs[0][:, cols] = grad.astype(low)
        return
    for c in range(grad.shape[0] // (2 * rows)):
        first = grad[2 * c * rows : (2 * c + 1) * rows]
        second = grad[(2 * c + 1) * rows : (2 * c + 2) * rows]
        outs[0][pl.ds(c * rows, rows), cols] = jnp.where(mine, first, second).astype(low)
        outs[1][pl.ds(c * rows, rows), cols] = jnp.where(mine, second, first).astype(low)


def shared_kernel(rows, experts, core_ref, h2, cb, w_in, w_down, w_router, shared_out, grad_h2, probs, *rest):
    f32, bf16 = jnp.float32, jnp.bfloat16
    *grads, gu, hs, dgu = rest
    tokens, width = h2.shape
    hidden = w_down.shape[0]
    mine = core_ref[0] == 0
    own = pl.ds(0, tokens)

    logits = jnp.dot(h2[...], w_router[...], preferred_element_type=f32)
    column = lax.broadcasted_iota(jnp.int32, logits.shape, 1)
    logits = jnp.where(column < experts - 1, logits, MASK_VALUE)
    ex = jnp.exp(logits - jnp.max(logits, axis=1, keepdims=True))
    probs[...] = ex / jnp.sum(ex, axis=1, keepdims=True)
    for start in range(0, 2 * hidden, 256):
        t = pl.ds(start, 256)
        gu[:, t] = jnp.dot(h2[...], w_in[:, t], preferred_element_type=f32)
    for start in range(0, hidden, 128):
        ta, tb = pl.ds(start, 128), pl.ds(hidden + start, 128)
        a, b = gu[:, ta], gu[:, tb]
        sig = jax.nn.sigmoid(a)
        silu = a * sig
        hs[:, ta] = (silu * b).astype(bf16)
        gu[:, ta] = b * (sig * (1.0 + a * (1.0 - sig)))
        gu[:, tb] = silu
    for start in range(0, hidden, 256):
        n = min(256, hidden - start)
        dhs = lax.dot_general(cb[own, :], w_down[pl.ds(start, n), :], NT, preferred_element_type=f32)
        for t in (pl.ds(start, n), pl.ds(hidden + start, n)):
            dgu[:, t] = (dhs * gu[:, t]).astype(bf16)
    for start in range(0, width, 256):
        t = pl.ds(start, 256)
        shared_out[:, t] = jnp.dot(hs[...], w_down[:, t], preferred_element_type=f32)
        grad_h2[:, t] = lax.dot_general(dgu[...], w_in[t, :], NT, preferred_element_type=f32)
    for start in range(0, 2 * hidden, 256):
        t = pl.ds(start, 256)
        grad = lax.dot_general(h2[...], dgu[:, t], TN, preferred_element_type=f32)
        store_grad(grad, t, rows, mine, grads)
    for start in range(0, hidden, 256):
        n = min(256, hidden - start)
        grad = lax.dot_general(cb[own, :], hs[:, pl.ds(start, n)], TN, preferred_element_type=f32)
        store_grad(grad, pl.ds(2 * hidden + start, n), rows, mine, grads)


def shared_expert(core, h2, cb, w_in, w_down, w_router, rows, experts):
    tokens, width = h2.shape
    hidden = w_down.shape[0]
    f32, bf16 = jnp.float32, jnp.bfloat16
    sd = jax.ShapeDtypeStruct
    vmem = pl.BlockSpec(memory_space=pltpu.VMEM)
    grads = [sd((width // 2, 3 * hidden), bf16)] * 2 if rows else [sd((width, 3 * hidden), bf16)]
    outs = [sd((tokens, width), f32), sd((tokens, width), f32), sd((tokens, w_router.shape[1]), f32)] + grads
    return pl.pallas_call(
        lambda *r: shared_kernel(rows, experts, *r),
        in_specs=[pl.BlockSpec(memory_space=pltpu.SMEM)] + [vmem] * 5,
        out_specs=[vmem] * len(outs),
        out_shape=outs,
        scratch_shapes=[pltpu.VMEM((tokens, 2 * hidden), f32), pltpu.VMEM((tokens, hidden), bf16), pltpu.VMEM((tokens, 2 * hidden), bf16)],
        compiler_params=pltpu.CompilerParams(vmem_limit_bytes=48 * 2**20),
        cost_estimate=pl.CostEstimate(flops=0, bytes_accessed=0, transcendentals=0),
        name="shared_expert",
    )(core, h2, cb, w_in, w_down, w_router)


def middle_kernel(experts, length_ref, home_a, home_b, home_c, grad_shared, probs, h2, w_router, x_mid, dout, gain, grad_mid, da, small):
    f32, bf16 = jnp.float32, jnp.bfloat16
    tokens = x_mid.shape[0]
    own, table = pl.ds(0, tokens), pl.ds(tokens, 2 * experts)
    total = lambda r, c: home_a[r, c].astype(f32) + home_b[r, c].astype(f32) + home_c[r, c].astype(f32)
    dots = total(table, own)
    dots = dots[:experts] + dots[experts:]
    grad_probs = jnp.concatenate([dots, jnp.zeros((128 - experts, tokens), f32)], axis=0).T
    p = probs[...]
    low = (p * (grad_probs - jnp.sum(grad_probs * p, axis=1, keepdims=True))).astype(bf16)
    incoming = total(own, slice(None)) + grad_shared[...]
    incoming += lax.dot_general(low, w_router[...], NT, preferred_element_type=f32)
    mid = x_mid[...]
    inverse = lax.rsqrt(jnp.mean(mid * mid, axis=-1, keepdims=True) + NORM_EPS)
    scaled = mid * inverse
    column = lax.broadcasted_iota(jnp.int32, (tokens, 128), 1)
    small[...] = lax.dot_general(h2[...], low, TN, preferred_element_type=f32) + lax.dot_general(
        incoming * scaled, jnp.where(column == experts, 1.0, 0.0), TN,
        precision=lax.Precision.HIGHEST, preferred_element_type=f32,
    )
    inner = incoming * gain[...]
    back = inverse * (inner - scaled * jnp.mean(inner * scaled, axis=-1, keepdims=True))
    grad = dout[...].astype(f32) + back
    grad_mid[...] = grad
    live = lax.broadcasted_iota(jnp.int32, (tokens, 1), 0) < length_ref[0]
    da[...] = jnp.where(live, grad, 0.0).astype(bf16)


def middle_back(lengths, home, grad_shared, probs, h2, w_router, x_mid, dout, gain, experts):
    tokens, width = x_mid.shape
    f32 = jnp.float32
    sd = jax.ShapeDtypeStruct
    vmem = pl.BlockSpec(memory_space=pltpu.VMEM)
    return pl.pallas_call(
        lambda *r: middle_kernel(experts, *r),
        in_specs=[pl.BlockSpec(memory_space=pltpu.SMEM)] + [vmem] * 10,
        out_specs=[vmem] * 3,
        out_shape=[sd((tokens, width), f32), sd((tokens, width), jnp.bfloat16), sd((width, 128), f32)],
        compiler_params=pltpu.CompilerParams(vmem_limit_bytes=48 * 2**20),
        cost_estimate=pl.CostEstimate(flops=0, bytes_accessed=0, transcendentals=0),
        name="middle_back",
    )(lengths, *home, grad_shared, probs, h2, w_router, x_mid, dout, gain)


def weight_grad_kernel(parts, bit, index_ref, lhs, rhs, keep, away):
    f32, bf16 = jnp.float32, jnp.bfloat16
    grad = lax.dot_general(lhs[0], rhs[0], TN, preferred_element_type=f32)
    mine = ((index_ref[0] >> bit) & 1) == 0
    rows = grad.shape[0] // parts
    at = 0
    for c in range(parts):
        if (c >> bit) & 1:
            continue
        other = c | (1 << bit)
        first = grad[c * rows : (c + 1) * rows]
        second = grad[other * rows : (other + 1) * rows]
        keep[pl.ds(at, rows), :] = jnp.where(mine, first, second).astype(bf16)
        away[pl.ds(at, rows), :] = jnp.where(mine, second, first).astype(bf16)
        at += rows


def weight_grad(index, lhs, rhs, expert, parts, bit):
    _, rows, m = lhs.shape
    n = rhs.shape[2]
    tile = 256
    return pl.pallas_call(
        lambda *r: weight_grad_kernel(parts, bit, *r),
        grid=(n // tile,),
        in_specs=[
            pl.BlockSpec(memory_space=pltpu.SMEM),
            pl.BlockSpec((1, rows, m), lambda i: (expert, 0, 0)),
            pl.BlockSpec((1, rows, tile), lambda i: (expert, 0, i)),
        ],
        out_specs=[pl.BlockSpec((m // 2, tile), lambda i: (0, i))] * 2,
        out_shape=[jax.ShapeDtypeStruct((m // 2, n), jnp.bfloat16)] * 2,
        compiler_params=pltpu.CompilerParams(vmem_limit_bytes=48 * 2**20),
        cost_estimate=pl.CostEstimate(flops=0, bytes_accessed=0, transcendentals=0),
        name="weight_grad",
    )(index, lhs, rhs)


def rope_tables(seq_slots):
    half_dim = HEAD_DIM // 2
    inv_freq = 1.0 / 10000.0 ** (jnp.arange(half_dim, dtype=jnp.float32) * 2.0 / HEAD_DIM)
    angles = jnp.arange(seq_slots, dtype=jnp.float32)[:, None] * inv_freq[None, :]
    cosine, sine = jnp.cos(angles), jnp.sin(angles)
    return jnp.concatenate([cosine, cosine], axis=1), jnp.concatenate([-sine, sine], axis=1)


def assemble_kernel(wide, *refs):
    *pieces, qkv, out = refs
    pair, pairs = 0, out.shape[1] // wide
    for piece, count in zip(pieces, (pairs // 2, pairs // 2, pairs - 2 * (pairs // 2))):
        step = piece.shape[1] // count
        for at in range(count):
            for kind in range(4):
                block = piece[:, at * step + kind * wide : at * step + (kind + 1) * wide]
                if kind < 3:
                    qkv[:, pl.ds((kind * pairs + pair) * wide, wide)] = block
                else:
                    out[:, pl.ds(pair * wide, wide)] = block
            pair += 1


def assemble(pieces, width):
    rows = pieces[0].shape[0]
    vmem = pl.BlockSpec(memory_space=pltpu.VMEM)
    return pl.pallas_call(
        lambda *r: assemble_kernel(2 * HEAD_DIM, *r),
        in_specs=[vmem] * len(pieces),
        out_specs=[vmem] * 2,
        out_shape=[jax.ShapeDtypeStruct((rows, n), jnp.float32) for n in (3 * width, width)],
        cost_estimate=pl.CostEstimate(flops=0, bytes_accessed=0, transcendentals=0),
        name="assemble",
    )(*pieces)


def swap_cores(values_in):
    owners = lax.axis_size("expert")
    return lax.ppermute(values_in, "expert", [(i, i ^ 1) for i in range(owners)])


def next_chip(values_in):
    owners = lax.axis_size("expert")
    return lax.ppermute(values_in, "expert", [(i, (i + 2) % owners) for i in range(owners)])


def axis_bits(name):
    return [(name, bit) for bit in range(lax.axis_size(name).bit_length() - 1)]


def row_bits():
    return axis_bits("dp")[::-1] + axis_bits("expert")[::-1]


def sum_terms(parts):
    summed = parts[0].astype(jnp.float32)
    for term in parts[1:]:
        summed = summed + term.astype(jnp.float32)
    return summed


def after(values_in, *earlier):
    return lax.optimization_barrier((values_in, earlier))[0]


def picked(term, choices):
    for dim, index in choices:
        term = lax.dynamic_index_in_dim(term, index, dim, keepdims=False)
    return term


class Scatter:
    def __init__(self, terms, open_bits, order):
        self.terms, self.choices = list(terms), [[] for _ in terms]
        self.open_bits, self.order = list(open_bits), list(order)

    def advance(self, *earlier):
        name, bit = self.order.pop(0)
        dim = self.open_bits.index((name, bit))
        mine = (lax.axis_index(name) >> bit) & 1
        terms = after(self.terms, *earlier) if earlier else self.terms
        away = sum_terms(
            [picked(term, made + [(dim, 1 - mine)]) for term, made in zip(terms, self.choices)]
        ).astype(terms[0].dtype)
        came = lax.ppermute(
            away, name, [(i, i ^ (1 << bit)) for i in range(lax.axis_size(name))]
        )
        self.choices = [made + [(dim, mine)] for made in self.choices] + [[]]
        self.terms.append(came)
        self.open_bits.pop(dim)
        return away

    def finish(self):
        while self.order:
            self.advance()
        return sum_terms([picked(term, made) for term, made in zip(self.terms, self.choices)])


def split_rows(part, bits):
    rows = part.shape[0] >> len(bits)
    return part.reshape((2,) * len(bits) + (rows, part.shape[1]))


def scatter_orders():
    core, *line = axis_bits("expert")
    plane = axis_bits("dp")
    return ([core] + plane + line, [core] + plane[::-1] + line, [core] + plane + line)


def per_device(
    layer_input,
    lengths,
    expert_ids,
    norm1,
    w_qkv,
    w_out,
    norm2,
    w_router,
    w_shared_in,
    w_shared_down,
    w_expert_in,
    w_expert_down,
    dout,
):
    seq_slots, width = layer_input.shape
    top_k = expert_ids.shape[1]
    experts = w_router.shape[1]
    local_experts = w_expert_in.shape[0]
    hidden_units = w_shared_down.shape[0]
    capacity = (seq_slots * top_k // (experts - 1) // 8 + 1) * 8
    live_col = (jnp.arange(seq_slots, dtype=jnp.int32) < lengths[0]).astype(jnp.float32)[:, None]
    cosine, sine = rope_tables(seq_slots)

    bits = row_bits()
    rows = width >> len(bits)
    rows = rows if rows % 8 == 0 else 0
    core = (lax.axis_index("expert") & 1).astype(jnp.int32)[None]
    orders = scatter_orders()
    chips = experts // local_experts // 2
    first_expert = (lax.axis_index("expert") * local_experts).astype(jnp.int32)[None]
    router_t = w_router.T

    def start_scatter(grads, order):
        if rows:
            terms = [split_rows(grads[0], bits[:-1]), split_rows(swap_cores(grads[1]), bits[:-1])]
            return Scatter(terms, bits[:-1], order[1:])
        return Scatter([split_rows(grads[0], bits)], bits, order)

    def run_step(step, h2_pair, grad_pair, kept, *earlier):
        sums, kept = expert_step(
            first_expert, after(h2_pair[0], *earlier), h2_pair[1], grad_pair[0], grad_pair[1],
            router_t, w_expert_in, w_expert_down, step, chips, capacity, kept,
        )
        parts.append(sums)
        return kept, sums[0]

    parts = []
    router_wide = jnp.pad(w_router, ((0, 0), (0, 128 - experts)))
    grad_table = token_rows(lengths, expert_ids, dout, experts)
    grad_here = (grad_table, swap_cores(grad_table))
    grad_next = next_chip(grad_table)
    counts_here = jnp.sum((grad_table[seq_slots:, :seq_slots] >= 0).astype(jnp.int32), axis=1)
    places = jnp.minimum(jnp.arange(width >> len(bits), dtype=jnp.int32), 30)
    digits = ((counts_here[None, :] >> places[:, None]) & 1).astype(jnp.float32)
    small_columns = -(-(2 * experts + 2) // 128) * 128
    digits = jnp.pad(
        jnp.tile(digits, (1 << len(bits), 1)),
        ((0, 0), (experts + 2, small_columns - 2 * experts - 2)),
    )
    h1_low, queries, keys_in, values_in, attended_low, log_norm, x_mid, h2_low = attention_forward(
        lengths, after(layer_input, grad_table), norm1[None, :], w_qkv, cosine, sine, w_out,
        norm2[None, :],
    )
    h2_here = (h2_low, swap_cores(h2_low))
    h2_next = next_chip(h2_low)
    grad_next = after(grad_next, h2_low)
    grad_other = swap_cores(grad_next)
    grad_ahead = next_chip(grad_next)
    kept, done = run_step(0, h2_here, grad_here, None, grad_next)
    shared_out, grad_shared, router_probs, *shared_grads = shared_expert(
        core, after(h2_low, done), grad_table, w_shared_in, w_shared_down, router_wide, rows, experts
    )
    fence = shared_out
    shared_away = []
    swapped = []
    shared_scatter = None
    travelling = None
    for step in range(1, chips):
        h2_next, grad_next = after(h2_next, fence), after(grad_next, fence)
        pair_h2 = (h2_next, swap_cores(h2_next))
        pair_grad = (grad_next, grad_other)
        if shared_scatter is None:
            ready = (fence, grad_ahead, pair_h2[1], grad_other)
            shared_scatter = start_scatter(after(shared_grads, *ready), orders[0])
            swapped.append(swap_cores(after(parts[0][3], *ready)))
        earlier = [] if travelling is None else [travelling]
        earlier += shared_away
        if step + 1 < chips:
            h2_next = next_chip(h2_next)
            grad_next = after(grad_ahead, fence)
            grad_other = swap_cores(grad_next)
            if step + 2 < chips:
                grad_ahead = next_chip(grad_next)
        kept, fence = run_step(step, pair_h2, pair_grad, kept, *earlier)
        mine, theirs = parts[step][:2]
        if step + 1 < chips:
            theirs = after(theirs, h2_next, grad_ahead)
        theirs = after(theirs, *swapped)
        if step == 2:
            first_routed = parts[1][2].astype(jnp.float32) + swapped[1].astype(jnp.float32)
            first_routed = first_routed.astype(jnp.bfloat16)
            theirs = after(theirs, first_routed)
        swapped.append(swap_cores(after(parts[step][3], theirs)))
        if shared_away:
            theirs = after(theirs, shared_scatter.terms[-1])
        if shared_scatter.order[0][0] == "dp":
            shared_away = [shared_scatter.advance(fence)]
            theirs = after(theirs, *shared_away)
        if travelling is None:
            total = mine.astype(jnp.float32) + swap_cores(theirs).astype(jnp.float32)
        else:
            came = next_chip(travelling)
            total = (
                mine.astype(jnp.float32)
                + swap_cores(after(theirs, came)).astype(jnp.float32)
                + came.astype(jnp.float32)
            )
        travelling = total.astype(mine.dtype)

    home_hop = next_chip(travelling)
    rows_held, grad_result, expert_hidden, grad_expert_gu = kept

    plane = axis_bits("dp")
    plane_index = lax.axis_index("dp").astype(jnp.int32)[None]

    def expert_grads(lhs, rhs, expert):
        order = plane if expert % 2 == 0 else plane[::-1]
        return order, weight_grad(
            plane_index, lhs, rhs, expert, 1 << len(plane), order[0][1]
        )

    def plane_scatter(order, grads, *earlier):
        name, bit = order[0]
        keep, away = after(grads, *earlier) if earlier else grads
        came = lax.ppermute(
            away, name, [(i, i ^ (1 << bit)) for i in range(lax.axis_size(name))]
        )
        open_bits = [place for place in plane[::-1] if place != order[0]]
        terms = [split_rows(piece, open_bits) for piece in (keep, came)]
        return Scatter(terms, open_bits, order[1:])

    fence = [travelling, shared_scatter.terms[-1]]
    down_parts, in_parts = [], []
    for i in range(local_experts):
        down_parts.append(expert_grads(after(expert_hidden, *fence), grad_result, i))
        fence = down_parts[-1][1]
    down_scatters = [plane_scatter(*part) for part in down_parts]
    for i in range(local_experts):
        in_parts.append(expert_grads(after(rows_held, *fence), grad_expert_gu, i))
        fence = in_parts[-1][1]

    mine, theirs = parts[0][:2]
    own_home = (mine, swap_cores(after(theirs, travelling)))
    out_order = list(range(1, chips)) + [0]

    def add_routed(index, came, *earlier):
        mine, theirs = after((parts[out_order[index]][2], swapped[out_order[index]]), *earlier)
        total = mine.astype(jnp.float32) + theirs.astype(jnp.float32)
        return total if came is None else total + came.astype(jnp.float32)

    routed = first_routed if chips > 2 else add_routed(0, None, travelling).astype(jnp.bfloat16)
    landed = list(fence) + [home_hop, own_home[1], swapped[-1], routed]
    landed += [scatter.terms[-1] for scatter in down_scatters]
    in_scatters = [plane_scatter(*part, *landed) for part in in_parts]
    out_hop = next_chip(after(routed, *landed))
    fence = landed
    for scatter in down_scatters:
        fence = [scatter.advance(*fence)]
    home = after((*own_home, home_hop), *fence)
    grad_mid, grad_attn_branch, small = middle_back(
        lengths, home, grad_shared, router_probs, h2_low, router_wide, x_mid, dout, norm2[None, :],
        experts,
    )
    small = digits + jnp.pad(small, ((0, 0), (0, small_columns - 128)))

    pairs = width // (2 * HEAD_DIM)
    half = (pairs - 1) // 2
    cuts = (0, half, 2 * half, pairs)
    running = None
    columns = []
    fence = [grad_attn_branch]
    for index, (first, last) in enumerate(zip(cuts[:-1], cuts[1:])):
        tail = None
        if last == pairs:
            tail = (experts, (layer_input, norm1[None, :], grad_mid, small))
        *grads, running = attention_backward(
            lengths, core, after(grad_attn_branch, *fence), w_out, queries, keys_in, values_in,
            log_norm, cosine, sine, h1_low, attended_low, w_qkv, running, first, last - first, rows,
            tail,
        )
        fence = [running]
        columns.append(grads)
        if index == 0:
            routed = add_routed(1, out_hop, running).astype(jnp.bfloat16)
            out_hop = next_chip(routed)
            fence.append(routed)
    grad_input = running
    landed = [running, out_hop]
    landed += [scatter.terms[-1] for scatter in in_scatters + down_scatters]
    scatters = []
    for grads, order in zip(columns, orders):
        scatters.append(start_scatter(after(grads, *landed), order))
    fence = landed
    hops = 2
    first_cols, second_cols, third_cols = scatters
    plan = [first_cols, second_cols, None, third_cols, shared_scatter, first_cols, second_cols, third_cols, shared_scatter, None, first_cols, second_cols, third_cols, in_scatters[0], in_scatters[1], first_cols, second_cols, third_cols]
    for scatter in plan:
        if scatter is not None:
            if scatter.order:
                fence = [scatter.advance(*fence)]
        elif hops < chips:
            routed = add_routed(hops, out_hop, *fence)
            hops += 1
            if hops < chips:
                out_hop = next_chip(routed.astype(jnp.bfloat16))
            fence = [routed]
    for hops in range(hops, chips):
        routed = add_routed(hops, out_hop, *fence)
        out_hop = next_chip(routed.astype(jnp.bfloat16))
    for scatter in down_scatters + in_scatters + [shared_scatter]:
        scatter.terms = after(scatter.terms, *fence)
    result = (x_mid + live_col * (shared_out + routed)).astype(jnp.bfloat16)
    shared_sum = shared_scatter.finish()
    expert_in_sum = jnp.stack([scatter.finish() for scatter in in_scatters])
    expert_down_sum = jnp.stack([scatter.finish() for scatter in down_scatters])
    pieces = [scatter.finish() for scatter in scatters]
    qkv_sum, out_sum = assemble(pieces, width)
    small_sum = pieces[-1][:, 8 * HEAD_DIM :]
    counts = jnp.sum(
        small_sum[:, experts + 2 : 2 * experts + 2] * (1 << places).astype(jnp.float32)[:, None],
        axis=0,
    )
    return (
        result,
        grad_input,
        small_sum[:, experts + 1],
        qkv_sum,
        out_sum,
        small_sum[:, experts],
        small_sum[:, :experts],
        shared_sum[:, : 2 * hidden_units],
        shared_sum[:, 2 * hidden_units :].T,
        expert_in_sum,
        expert_down_sum,
        counts.astype(jnp.int32),
    )


def solution(mesh):
    return jax.shard_map(
        per_device,
        mesh=mesh,
        in_specs=(
            P(("dp", "expert"), None),
            P(("dp", "expert")),
            P(("dp", "expert"), None),
            P(),
            P(),
            P(),
            P(),
            P(),
            P(),
            P(),
            P("expert", None, None),
            P("expert", None, None),
            P(("dp", "expert"), None),
        ),
        out_specs=(
            P(("dp", "expert"), None),
            P(("dp", "expert"), None),
            P(("dp", "expert")),
            P(("dp", "expert"), None),
            P(("dp", "expert"), None),
            P(("dp", "expert")),
            P(("dp", "expert"), None),
            P(("dp", "expert"), None),
            P(None, ("dp", "expert")),
            P("expert", "dp", None),
            P("expert", "dp", None),
            P(),
        ),
        check_vma=False,
    )
```

```python
import jax
import jax.numpy as jnp
from jax import lax
from jax.experimental import pallas as pl
from jax.experimental.pallas import tpu as pltpu
from jax.sharding import PartitionSpec as P

HEAD_DIM = 128
NORM_EPS = 1e-06
MASK_VALUE = -1e30
NT = (((1,), (1,)), ((), ()))
TN = (((0,), (0,)), ((), ()))

def turn(values_in, cosine, signed_sine):
    return values_in * cosine + pltpu.roll(values_in, HEAD_DIM // 2, 1) * signed_sine

def block_scores(q, k, start, seq_length):
    s = lax.dot_general(q, k, NT, preferred_element_type=jnp.float32) * HEAD_DIM ** (-0.5)
    query_pos = start + lax.broadcasted_iota(jnp.int32, s.shape, 0)
    key_pos = lax.broadcasted_iota(jnp.int32, s.shape, 1)
    return jnp.where((key_pos <= query_pos) & (key_pos < seq_length), s, MASK_VALUE)

def attention_kernel(length_ref, x, norm1, wq, wk, wv, cosine, sine, w_out, norm2, h1, q_o, k_o, v_o, att, lse, x_mid, h2):
    f32, bf16 = jnp.float32, jnp.bfloat16
    p = pl.program_id(0)
    tokens = x.shape[0]
    seq_length = length_ref[0]
    span = min(256, tokens)

    @pl.when(p == 0)
    def _():
        xf = x[...].astype(f32)
        inverse = lax.rsqrt(jnp.mean(xf * xf, axis=-1, keepdims=True) + NORM_EPS)
        h1[...] = (xf * inverse * norm1[...]).astype(bf16)
        lse[...] = jnp.zeros_like(lse)

    for w, o in ((wq, q_o), (wk, k_o), (wv, v_o)):
        full = jnp.dot(h1[...], w[...], preferred_element_type=f32)
        for j in (0, 1):
            part = full[:, j * HEAD_DIM:(j + 1) * HEAD_DIM]
            if w is not wv:
                part = turn(part, cosine[...], sine[...])
            o[:, pl.ds(j * HEAD_DIM, HEAD_DIM)] = part.astype(bf16)
    lane = lax.broadcasted_iota(jnp.int32, (span, lse.shape[1]), 1)
    for j in (0, 1):
        cols = pl.ds(j * HEAD_DIM, HEAD_DIM)
        for start in range(0, tokens, span):
            rows = pl.ds(start, span)
            seen = pl.ds(0, start + span)
            s = block_scores(q_o[rows, cols], k_o[seen, cols], start, seq_length)
            high = jnp.max(s, axis=-1, keepdims=True)
            ex = jnp.exp(s - high)
            total = jnp.sum(ex, axis=-1, keepdims=True)
            low = (ex / total).astype(bf16)
            out = jnp.dot(low, v_o[seen, cols], preferred_element_type=f32)
            att[rows, pl.ds(pl.multiple_of(p * 2 * HEAD_DIM + j * HEAD_DIM, HEAD_DIM), HEAD_DIM)] = out.astype(bf16)
            lse[rows, :] = jnp.where(lane == 2 * p + j, high + jnp.log(total), lse[rows, :])

    @pl.when(p == pl.num_programs(0) - 1)
    def _():
        branch = jnp.dot(att[...], w_out[...], preferred_element_type=f32)
        live = lax.broadcasted_iota(jnp.int32, (tokens, 1), 0) < seq_length
        mid = x[...].astype(f32) + jnp.where(live, branch, 0.0)
        x_mid[...] = mid
        inverse = lax.rsqrt(jnp.mean(mid * mid, axis=-1, keepdims=True) + NORM_EPS)
        h2[...] = (mid * inverse * norm2[...]).astype(bf16)

def whole(a):
    return pl.BlockSpec(a.shape, lambda p: (0,) * len(a.shape), pipeline_mode=pl.Buffered(1))

def attention_forward(lengths, x, norm1, w_qkv, cosine, sine, w_out, norm2):
    tokens, width = x.shape
    pairs = width // (2 * HEAD_DIM)
    f32, bf16 = jnp.float32, jnp.bfloat16
    wide = 2 * HEAD_DIM
    col = lambda k: pl.BlockSpec((width, wide), lambda p, k=k: (0, k * pairs + p))
    head = pl.BlockSpec((tokens, wide), lambda p: (0, p))
    full = pl.BlockSpec((tokens, width), lambda p: (0, 0))
    sd = jax.ShapeDtypeStruct
    return pl.pallas_call(
        attention_kernel, grid=(pairs,),
        in_specs=[pl.BlockSpec(memory_space=pltpu.SMEM), whole(x), whole(norm1), col(0), col(1), col(2), whole(cosine), whole(sine), whole(w_out), whole(norm2)],
        out_specs=[full, head, head, head, full, pl.BlockSpec((tokens, 128), lambda p: (0, 0)), full, full],
        out_shape=[pltpu.HBM((tokens, width), bf16)] * 5 + [pltpu.HBM((tokens, 128), f32), pltpu.HBM((tokens, width), f32), pltpu.HBM((tokens, width), bf16)],
        compiler_params=pltpu.CompilerParams(vmem_limit_bytes=48 * 2**20),
        cost_estimate=pl.CostEstimate(flops=0, bytes_accessed=0, transcendentals=0),
        name="attention_forward",
    )(lengths, x, norm1, w_qkv, w_qkv, w_qkv, cosine, sine, w_out, norm2)

def attention_back_kernel(rows, extra, carried, length_ref, core_ref, da, w_out, q, k, v, lse, cosine, sine, h1, att, wq, wk, wv, *rest):
    f32, bf16 = jnp.float32, jnp.bfloat16
    dh1_in = None
    if carried:
        dh1_in, *rest = rest
    if extra:
        x, gain, grad_mid, small, *rest = rest
    *grads, dh1, dk_s, dv_s, dproj = rest
    p = pl.program_id(0)
    pair = length_ref[1] + p
    tokens, width = da.shape
    seq_length = length_ref[0]
    span = min(256, tokens)
    scale = HEAD_DIM ** (-0.5)
    mine = core_ref[0] == 0
    wide = 2 * HEAD_DIM
    do_full = lax.dot_general(da[...], w_out[...], NT, preferred_element_type=f32).astype(bf16)
    lane = lax.broadcasted_iota(jnp.int32, (span, lse.shape[1]), 1)
    back_sine = -sine[...]
    for j in (0, 1):
        cols = pl.ds(j * HEAD_DIM, HEAD_DIM)
        do_head = do_full[:, j * HEAD_DIM : (j + 1) * HEAD_DIM]
        for start in range(tokens - span, -1, -span):
            r = pl.ds(start, span)
            seen = pl.ds(0, start + span)
            s = block_scores(q[r, cols], k[seen, cols], start, seq_length)
            norm = jnp.sum(jnp.where(lane == 2 * pair + j, lse[r, :], 0.0), axis=1, keepdims=True)
            probs = jnp.exp(s - norm)
            do = do_head[start : start + span]
            dp = lax.dot_general(do, v[seen, cols], NT, preferred_element_type=f32)
            row = jnp.sum(dp * probs, axis=1, keepdims=True)
            ds = (probs * (dp - row)).astype(bf16)
            dq = jnp.dot(ds, k[seen, cols], preferred_element_type=f32) * scale
            dproj[r, pl.ds(j * HEAD_DIM, HEAD_DIM)] = turn(
                dq, cosine[r, :], back_sine[start : start + span]
            ).astype(bf16)
            dk = lax.dot_general(ds, q[r, cols], TN, preferred_element_type=f32) * scale
            dv = lax.dot_general(probs.astype(bf16), do, TN, preferred_element_type=f32)
            if start == tokens - span:
                dk_s[seen, :] = dk
                dv_s[seen, :] = dv
            else:
                dk_s[seen, :] += dk
                dv_s[seen, :] += dv
        dproj[:, pl.ds(wide + j * HEAD_DIM, HEAD_DIM)] = turn(dk_s[...], cosine[...], back_sine).astype(bf16)
        dproj[:, pl.ds(2 * wide + j * HEAD_DIM, HEAD_DIM)] = dv_s[...].astype(bf16)
    total = jnp.where(p == 0, dh1_in[...] if carried else 0.0, dh1[...])
    for i, w in enumerate((wq, wk, wv)):
        part = dproj[:, pl.ds(i * wide, wide)]
        grad = lax.dot_general(h1[...], part, TN, preferred_element_type=f32)
        store_grad(grad, pl.ds(i * wide, wide), rows, mine, grads)
        total += lax.dot_general(part, w[...], NT, preferred_element_type=f32)
    part = da[:, pl.ds(pl.multiple_of(pair * wide, wide), wide)]
    grad = lax.dot_general(att[...], part, TN, preferred_element_type=f32)
    store_grad(grad, pl.ds(3 * wide, wide), rows, mine, grads)
    dh1[...] = total
    if not extra:
        return

    @pl.when(p < pl.num_programs(0) - 1)
    def _():
        store_grad(jnp.zeros(small.shape, f32), pl.ds(4 * wide, small.shape[1]), rows, mine, grads)

    @pl.when(p == pl.num_programs(0) - 1)
    def _():
        full = x[...].astype(f32)
        inverse = lax.rsqrt(jnp.mean(full * full, axis=-1, keepdims=True) + NORM_EPS)
        scaled = full * inverse
        inner = total * gain[...]
        dh1[...] = grad_mid[...] + inverse * (
            inner - scaled * jnp.mean(inner * scaled, axis=-1, keepdims=True)
        )
        column = lax.broadcasted_iota(jnp.int32, (tokens, small.shape[1]), 1)
        grad = small[...] + lax.dot_general(
            total * scaled, jnp.where(column == extra + 1, 1.0, 0.0), TN,
            precision=lax.Precision.HIGHEST, preferred_element_type=f32,
        )
        store_grad(grad, pl.ds(4 * wide, small.shape[1]), rows, mine, grads)


def attention_backward(lengths, core, da, w_out, q, k, v, lse, cosine, sine, h1, att, w_qkv, dh1_in, first, count, rows, tail):
    tokens, width = da.shape
    pairs = width // (2 * HEAD_DIM)
    wide = 2 * HEAD_DIM
    f32, bf16 = jnp.float32, jnp.bfloat16
    col = lambda k: pl.BlockSpec((width, wide), lambda p, k=k: (0, k * pairs + first + p))
    head = pl.BlockSpec((tokens, wide), lambda p: (0, first + p))
    sd = jax.ShapeDtypeStruct
    smem = pl.BlockSpec(memory_space=pltpu.SMEM)
    n = width // 2 if rows else width
    extra, tail_args = tail if tail else (0, ())
    columns = 4 * wide + (tail_args[-1].shape[1] if extra else 0)
    grads = [sd((n, count * columns), bf16)] * (2 if rows else 1)
    carried = dh1_in is not None
    tail_args = ((dh1_in,) if carried else ()) + tuple(tail_args)
    whole_args = (da, lse, cosine, sine, h1, att) + tail_args
    spec = {id(a): whole(a) for a in whole_args}
    *held, h1_held, att_held = (
        pltpu.with_memory_space_constraint(a, pltpu.HBM) for a in (q, k, v, h1, att)
    )
    return pl.pallas_call(
        lambda *r: attention_back_kernel(rows, extra, carried, *r),
        grid=(count,),
        in_specs=[smem, smem, spec[id(da)], pl.BlockSpec((wide, width), lambda p: (first + p, 0)), head, head, head]
        + [spec[id(a)] for a in (lse, cosine, sine, h1, att)]
        + [col(0), col(1), col(2)]
        + [spec[id(a)] for a in tail_args],
        out_specs=[pl.BlockSpec((n, columns), lambda p: (0, p))] * len(grads)
        + [pl.BlockSpec((tokens, width), lambda p: (0, 0))],
        out_shape=grads + [sd((tokens, width), f32)],
        scratch_shapes=[pltpu.VMEM((tokens, HEAD_DIM), f32), pltpu.VMEM((tokens, HEAD_DIM), f32), pltpu.VMEM((tokens, 3 * wide), bf16)],
        compiler_params=pltpu.CompilerParams(vmem_limit_bytes=48 * 2**20),
        cost_estimate=pl.CostEstimate(flops=0, bytes_accessed=0, transcendentals=0),
        name="attention_backward",
    )(
        jnp.concatenate([lengths, jnp.full((1,), first, jnp.int32)]), core, da, w_out, *held,
        lse, cosine, sine, h1_held, att_held, w_qkv, w_qkv, w_qkv, *tail_args,
    )


def expert_kernel(cap, tokens, hidden, unrolled, *refs):
    (first_ref, h2a, h2b, cba, cbb, wr, w_in, w_down) = refs[:8]
    (dra, drb, outa, outb, rows_o, dy_o, act_o, dgu_o, gu, cbrow, oh, gy, drs, probs, dots) = refs[-15:]
    f32, bf16 = jnp.float32, jnp.bfloat16
    e = pl.program_id(0)
    experts = wr.shape[0]
    width = wr.shape[1]
    mine = first_ref[0] + e
    table_rows = probs.shape[1]

    @pl.when(e == 0)
    def _():
        for src, h2 in ((0, h2a), (1, h2b)):
            logits = lax.dot_general(wr[...], h2[...], (((1,), (1,)), ((), ())), preferred_element_type=f32)
            row = lax.broadcasted_iota(jnp.int32, logits.shape, 0)
            logits = jnp.where(row < experts - 1, logits, MASK_VALUE)
            ex = jnp.exp(logits - jnp.max(logits, axis=0, keepdims=True))
            probs[src] = ex / jnp.sum(ex, axis=0, keepdims=True)
            dots[src] = jnp.zeros_like(probs[src])

    gates = []
    masks = []
    for src, h2, cb in ((0, h2a, cba), (1, h2b, cbb)):
        row_id = lax.broadcasted_iota(jnp.int32, (table_rows, tokens), 0)
        table = cb[pl.ds(tokens, table_rows), pl.ds(0, tokens)].astype(f32)
        rank = jnp.sum(jnp.where(row_id == mine, table, 0.0), axis=0, keepdims=True)
        prob = jnp.sum(jnp.where(row_id == mine, probs[src], 0.0), axis=0, keepdims=True)
        hit = lax.broadcasted_iota(jnp.int32, (cap, tokens), 0).astype(f32) == rank
        masks.append(hit)
        gates.append(jnp.sum(jnp.where(hit, prob, 0.0), axis=1, keepdims=True))
        onehot = jnp.where(hit, 1.0, 0.0).astype(bf16)
        oh[src, pl.ds(e * cap, cap), :] = onehot
        half = pl.ds(src * cap, cap)
        @pl.loop(0, width // 256, unroll=unrolled)
        def _(i):
            t = pl.ds(pl.multiple_of(i * 256, 256), 256)
            rows_o[0, half, t] = jnp.dot(onehot, h2[:, t], preferred_element_type=f32).astype(bf16)
            cbrow[half, t] = jnp.dot(onehot, cb[pl.ds(0, tokens), t], preferred_element_type=f32).astype(bf16)
    gate = jnp.concatenate(gates, axis=0)

    @pl.loop(0, 2 * hidden // 256, unroll=unrolled)
    def _(i):
        t = pl.ds(pl.multiple_of(i * 256, 256), 256)
        gu[:, t] = jnp.dot(rows_o[0], w_in[0, :, t], preferred_element_type=f32)

    @pl.loop(0, hidden // 128, unroll=unrolled)
    def _(i):
        ta = pl.ds(pl.multiple_of(i * 128, 128), 128)
        tb = pl.ds(pl.multiple_of(hidden + i * 128, 128), 128)
        a = gu[:, ta]
        b = gu[:, tb]
        sig = jax.nn.sigmoid(a)
        silu = a * sig
        act_o[0, :, ta] = (silu * b).astype(bf16)
        gu[:, ta] = b * (sig * (1.0 + a * (1.0 - sig)))
        gu[:, tb] = silu

    def down(i, dot):
        t = pl.ds(pl.multiple_of(i * 256, 256), 256)
        y = jnp.dot(act_o[0], w_down[0, :, t], preferred_element_type=f32).astype(bf16).astype(f32)
        c = cbrow[:, t].astype(f32)
        gyt = (gate * y).astype(bf16)
        for src in (0, 1):
            gy[src, pl.ds(e * cap, cap), t] = gyt[src * cap:(src + 1) * cap]
        dy_o[0, :, t] = (gate * c).astype(bf16)
        return dot + jnp.sum(y * c, axis=1, keepdims=True)
    dot = lax.fori_loop(0, width // 256, down, jnp.zeros((2 * cap, 1), f32), unroll=unrolled)
    for src in (0, 1):
        back = jnp.sum(jnp.where(masks[src], dot[src * cap:(src + 1) * cap], 0.0), axis=0, keepdims=True)
        row_id = lax.broadcasted_iota(jnp.int32, (table_rows, tokens), 0)
        dots[src] += jnp.where(row_id == mine, back, 0.0)

    for start in range(0, hidden, 256):
        n = min(256, hidden - start)
        dact = lax.dot_general(dy_o[0], w_down[0, pl.ds(start, n), :], (((1,), (1,)), ((), ())), preferred_element_type=f32)
        dgu_o[0, :, pl.ds(start, n)] = (dact * gu[:, pl.ds(start, n)]).astype(bf16)
        dgu_o[0, :, pl.ds(hidden + start, n)] = (dact * gu[:, pl.ds(hidden + start, n)]).astype(bf16)

    @pl.loop(0, width // 256, unroll=unrolled)
    def _(i):
        t = pl.ds(pl.multiple_of(i * 256, 256), 256)
        dr = lax.dot_general(dgu_o[0], w_in[0, t, :], (((1,), (1,)), ((), ())), preferred_element_type=f32).astype(bf16)
        for src in (0, 1):
            drs[src, pl.ds(e * cap, cap), t] = dr[src * cap:(src + 1) * cap]

    @pl.when(e == pl.num_programs(0) - 1)
    def _():
        for src, dro, outo in ((0, dra, outa), (1, drb, outb)):
            @pl.loop(0, width // 256, unroll=unrolled)
            def _(i):
                t = pl.ds(pl.multiple_of(i * 256, 256), 256)
                dims = (((0,), (0,)), ((), ()))
                outo[:, t] = lax.dot_general(oh[src], gy[src, :, t], dims, preferred_element_type=f32).astype(bf16)
                dro[pl.ds(0, tokens), t] = lax.dot_general(oh[src], drs[src, :, t], dims, preferred_element_type=f32).astype(bf16)
            hi = dots[src].astype(bf16)
            lo = (dots[src] - hi.astype(f32)).astype(bf16)
            pad = jnp.zeros((2 * table_rows, width - tokens), bf16)
            dro[pl.ds(tokens, table_rows), pl.ds(0, tokens)] = hi
            dro[pl.ds(tokens + table_rows, table_rows), pl.ds(0, tokens)] = lo
            dro[pl.ds(tokens, 2 * table_rows), pl.ds(tokens, width - tokens)] = pad

def expert_step(first, h2a, h2b, cba, cbb, wr, w_in, w_down, step, steps, cap, kept):
    tokens, width = h2a.shape
    local, _, hidden2 = w_in.shape
    hidden = hidden2 // 2
    table_rows = cba.shape[0] - tokens
    bf16, f32 = jnp.bfloat16, jnp.float32
    whole = lambda a: pl.BlockSpec(a.shape, lambda e: (0,) * a.ndim, pipeline_mode=pl.Buffered(1))
    ins = [pl.BlockSpec(memory_space=pltpu.SMEM)] + [whole(a) for a in (h2a, h2b, cba, cbb, wr)]
    ins += [pl.BlockSpec((1,) + w_in.shape[1:], lambda e: (e, 0, 0)), pl.BlockSpec((1,) + w_down.shape[1:], lambda e: (e, 0, 0))]
    kept_shapes = [jax.ShapeDtypeStruct((local, steps * 2 * cap, n), bf16) for n in (width, width, hidden, 2 * hidden)]
    sums = [jax.ShapeDtypeStruct((tokens + 2 * table_rows, width), bf16)] * 2 + [jax.ShapeDtypeStruct((tokens, width), bf16)] * 2
    args = [first, h2a, h2b, cba, cbb, wr, w_in, w_down]
    alias = {}
    if kept is not None:
        ins += [pl.BlockSpec(memory_space=pl.ANY)] * 4
        alias = {len(args) + i: 4 + i for i in range(4)}
        args += list(kept)
    outs = [pl.BlockSpec(s.shape, lambda e: (0, 0), pipeline_mode=pl.Buffered(1)) for s in sums]
    outs += [pl.BlockSpec((1, 2 * cap, s.shape[2]), lambda e: (e, step, 0)) for s in kept_shapes]
    rows = 2 * cap
    flops = 2 * local * rows * (2 * (3 * width * hidden) + 4 * tokens * width)
    res = pl.pallas_call(
        lambda *r: expert_kernel(cap, tokens, hidden, step in (0, steps - 1), *r),
        grid=(local,),
        in_specs=ins, out_specs=outs, out_shape=[pltpu.HBM(x.shape, x.dtype) for x in sums + kept_shapes],
        scratch_shapes=[pltpu.VMEM((rows, 2 * hidden), f32), pltpu.VMEM((rows, width), bf16), pltpu.VMEM((2, local * cap, tokens), bf16),
                        pltpu.VMEM((2, local * cap, width), bf16), pltpu.VMEM((2, local * cap, width), bf16),
                        pltpu.VMEM((2, table_rows, tokens), f32), pltpu.VMEM((2, table_rows, tokens), f32)],
        input_output_aliases=alias,
        compiler_params=pltpu.CompilerParams(vmem_limit_bytes=50 * 2**20),
        cost_estimate=pl.CostEstimate(flops=0, bytes_accessed=0, transcendentals=0),
        name="expert_step",
    )(*args)
    return res[:4], res[4:]


def token_kernel(length_ref, ids, dout, rows_o):
    f32, bf16 = jnp.float32, jnp.bfloat16
    tokens = dout.shape[0]
    table_rows = rows_o.shape[0] - tokens
    live = lax.broadcasted_iota(jnp.int32, (tokens, 1), 0) < length_ref[0]
    rows_o[pl.ds(0, tokens), :] = jnp.where(live, dout[...].astype(f32), 0.0).astype(bf16)
    lane = lax.broadcasted_iota(jnp.int32, (tokens, 128), 1)
    picked = jnp.zeros((tokens, 128), f32)
    for k in range(ids.shape[1]):
        picked = jnp.where(lane == ids[:, k:k + 1], 1.0, picked)
    picked = jnp.where(live, picked, 0.0).astype(bf16)
    earlier = lax.broadcasted_iota(jnp.int32, (tokens, tokens), 0)
    later = lax.broadcasted_iota(jnp.int32, (tokens, tokens), 1)
    before = jnp.where(earlier < later, 1.0, 0.0).astype(bf16)
    same = jnp.where(earlier == later, 1.0, 0.0).astype(bf16)
    rank = lax.dot_general(picked, before, TN, preferred_element_type=f32)
    hit = lax.dot_general(picked, same, TN, preferred_element_type=f32)
    table = jnp.where(hit > 0.5, rank, -1.0)[:table_rows].astype(bf16)
    rows_o[pl.ds(tokens, table_rows), pl.ds(0, tokens)] = table
    rows_o[pl.ds(tokens, table_rows), pl.ds(tokens, dout.shape[1] - tokens)] = jnp.zeros(
        (table_rows, dout.shape[1] - tokens), bf16
    )


def token_rows(lengths, expert_ids, dout, experts):
    return pl.pallas_call(
        token_kernel,
        in_specs=[
            pl.BlockSpec(memory_space=pltpu.SMEM),
            pl.BlockSpec(memory_space=pltpu.VMEM),
            pl.BlockSpec(memory_space=pltpu.VMEM),
        ],
        out_specs=pl.BlockSpec(memory_space=pltpu.VMEM),
        out_shape=jax.ShapeDtypeStruct((dout.shape[0] + experts, dout.shape[1]), jnp.bfloat16),
        cost_estimate=pl.CostEstimate(flops=0, bytes_accessed=0, transcendentals=0),
        name="token_rows",
    )(lengths, expert_ids, dout)


def store_grad(grad, cols, rows, mine, outs):
    low = jnp.bfloat16
    if not rows:
        outs[0][:, cols] = grad.astype(low)
        return
    for c in range(grad.shape[0] // (2 * rows)):
        first = grad[2 * c * rows : (2 * c + 1) * rows]
        second = grad[(2 * c + 1) * rows : (2 * c + 2) * rows]
        outs[0][pl.ds(c * rows, rows), cols] = jnp.where(mine, first, second).astype(low)
        outs[1][pl.ds(c * rows, rows), cols] = jnp.where(mine, second, first).astype(low)


def shared_kernel(rows, experts, core_ref, h2, cb, w_in, w_down, w_router, shared_out, grad_h2, probs, *rest):
    f32, bf16 = jnp.float32, jnp.bfloat16
    *grads, gu, hs, dgu = rest
    tokens, width = h2.shape
    hidden = w_down.shape[0]
    mine = core_ref[0] == 0
    own = pl.ds(0, tokens)

    logits = jnp.dot(h2[...], w_router[...], preferred_element_type=f32)
    column = lax.broadcasted_iota(jnp.int32, logits.shape, 1)
    logits = jnp.where(column < experts - 1, logits, MASK_VALUE)
    ex = jnp.exp(logits - jnp.max(logits, axis=1, keepdims=True))
    probs[...] = ex / jnp.sum(ex, axis=1, keepdims=True)
    for start in range(0, 2 * hidden, 256):
        t = pl.ds(start, 256)
        gu[:, t] = jnp.dot(h2[...], w_in[:, t], preferred_element_type=f32)
    for start in range(0, hidden, 128):
        ta, tb = pl.ds(start, 128), pl.ds(hidden + start, 128)
        a, b = gu[:, ta], gu[:, tb]
        sig = jax.nn.sigmoid(a)
        silu = a * sig
        hs[:, ta] = (silu * b).astype(bf16)
        gu[:, ta] = b * (sig * (1.0 + a * (1.0 - sig)))
        gu[:, tb] = silu
    for start in range(0, hidden, 256):
        n = min(256, hidden - start)
        dhs = lax.dot_general(cb[own, :], w_down[pl.ds(start, n), :], NT, preferred_element_type=f32)
        for t in (pl.ds(start, n), pl.ds(hidden + start, n)):
            dgu[:, t] = (dhs * gu[:, t]).astype(bf16)
    for start in range(0, width, 256):
        t = pl.ds(start, 256)
        shared_out[:, t] = jnp.dot(hs[...], w_down[:, t], preferred_element_type=f32)
        grad_h2[:, t] = lax.dot_general(dgu[...], w_in[t, :], NT, preferred_element_type=f32)
    for start in range(0, 2 * hidden, 256):
        t = pl.ds(start, 256)
        grad = lax.dot_general(h2[...], dgu[:, t], TN, preferred_element_type=f32)
        store_grad(grad, t, rows, mine, grads)
    for start in range(0, hidden, 256):
        n = min(256, hidden - start)
        grad = lax.dot_general(cb[own, :], hs[:, pl.ds(start, n)], TN, preferred_element_type=f32)
        store_grad(grad, pl.ds(2 * hidden + start, n), rows, mine, grads)


def shared_expert(core, h2, cb, w_in, w_down, w_router, rows, experts):
    tokens, width = h2.shape
    hidden = w_down.shape[0]
    f32, bf16 = jnp.float32, jnp.bfloat16
    sd = jax.ShapeDtypeStruct
    vmem = pl.BlockSpec(memory_space=pltpu.VMEM)
    grads = [sd((width // 2, 3 * hidden), bf16)] * 2 if rows else [sd((width, 3 * hidden), bf16)]
    outs = [sd((tokens, width), f32), sd((tokens, width), f32), sd((tokens, w_router.shape[1]), f32)] + grads
    return pl.pallas_call(
        lambda *r: shared_kernel(rows, experts, *r),
        in_specs=[pl.BlockSpec(memory_space=pltpu.SMEM)] + [vmem] * 5,
        out_specs=[vmem] * len(outs),
        out_shape=outs,
        scratch_shapes=[pltpu.VMEM((tokens, 2 * hidden), f32), pltpu.VMEM((tokens, hidden), bf16), pltpu.VMEM((tokens, 2 * hidden), bf16)],
        compiler_params=pltpu.CompilerParams(vmem_limit_bytes=48 * 2**20),
        cost_estimate=pl.CostEstimate(flops=0, bytes_accessed=0, transcendentals=0),
        name="shared_expert",
    )(core, h2, cb, w_in, w_down, w_router)


def middle_kernel(experts, length_ref, home_a, home_b, home_c, grad_shared, probs, h2, w_router, x_mid, dout, gain, digits, grad_mid, da, small):
    f32, bf16 = jnp.float32, jnp.bfloat16
    tokens = x_mid.shape[0]
    own, table = pl.ds(0, tokens), pl.ds(tokens, 2 * experts)
    total = lambda r, c: home_a[r, c].astype(f32) + home_b[r, c].astype(f32) + home_c[r, c].astype(f32)
    dots = total(table, own)
    dots = dots[:experts] + dots[experts:]
    grad_probs = jnp.concatenate([dots, jnp.zeros((128 - experts, tokens), f32)], axis=0).T
    p = probs[...]
    low = (p * (grad_probs - jnp.sum(grad_probs * p, axis=1, keepdims=True))).astype(bf16)
    incoming = total(own, slice(None)) + grad_shared[...]
    incoming += lax.dot_general(low, w_router[...], NT, preferred_element_type=f32)
    mid = x_mid[...]
    inverse = lax.rsqrt(jnp.mean(mid * mid, axis=-1, keepdims=True) + NORM_EPS)
    scaled = mid * inverse
    column = lax.broadcasted_iota(jnp.int32, (tokens, 128), 1)
    small[...] = digits[...]
    small[:, pl.ds(0, 128)] += lax.dot_general(h2[...], low, TN, preferred_element_type=f32) + lax.dot_general(
        incoming * scaled, jnp.where(column == experts, 1.0, 0.0), TN,
        precision=lax.Precision.HIGHEST, preferred_element_type=f32,
    )
    inner = incoming * gain[...]
    back = inverse * (inner - scaled * jnp.mean(inner * scaled, axis=-1, keepdims=True))
    grad = dout[...].astype(f32) + back
    grad_mid[...] = grad
    live = lax.broadcasted_iota(jnp.int32, (tokens, 1), 0) < length_ref[0]
    da[...] = jnp.where(live, grad, 0.0).astype(bf16)


def middle_back(lengths, home, grad_shared, probs, h2, w_router, x_mid, dout, gain, digits, experts):
    tokens, width = x_mid.shape
    f32 = jnp.float32
    sd = jax.ShapeDtypeStruct
    vmem = pl.BlockSpec(memory_space=pltpu.VMEM)
    return pl.pallas_call(
        lambda *r: middle_kernel(experts, *r),
        in_specs=[pl.BlockSpec(memory_space=pltpu.SMEM)] + [vmem] * 11,
        out_specs=[vmem] * 3,
        out_shape=[sd((tokens, width), f32), sd((tokens, width), jnp.bfloat16), sd(digits.shape, f32)],
        compiler_params=pltpu.CompilerParams(vmem_limit_bytes=48 * 2**20),
        cost_estimate=pl.CostEstimate(flops=0, bytes_accessed=0, transcendentals=0),
        name="middle_back",
    )(lengths, *home, grad_shared, probs, h2, w_router, x_mid, dout, gain, digits)


def weight_grad_kernel(parts, bit, index_ref, lhs, rhs, keep, away):
    f32, bf16 = jnp.float32, jnp.bfloat16
    grad = lax.dot_general(lhs[0], rhs[0], TN, preferred_element_type=f32)
    mine = ((index_ref[0] >> bit) & 1) == 0
    rows = grad.shape[0] // parts
    at = 0
    for c in range(parts):
        if (c >> bit) & 1:
            continue
        other = c | (1 << bit)
        first = grad[c * rows : (c + 1) * rows]
        second = grad[other * rows : (other + 1) * rows]
        keep[pl.ds(at, rows), :] = jnp.where(mine, first, second).astype(bf16)
        away[pl.ds(at, rows), :] = jnp.where(mine, second, first).astype(bf16)
        at += rows


def weight_grad(index, lhs, rhs, expert, parts, bit):
    _, rows, m = lhs.shape
    n = rhs.shape[2]
    tile = 256
    return pl.pallas_call(
        lambda *r: weight_grad_kernel(parts, bit, *r),
        grid=(n // tile,),
        in_specs=[
            pl.BlockSpec(memory_space=pltpu.SMEM),
            pl.BlockSpec((1, rows, m), lambda i: (expert, 0, 0)),
            pl.BlockSpec((1, rows, tile), lambda i: (expert, 0, i)),
        ],
        out_specs=[pl.BlockSpec((m // 2, tile), lambda i: (0, i))] * 2,
        out_shape=[jax.ShapeDtypeStruct((m // 2, n), jnp.bfloat16)] * 2,
        compiler_params=pltpu.CompilerParams(vmem_limit_bytes=48 * 2**20),
        cost_estimate=pl.CostEstimate(flops=0, bytes_accessed=0, transcendentals=0),
        name="weight_grad",
    )(index, lhs, rhs)


def rope_tables(seq_slots):
    half_dim = HEAD_DIM // 2
    inv_freq = 1.0 / 10000.0 ** (jnp.arange(half_dim, dtype=jnp.float32) * 2.0 / HEAD_DIM)
    angles = jnp.arange(seq_slots, dtype=jnp.float32)[:, None] * inv_freq[None, :]
    cosine, sine = jnp.cos(angles), jnp.sin(angles)
    return jnp.concatenate([cosine, cosine], axis=1), jnp.concatenate([-sine, sine], axis=1)


def assemble_kernel(wide, *refs):
    *pieces, qkv, out = refs
    pair, pairs = 0, out.shape[1] // wide
    for piece, count in zip(pieces, (pairs // 2, pairs // 2, pairs - 2 * (pairs // 2))):
        step = piece.shape[1] // count
        for at in range(count):
            for kind in range(4):
                block = piece[:, at * step + kind * wide : at * step + (kind + 1) * wide]
                if kind < 3:
                    qkv[:, pl.ds((kind * pairs + pair) * wide, wide)] = block
                else:
                    out[:, pl.ds(pair * wide, wide)] = block
            pair += 1


def assemble(pieces, width):
    rows = pieces[0].shape[0]
    vmem = pl.BlockSpec(memory_space=pltpu.VMEM)
    return pl.pallas_call(
        lambda *r: assemble_kernel(2 * HEAD_DIM, *r),
        in_specs=[vmem] * len(pieces),
        out_specs=[vmem] * 2,
        out_shape=[jax.ShapeDtypeStruct((rows, n), jnp.float32) for n in (3 * width, width)],
        cost_estimate=pl.CostEstimate(flops=0, bytes_accessed=0, transcendentals=0),
        name="assemble",
    )(*pieces)


def final_kernel(chosen_ref, *refs):
    *terms, out = refs
    for i in range(len(terms) // 3):
        keep, came, last = (term[...].astype(jnp.float32) for term in terms[3 * i : 3 * i + 3])
        out[i] = keep + came + last


def final_sums(chosen, groups):
    rows, n = groups[0][2].shape
    cut = rows // 4
    half = lambda i: pl.BlockSpec((cut, n), lambda c, chosen, i=i: (chosen[i] * 4 + c, 0))
    row = pl.BlockSpec((cut, n), lambda c, chosen: (c, 0))
    return pl.pallas_call(
        final_kernel,
        grid_spec=pltpu.PrefetchScalarGridSpec(
            num_scalar_prefetch=1,
            grid=(4,),
            in_specs=[spec for i in range(len(groups)) for spec in (half(i), half(i), row)],
            out_specs=pl.BlockSpec((len(groups), cut, n), lambda c, chosen: (0, c, 0)),
        ),
        out_shape=jax.ShapeDtypeStruct((len(groups), rows, n), jnp.float32),
        compiler_params=pltpu.CompilerParams(vmem_limit_bytes=24 * 2**20),
        cost_estimate=pl.CostEstimate(flops=0, bytes_accessed=0, transcendentals=0),
        name="final_sums",
    )(chosen, *[term for group in groups for term in group])


def expert_sums(scatters):
    flat = lambda term: term.reshape(-1, term.shape[-1])
    if True or any(len(scatter.choices[0]) != 1 for scatter in scatters):
        return jnp.stack([scatter.finish() for scatter in scatters])
    chosen = jnp.stack([scatter.choices[0][0][1] for scatter in scatters]).astype(jnp.int32)
    return final_sums(chosen, [[flat(term) for term in scatter.terms] for scatter in scatters])


def swap_cores(values_in):
    owners = lax.axis_size("expert")
    return lax.ppermute(values_in, "expert", [(i, i ^ 1) for i in range(owners)])


def next_chip(values_in):
    owners = lax.axis_size("expert")
    return lax.ppermute(values_in, "expert", [(i, (i + 2) % owners) for i in range(owners)])


def axis_bits(name):
    return [(name, bit) for bit in range(lax.axis_size(name).bit_length() - 1)]


def row_bits():
    return axis_bits("dp")[::-1] + axis_bits("expert")[::-1]


def sum_terms(parts):
    summed = parts[0].astype(jnp.float32)
    for term in parts[1:]:
        summed = summed + term.astype(jnp.float32)
    return summed


def after(values_in, *earlier):
    return lax.optimization_barrier((values_in, earlier))[0]


def picked(term, choices):
    for dim, index in choices:
        term = lax.dynamic_index_in_dim(term, index, dim, keepdims=False)
    return term


class Scatter:
    def __init__(self, terms, open_bits, order):
        self.terms, self.choices = list(terms), [[] for _ in terms]
        self.open_bits, self.order = list(open_bits), list(order)

    def advance(self, *earlier):
        name, bit = self.order.pop(0)
        dim = self.open_bits.index((name, bit))
        mine = (lax.axis_index(name) >> bit) & 1
        terms = after(self.terms, *earlier) if earlier else self.terms
        away = sum_terms(
            [picked(term, made + [(dim, 1 - mine)]) for term, made in zip(terms, self.choices)]
        ).astype(terms[0].dtype)
        came = lax.ppermute(
            away, name, [(i, i ^ (1 << bit)) for i in range(lax.axis_size(name))]
        )
        self.choices = [made + [(dim, mine)] for made in self.choices] + [[]]
        self.terms.append(came)
        self.open_bits.pop(dim)
        return away

    def finish(self):
        while self.order:
            self.advance()
        return sum_terms([picked(term, made) for term, made in zip(self.terms, self.choices)])


def split_rows(part, bits):
    rows = part.shape[0] >> len(bits)
    return part.reshape((2,) * len(bits) + (rows, part.shape[1]))


def scatter_orders():
    core, *line = axis_bits("expert")
    plane = axis_bits("dp")
    return ([core] + plane + line, [core] + plane[::-1] + line, [core] + plane + line)


def per_device(
    layer_input,
    lengths,
    expert_ids,
    norm1,
    w_qkv,
    w_out,
    norm2,
    w_router,
    w_shared_in,
    w_shared_down,
    w_expert_in,
    w_expert_down,
    dout,
):
    seq_slots, width = layer_input.shape
    top_k = expert_ids.shape[1]
    experts = w_router.shape[1]
    local_experts = w_expert_in.shape[0]
    hidden_units = w_shared_down.shape[0]
    capacity = (seq_slots * top_k // (experts - 1) // 8 + 1) * 8
    live_col = (jnp.arange(seq_slots, dtype=jnp.int32) < lengths[0]).astype(jnp.float32)[:, None]
    cosine, sine = rope_tables(seq_slots)

    bits = row_bits()
    rows = width >> len(bits)
    rows = rows if rows % 8 == 0 else 0
    core = (lax.axis_index("expert") & 1).astype(jnp.int32)[None]
    orders = scatter_orders()
    chips = experts // local_experts // 2
    first_expert = (lax.axis_index("expert") * local_experts).astype(jnp.int32)[None]
    router_t = w_router.T

    def start_scatter(grads, order):
        if rows:
            terms = [split_rows(grads[0], bits[:-1]), split_rows(swap_cores(grads[1]), bits[:-1])]
            return Scatter(terms, bits[:-1], order[1:])
        return Scatter([split_rows(grads[0], bits)], bits, order)

    def run_step(step, h2_pair, grad_pair, kept, *earlier):
        sums, kept = expert_step(
            first_expert, after(h2_pair[0], *earlier), h2_pair[1], grad_pair[0], grad_pair[1],
            router_t, w_expert_in, w_expert_down, step, chips, capacity, kept,
        )
        parts.append(sums)
        return kept, sums[0]

    parts = []
    router_wide = jnp.pad(w_router, ((0, 0), (0, 128 - experts)))
    grad_table = token_rows(lengths, expert_ids, dout, experts)
    grad_here = (grad_table, swap_cores(grad_table))
    grad_next = next_chip(grad_table)
    counts_here = jnp.sum((grad_table[seq_slots:, :seq_slots] >= 0).astype(jnp.int32), axis=1)
    places = jnp.minimum(jnp.arange(width >> len(bits), dtype=jnp.int32), 30)
    digits = ((counts_here[None, :] >> places[:, None]) & 1).astype(jnp.float32)
    small_columns = -(-(2 * experts + 2) // 128) * 128
    digits = jnp.pad(
        jnp.tile(digits, (1 << len(bits), 1)),
        ((0, 0), (experts + 2, small_columns - 2 * experts - 2)),
    )
    h1_low, queries, keys_in, values_in, attended_low, log_norm, x_mid, h2_low = attention_forward(
        lengths, after(layer_input, grad_table), norm1[None, :], w_qkv, cosine, sine, w_out,
        norm2[None, :],
    )
    h2_here = (h2_low, swap_cores(h2_low))
    h2_next = next_chip(h2_low)
    grad_next = after(grad_next, h2_low)
    grad_other = swap_cores(grad_next)
    grad_ahead = next_chip(grad_next)
    kept, done = run_step(0, h2_here, grad_here, None, grad_next)
    shared_out, grad_shared, router_probs, *shared_grads = shared_expert(
        core, after(h2_low, done), grad_table, w_shared_in, w_shared_down, router_wide, rows, experts
    )
    fence = shared_out
    shared_away = []
    swapped = []
    shared_scatter = None
    travelling = None
    for step in range(1, chips):
        h2_next, grad_next = after(h2_next, fence), after(grad_next, fence)
        pair_h2 = (h2_next, swap_cores(h2_next))
        pair_grad = (grad_next, grad_other)
        if shared_scatter is None:
            ready = (fence, grad_ahead, pair_h2[1], grad_other)
            shared_scatter = start_scatter(after(shared_grads, *ready), orders[0])
            swapped.append(swap_cores(after(parts[0][3], *ready)))
        earlier = [] if travelling is None else [travelling]
        earlier += shared_away
        if step + 1 < chips:
            h2_next = next_chip(h2_next)
            grad_next = after(grad_ahead, fence)
            grad_other = swap_cores(grad_next)
            if step + 2 < chips:
                grad_ahead = next_chip(grad_next)
        kept, fence = run_step(step, pair_h2, pair_grad, kept, *earlier)
        mine, theirs = parts[step][:2]
        if step + 1 < chips:
            theirs = after(theirs, h2_next, grad_ahead)
        theirs = after(theirs, *swapped)
        if step == 2:
            first_routed = parts[1][2].astype(jnp.float32) + swapped[1].astype(jnp.float32)
            first_routed = first_routed.astype(jnp.bfloat16)
            theirs = after(theirs, first_routed)
        swapped.append(swap_cores(after(parts[step][3], theirs)))
        if shared_away:
            theirs = after(theirs, shared_scatter.terms[-1])
        if shared_scatter.order[0][0] == "dp":
            shared_away = [shared_scatter.advance(fence)]
            theirs = after(theirs, *shared_away)
        if travelling is None:
            total = mine.astype(jnp.float32) + swap_cores(theirs).astype(jnp.float32)
        else:
            came = next_chip(travelling)
            total = (
                mine.astype(jnp.float32)
                + swap_cores(after(theirs, came)).astype(jnp.float32)
                + came.astype(jnp.float32)
            )
        travelling = total.astype(mine.dtype)

    home_hop = next_chip(travelling)
    rows_held, grad_result, expert_hidden, grad_expert_gu = kept

    plane = axis_bits("dp")
    plane_index = lax.axis_index("dp").astype(jnp.int32)[None]

    def expert_grads(lhs, rhs, expert):
        order = plane if expert % 2 == 0 else plane[::-1]
        return order, weight_grad(
            plane_index, lhs, rhs, expert, 1 << len(plane), order[0][1]
        )

    def plane_scatter(order, grads, *earlier):
        name, bit = order[0]
        keep, away = after(grads, *earlier) if earlier else grads
        came = lax.ppermute(
            away, name, [(i, i ^ (1 << bit)) for i in range(lax.axis_size(name))]
        )
        open_bits = [place for place in plane[::-1] if place != order[0]]
        terms = [split_rows(piece, open_bits) for piece in (keep, came)]
        return Scatter(terms, open_bits, order[1:])

    fence = [travelling, shared_scatter.terms[-1]]
    down_parts, in_parts = [], []
    for i in range(local_experts):
        down_parts.append(expert_grads(after(expert_hidden, *fence), grad_result, i))
        fence = down_parts[-1][1]
    down_scatters = [plane_scatter(*part) for part in down_parts]
    for i in range(local_experts):
        in_parts.append(expert_grads(after(rows_held, *fence), grad_expert_gu, i))
        fence = in_parts[-1][1]

    mine, theirs = parts[0][:2]
    own_home = (mine, swap_cores(after(theirs, travelling)))
    out_order = list(range(1, chips)) + [0]

    def add_routed(index, came, *earlier):
        mine, theirs = after((parts[out_order[index]][2], swapped[out_order[index]]), *earlier)
        total = mine.astype(jnp.float32) + theirs.astype(jnp.float32)
        return total if came is None else total + came.astype(jnp.float32)

    routed = first_routed if chips > 2 else add_routed(0, None, travelling).astype(jnp.bfloat16)
    landed = list(fence) + [home_hop, own_home[1], swapped[-1], routed]
    landed += [scatter.terms[-1] for scatter in down_scatters]
    in_scatters = [plane_scatter(*part, *landed) for part in in_parts]
    out_hop = next_chip(after(routed, *landed))
    fence = landed
    for scatter in down_scatters:
        fence = [scatter.advance(*fence)]
    home = after((*own_home, home_hop), *fence)
    grad_mid, grad_attn_branch, small = middle_back(
        lengths, home, grad_shared, router_probs, h2_low, router_wide, x_mid, dout, norm2[None, :],
        digits, experts,
    )

    pairs = width // (2 * HEAD_DIM)
    half = (pairs - 1) // 2
    cuts = (0, half, 2 * half, pairs)
    running = None
    columns = []
    fence = [grad_attn_branch]
    for index, (first, last) in enumerate(zip(cuts[:-1], cuts[1:])):
        tail = None
        if last == pairs:
            tail = (experts, (layer_input, norm1[None, :], grad_mid, small))
        *grads, running = attention_backward(
            lengths, core, after(grad_attn_branch, *fence), w_out, queries, keys_in, values_in,
            log_norm, cosine, sine, h1_low, attended_low, w_qkv, running, first, last - first, rows,
            tail,
        )
        fence = [running]
        columns.append(grads)
        if index == 0:
            routed = add_routed(1, out_hop, running).astype(jnp.bfloat16)
            out_hop = next_chip(routed)
            fence.append(routed)
    grad_input = running
    landed = [running, out_hop]
    landed += [scatter.terms[-1] for scatter in in_scatters + down_scatters]
    scatters = []
    fence = landed
    for grads, order in zip(columns, orders):
        scatters.append(start_scatter(after(grads, *landed, *fence), order))
    hops = 2
    first_cols, second_cols, third_cols = scatters
    plan = [first_cols, second_cols, None, third_cols, shared_scatter, first_cols, second_cols, third_cols, shared_scatter, None, first_cols, second_cols, third_cols, in_scatters[0], in_scatters[1], first_cols, second_cols, third_cols]
    for position, scatter in enumerate(plan):
        if position == 5:
            for held in down_scatters:
                held.terms = after(held.terms, *fence)
            expert_down_sum = expert_sums(down_scatters)
            fence = fence + [expert_down_sum]
        if scatter is not None:
            if scatter.order:
                fence = [scatter.advance(*fence)]
        elif hops < chips:
            routed = add_routed(hops, out_hop, *fence)
            hops += 1
            if hops < chips:
                out_hop = next_chip(routed.astype(jnp.bfloat16))
            fence = [routed]
    for hops in range(hops, chips):
        routed = add_routed(hops, out_hop, *fence)
        out_hop = next_chip(routed.astype(jnp.bfloat16))
    for scatter in in_scatters + [shared_scatter]:
        scatter.terms = after(scatter.terms, *fence)
    result = (x_mid + live_col * (shared_out + routed)).astype(jnp.bfloat16)
    shared_sum = shared_scatter.finish()
    expert_in_sum = expert_sums(in_scatters)
    pieces = [scatter.finish() for scatter in scatters]
    qkv_sum, out_sum = assemble(pieces, width)
    small_sum = pieces[-1][:, 8 * HEAD_DIM :]
    counts = jnp.sum(
        small_sum[:, experts + 2 : 2 * experts + 2] * (1 << places).astype(jnp.float32)[:, None],
        axis=0,
    )
    return (
        result,
        grad_input,
        small_sum[:, experts + 1],
        qkv_sum,
        out_sum,
        small_sum[:, experts],
        small_sum[:, :experts],
        shared_sum[:, : 2 * hidden_units],
        shared_sum[:, 2 * hidden_units :].T,
        expert_in_sum,
        expert_down_sum,
        counts.astype(jnp.int32),
    )


def solution(mesh):
    return jax.shard_map(
        per_device,
        mesh=mesh,
        in_specs=(
            P(("dp", "expert"), None),
            P(("dp", "expert")),
            P(("dp", "expert"), None),
            P(),
            P(),
            P(),
            P(),
            P(),
            P(),
            P(),
            P("expert", None, None),
            P("expert", None, None),
            P(("dp", "expert"), None),
        ),
        out_specs=(
            P(("dp", "expert"), None),
            P(("dp", "expert"), None),
            P(("dp", "expert")),
            P(("dp", "expert"), None),
            P(("dp", "expert"), None),
            P(("dp", "expert")),
            P(("dp", "expert"), None),
            P(("dp", "expert"), None),
            P(None, ("dp", "expert")),
            P("expert", "dp", None),
            P("expert", "dp", None),
            P(),
        ),
        check_vma=False,
    )
```

```python
import jax
import jax.numpy as jnp
from jax import lax
from jax.experimental import pallas as pl
from jax.experimental.pallas import tpu as pltpu
from jax.sharding import PartitionSpec as P

HEAD_DIM = 128
NORM_EPS = 1e-06
MASK_VALUE = -1e30
NT = (((1,), (1,)), ((), ()))
TN = (((0,), (0,)), ((), ()))

def turn(values_in, cosine, signed_sine):
    return values_in * cosine + pltpu.roll(values_in, HEAD_DIM // 2, 1) * signed_sine

def block_scores(q, k, start, seq_length):
    s = lax.dot_general(q, k, NT, preferred_element_type=jnp.float32) * HEAD_DIM ** (-0.5)
    query_pos = start + lax.broadcasted_iota(jnp.int32, s.shape, 0)
    key_pos = lax.broadcasted_iota(jnp.int32, s.shape, 1)
    return jnp.where((key_pos <= query_pos) & (key_pos < seq_length), s, MASK_VALUE)

def attention_kernel(length_ref, x, norm1, wq, wk, wv, cosine, sine, w_out, norm2, h1, q_o, k_o, v_o, att, lse, x_mid, h2):
    f32, bf16 = jnp.float32, jnp.bfloat16
    p = pl.program_id(0)
    tokens = x.shape[0]
    seq_length = length_ref[0]
    span = min(256, tokens)

    @pl.when(p == 0)
    def _():
        xf = x[...].astype(f32)
        inverse = lax.rsqrt(jnp.mean(xf * xf, axis=-1, keepdims=True) + NORM_EPS)
        h1[...] = (xf * inverse * norm1[...]).astype(bf16)
        lse[...] = jnp.zeros_like(lse)

    for w, o in ((wq, q_o), (wk, k_o), (wv, v_o)):
        full = jnp.dot(h1[...], w[...], preferred_element_type=f32)
        for j in (0, 1):
            part = full[:, j * HEAD_DIM:(j + 1) * HEAD_DIM]
            if w is not wv:
                part = turn(part, cosine[...], sine[...])
            o[:, pl.ds(j * HEAD_DIM, HEAD_DIM)] = part.astype(bf16)
    lane = lax.broadcasted_iota(jnp.int32, (span, lse.shape[1]), 1)
    for j in (0, 1):
        cols = pl.ds(j * HEAD_DIM, HEAD_DIM)
        for start in range(0, tokens, span):
            rows = pl.ds(start, span)
            seen = pl.ds(0, start + span)
            s = block_scores(q_o[rows, cols], k_o[seen, cols], start, seq_length)
            high = jnp.max(s, axis=-1, keepdims=True)
            ex = jnp.exp(s - high)
            total = jnp.sum(ex, axis=-1, keepdims=True)
            low = (ex / total).astype(bf16)
            out = jnp.dot(low, v_o[seen, cols], preferred_element_type=f32)
            att[rows, pl.ds(pl.multiple_of(p * 2 * HEAD_DIM + j * HEAD_DIM, HEAD_DIM), HEAD_DIM)] = out.astype(bf16)
            lse[rows, :] = jnp.where(lane == 2 * p + j, high + jnp.log(total), lse[rows, :])

    @pl.when(p == pl.num_programs(0) - 1)
    def _():
        branch = jnp.dot(att[...], w_out[...], preferred_element_type=f32)
        live = lax.broadcasted_iota(jnp.int32, (tokens, 1), 0) < seq_length
        mid = x[...].astype(f32) + jnp.where(live, branch, 0.0)
        x_mid[...] = mid
        inverse = lax.rsqrt(jnp.mean(mid * mid, axis=-1, keepdims=True) + NORM_EPS)
        h2[...] = (mid * inverse * norm2[...]).astype(bf16)

def whole(a):
    return pl.BlockSpec(a.shape, lambda p: (0,) * len(a.shape), pipeline_mode=pl.Buffered(1))

def attention_forward(lengths, x, norm1, w_qkv, cosine, sine, w_out, norm2):
    tokens, width = x.shape
    pairs = width // (2 * HEAD_DIM)
    f32, bf16 = jnp.float32, jnp.bfloat16
    wide = 2 * HEAD_DIM
    col = lambda k: pl.BlockSpec((width, wide), lambda p, k=k: (0, k * pairs + p))
    head = pl.BlockSpec((tokens, wide), lambda p: (0, p))
    full = pl.BlockSpec((tokens, width), lambda p: (0, 0))
    sd = jax.ShapeDtypeStruct
    return pl.pallas_call(
        attention_kernel, grid=(pairs,),
        in_specs=[pl.BlockSpec(memory_space=pltpu.SMEM), whole(x), whole(norm1), col(0), col(1), col(2), whole(cosine), whole(sine), whole(w_out), whole(norm2)],
        out_specs=[full, head, head, head, full, pl.BlockSpec((tokens, 128), lambda p: (0, 0)), full, full],
        out_shape=[pltpu.HBM((tokens, width), bf16)] * 5 + [pltpu.HBM((tokens, 128), f32), pltpu.HBM((tokens, width), f32), pltpu.HBM((tokens, width), bf16)],
        compiler_params=pltpu.CompilerParams(vmem_limit_bytes=48 * 2**20),
        cost_estimate=pl.CostEstimate(flops=0, bytes_accessed=0, transcendentals=0),
        name="attention_forward",
    )(lengths, x, norm1, w_qkv, w_qkv, w_qkv, cosine, sine, w_out, norm2)

def attention_back_kernel(rows, extra, carried, length_ref, core_ref, da, w_out, q, k, v, lse, cosine, sine, h1, att, wq, wk, wv, *rest):
    f32, bf16 = jnp.float32, jnp.bfloat16
    dh1_in = None
    if carried:
        dh1_in, *rest = rest
    if extra:
        x, gain, grad_mid, small, *rest = rest
    *grads, dh1, dk_s, dv_s, dproj = rest
    p = pl.program_id(0)
    pair = length_ref[1] + p
    tokens, width = da.shape
    seq_length = length_ref[0]
    span = min(256, tokens)
    scale = HEAD_DIM ** (-0.5)
    mine = core_ref[0] == 0
    wide = 2 * HEAD_DIM
    do_full = lax.dot_general(da[...], w_out[...], NT, preferred_element_type=f32).astype(bf16)
    lane = lax.broadcasted_iota(jnp.int32, (span, lse.shape[1]), 1)
    back_sine = -sine[...]
    for j in (0, 1):
        cols = pl.ds(j * HEAD_DIM, HEAD_DIM)
        do_head = do_full[:, j * HEAD_DIM : (j + 1) * HEAD_DIM]
        for start in range(tokens - span, -1, -span):
            r = pl.ds(start, span)
            seen = pl.ds(0, start + span)
            s = block_scores(q[r, cols], k[seen, cols], start, seq_length)
            norm = jnp.sum(jnp.where(lane == 2 * pair + j, lse[r, :], 0.0), axis=1, keepdims=True)
            probs = jnp.exp(s - norm)
            do = do_head[start : start + span]
            dp = lax.dot_general(do, v[seen, cols], NT, preferred_element_type=f32)
            row = jnp.sum(dp * probs, axis=1, keepdims=True)
            ds = (probs * (dp - row)).astype(bf16)
            dq = jnp.dot(ds, k[seen, cols], preferred_element_type=f32) * scale
            dproj[r, pl.ds(j * HEAD_DIM, HEAD_DIM)] = turn(
                dq, cosine[r, :], back_sine[start : start + span]
            ).astype(bf16)
            dk = lax.dot_general(ds, q[r, cols], TN, preferred_element_type=f32) * scale
            dv = lax.dot_general(probs.astype(bf16), do, TN, preferred_element_type=f32)
            if start == tokens - span:
                dk_s[seen, :] = dk
                dv_s[seen, :] = dv
            else:
                dk_s[seen, :] += dk
                dv_s[seen, :] += dv
        dproj[:, pl.ds(wide + j * HEAD_DIM, HEAD_DIM)] = turn(dk_s[...], cosine[...], back_sine).astype(bf16)
        dproj[:, pl.ds(2 * wide + j * HEAD_DIM, HEAD_DIM)] = dv_s[...].astype(bf16)
    total = jnp.where(p == 0, dh1_in[...] if carried else 0.0, dh1[...])
    for i, w in enumerate((wq, wk, wv)):
        part = dproj[:, pl.ds(i * wide, wide)]
        grad = lax.dot_general(h1[...], part, TN, preferred_element_type=f32)
        store_grad(grad, pl.ds(i * wide, wide), rows, mine, grads)
        total += lax.dot_general(part, w[...], NT, preferred_element_type=f32)
    part = da[:, pl.ds(pl.multiple_of(pair * wide, wide), wide)]
    grad = lax.dot_general(att[...], part, TN, preferred_element_type=f32)
    store_grad(grad, pl.ds(3 * wide, wide), rows, mine, grads)
    dh1[...] = total
    if not extra:
        return

    @pl.when(p < pl.num_programs(0) - 1)
    def _():
        store_grad(jnp.zeros(small.shape, f32), pl.ds(4 * wide, small.shape[1]), rows, mine, grads)

    @pl.when(p == pl.num_programs(0) - 1)
    def _():
        full = x[...].astype(f32)
        inverse = lax.rsqrt(jnp.mean(full * full, axis=-1, keepdims=True) + NORM_EPS)
        scaled = full * inverse
        inner = total * gain[...]
        dh1[...] = grad_mid[...] + inverse * (
            inner - scaled * jnp.mean(inner * scaled, axis=-1, keepdims=True)
        )
        column = lax.broadcasted_iota(jnp.int32, (tokens, small.shape[1]), 1)
        grad = small[...] + lax.dot_general(
            total * scaled, jnp.where(column == extra + 1, 1.0, 0.0), TN,
            precision=lax.Precision.HIGHEST, preferred_element_type=f32,
        )
        store_grad(grad, pl.ds(4 * wide, small.shape[1]), rows, mine, grads)


def attention_backward(lengths, core, da, w_out, q, k, v, lse, cosine, sine, h1, att, w_qkv, dh1_in, first, count, rows, tail):
    tokens, width = da.shape
    pairs = width // (2 * HEAD_DIM)
    wide = 2 * HEAD_DIM
    f32, bf16 = jnp.float32, jnp.bfloat16
    col = lambda k: pl.BlockSpec((width, wide), lambda p, k=k: (0, k * pairs + first + p))
    head = pl.BlockSpec((tokens, wide), lambda p: (0, first + p))
    sd = jax.ShapeDtypeStruct
    smem = pl.BlockSpec(memory_space=pltpu.SMEM)
    n = width // 2 if rows else width
    extra, tail_args = tail if tail else (0, ())
    columns = 4 * wide + (tail_args[-1].shape[1] if extra else 0)
    grads = [sd((n, count * columns), bf16)] * (2 if rows else 1)
    carried = dh1_in is not None
    tail_args = ((dh1_in,) if carried else ()) + tuple(tail_args)
    whole_args = (da, lse, cosine, sine, h1, att) + tail_args
    spec = {id(a): whole(a) for a in whole_args}
    *held, h1_held, att_held = (
        pltpu.with_memory_space_constraint(a, pltpu.HBM) for a in (q, k, v, h1, att)
    )
    return pl.pallas_call(
        lambda *r: attention_back_kernel(rows, extra, carried, *r),
        grid=(count,),
        in_specs=[smem, smem, spec[id(da)], pl.BlockSpec((wide, width), lambda p: (first + p, 0)), head, head, head]
        + [spec[id(a)] for a in (lse, cosine, sine, h1, att)]
        + [col(0), col(1), col(2)]
        + [spec[id(a)] for a in tail_args],
        out_specs=[pl.BlockSpec((n, columns), lambda p: (0, p))] * len(grads)
        + [pl.BlockSpec((tokens, width), lambda p: (0, 0))],
        out_shape=grads + [sd((tokens, width), f32)],
        scratch_shapes=[pltpu.VMEM((tokens, HEAD_DIM), f32), pltpu.VMEM((tokens, HEAD_DIM), f32), pltpu.VMEM((tokens, 3 * wide), bf16)],
        compiler_params=pltpu.CompilerParams(vmem_limit_bytes=48 * 2**20),
        cost_estimate=pl.CostEstimate(flops=0, bytes_accessed=0, transcendentals=0),
        name="attention_backward",
    )(
        jnp.concatenate([lengths, jnp.full((1,), first, jnp.int32)]), core, da, w_out, *held,
        lse, cosine, sine, h1_held, att_held, w_qkv, w_qkv, w_qkv, *tail_args,
    )


def expert_kernel(cap, tokens, hidden, unrolled, *refs):
    (first_ref, h2a, h2b, cba, cbb, wr, w_in, w_down) = refs[:8]
    (dra, drb, outa, outb, rows_o, dy_o, act_o, dgu_o, gu, cbrow, oh, gy, drs, probs, dots) = refs[-15:]
    f32, bf16 = jnp.float32, jnp.bfloat16
    e = pl.program_id(0)
    experts = wr.shape[0]
    width = wr.shape[1]
    mine = first_ref[0] + e
    table_rows = probs.shape[1]

    @pl.when(e == 0)
    def _():
        for src, h2 in ((0, h2a), (1, h2b)):
            logits = lax.dot_general(wr[...], h2[...], (((1,), (1,)), ((), ())), preferred_element_type=f32)
            row = lax.broadcasted_iota(jnp.int32, logits.shape, 0)
            logits = jnp.where(row < experts - 1, logits, MASK_VALUE)
            ex = jnp.exp(logits - jnp.max(logits, axis=0, keepdims=True))
            probs[src] = ex / jnp.sum(ex, axis=0, keepdims=True)
            dots[src] = jnp.zeros_like(probs[src])

    gates = []
    masks = []
    for src, h2, cb in ((0, h2a, cba), (1, h2b, cbb)):
        row_id = lax.broadcasted_iota(jnp.int32, (table_rows, tokens), 0)
        table = cb[pl.ds(tokens, table_rows), pl.ds(0, tokens)].astype(f32)
        rank = jnp.sum(jnp.where(row_id == mine, table, 0.0), axis=0, keepdims=True)
        prob = jnp.sum(jnp.where(row_id == mine, probs[src], 0.0), axis=0, keepdims=True)
        hit = lax.broadcasted_iota(jnp.int32, (cap, tokens), 0).astype(f32) == rank
        masks.append(hit)
        gates.append(jnp.sum(jnp.where(hit, prob, 0.0), axis=1, keepdims=True))
        onehot = jnp.where(hit, 1.0, 0.0).astype(bf16)
        oh[src, pl.ds(e * cap, cap), :] = onehot
        half = pl.ds(src * cap, cap)
        @pl.loop(0, width // 256, unroll=unrolled)
        def _(i):
            t = pl.ds(pl.multiple_of(i * 256, 256), 256)
            rows_o[0, half, t] = jnp.dot(onehot, h2[:, t], preferred_element_type=f32).astype(bf16)
            cbrow[half, t] = jnp.dot(onehot, cb[pl.ds(0, tokens), t], preferred_element_type=f32).astype(bf16)
    gate = jnp.concatenate(gates, axis=0)

    @pl.loop(0, 2 * hidden // 256, unroll=unrolled)
    def _(i):
        t = pl.ds(pl.multiple_of(i * 256, 256), 256)
        gu[:, t] = jnp.dot(rows_o[0], w_in[0, :, t], preferred_element_type=f32)

    @pl.loop(0, hidden // 128, unroll=unrolled)
    def _(i):
        ta = pl.ds(pl.multiple_of(i * 128, 128), 128)
        tb = pl.ds(pl.multiple_of(hidden + i * 128, 128), 128)
        a = gu[:, ta]
        b = gu[:, tb]
        sig = jax.nn.sigmoid(a)
        silu = a * sig
        act_o[0, :, ta] = (silu * b).astype(bf16)
        gu[:, ta] = b * (sig * (1.0 + a * (1.0 - sig)))
        gu[:, tb] = silu

    def down(i, dot):
        t = pl.ds(pl.multiple_of(i * 256, 256), 256)
        y = jnp.dot(act_o[0], w_down[0, :, t], preferred_element_type=f32).astype(bf16).astype(f32)
        c = cbrow[:, t].astype(f32)
        gyt = (gate * y).astype(bf16)
        for src in (0, 1):
            gy[src, pl.ds(e * cap, cap), t] = gyt[src * cap:(src + 1) * cap]
        dy_o[0, :, t] = (gate * c).astype(bf16)
        return dot + jnp.sum(y * c, axis=1, keepdims=True)
    dot = lax.fori_loop(0, width // 256, down, jnp.zeros((2 * cap, 1), f32), unroll=unrolled)
    for src in (0, 1):
        back = jnp.sum(jnp.where(masks[src], dot[src * cap:(src + 1) * cap], 0.0), axis=0, keepdims=True)
        row_id = lax.broadcasted_iota(jnp.int32, (table_rows, tokens), 0)
        dots[src] += jnp.where(row_id == mine, back, 0.0)

    for start in range(0, hidden, 256):
        n = min(256, hidden - start)
        dact = lax.dot_general(dy_o[0], w_down[0, pl.ds(start, n), :], (((1,), (1,)), ((), ())), preferred_element_type=f32)
        dgu_o[0, :, pl.ds(start, n)] = (dact * gu[:, pl.ds(start, n)]).astype(bf16)
        dgu_o[0, :, pl.ds(hidden + start, n)] = (dact * gu[:, pl.ds(hidden + start, n)]).astype(bf16)

    @pl.loop(0, width // 256, unroll=unrolled)
    def _(i):
        t = pl.ds(pl.multiple_of(i * 256, 256), 256)
        dr = lax.dot_general(dgu_o[0], w_in[0, t, :], (((1,), (1,)), ((), ())), preferred_element_type=f32).astype(bf16)
        for src in (0, 1):
            drs[src, pl.ds(e * cap, cap), t] = dr[src * cap:(src + 1) * cap]

    @pl.when(e == pl.num_programs(0) - 1)
    def _():
        for src, dro, outo in ((0, dra, outa), (1, drb, outb)):
            @pl.loop(0, width // 256, unroll=unrolled)
            def _(i):
                t = pl.ds(pl.multiple_of(i * 256, 256), 256)
                dims = (((0,), (0,)), ((), ()))
                outo[:, t] = lax.dot_general(oh[src], gy[src, :, t], dims, preferred_element_type=f32).astype(bf16)
                dro[pl.ds(0, tokens), t] = lax.dot_general(oh[src], drs[src, :, t], dims, preferred_element_type=f32).astype(bf16)
            hi = dots[src].astype(bf16)
            lo = (dots[src] - hi.astype(f32)).astype(bf16)
            pad = jnp.zeros((2 * table_rows, width - tokens), bf16)
            dro[pl.ds(tokens, table_rows), pl.ds(0, tokens)] = hi
            dro[pl.ds(tokens + table_rows, table_rows), pl.ds(0, tokens)] = lo
            dro[pl.ds(tokens, 2 * table_rows), pl.ds(tokens, width - tokens)] = pad

def expert_step(first, h2a, h2b, cba, cbb, wr, w_in, w_down, step, steps, cap, kept):
    tokens, width = h2a.shape
    local, _, hidden2 = w_in.shape
    hidden = hidden2 // 2
    table_rows = cba.shape[0] - tokens
    bf16, f32 = jnp.bfloat16, jnp.float32
    whole = lambda a: pl.BlockSpec(a.shape, lambda e: (0,) * a.ndim, pipeline_mode=pl.Buffered(1))
    ins = [pl.BlockSpec(memory_space=pltpu.SMEM)] + [whole(a) for a in (h2a, h2b, cba, cbb, wr)]
    ins += [pl.BlockSpec((1,) + w_in.shape[1:], lambda e: (e, 0, 0)), pl.BlockSpec((1,) + w_down.shape[1:], lambda e: (e, 0, 0))]
    kept_shapes = [jax.ShapeDtypeStruct((local, steps * 2 * cap, n), bf16) for n in (width, width, hidden, 2 * hidden)]
    sums = [jax.ShapeDtypeStruct((tokens + 2 * table_rows, width), bf16)] * 2 + [jax.ShapeDtypeStruct((tokens, width), bf16)] * 2
    args = [first, h2a, h2b, cba, cbb, wr, w_in, w_down]
    alias = {}
    if kept is not None:
        ins += [pl.BlockSpec(memory_space=pl.ANY)] * 4
        alias = {len(args) + i: 4 + i for i in range(4)}
        args += list(kept)
    outs = [pl.BlockSpec(s.shape, lambda e: (0, 0), pipeline_mode=pl.Buffered(1)) for s in sums]
    outs += [pl.BlockSpec((1, 2 * cap, s.shape[2]), lambda e: (e, step, 0)) for s in kept_shapes]
    rows = 2 * cap
    flops = 2 * local * rows * (2 * (3 * width * hidden) + 4 * tokens * width)
    res = pl.pallas_call(
        lambda *r: expert_kernel(cap, tokens, hidden, step in (0, steps - 1), *r),
        grid=(local,),
        in_specs=ins, out_specs=outs, out_shape=[pltpu.HBM(x.shape, x.dtype) for x in sums + kept_shapes],
        scratch_shapes=[pltpu.VMEM((rows, 2 * hidden), f32), pltpu.VMEM((rows, width), bf16), pltpu.VMEM((2, local * cap, tokens), bf16),
                        pltpu.VMEM((2, local * cap, width), bf16), pltpu.VMEM((2, local * cap, width), bf16),
                        pltpu.VMEM((2, table_rows, tokens), f32), pltpu.VMEM((2, table_rows, tokens), f32)],
        input_output_aliases=alias,
        compiler_params=pltpu.CompilerParams(vmem_limit_bytes=50 * 2**20),
        cost_estimate=pl.CostEstimate(flops=0, bytes_accessed=0, transcendentals=0),
        name="expert_step",
    )(*args)
    return res[:4], res[4:]


def token_kernel(length_ref, ids, dout, rows_o):
    f32, bf16 = jnp.float32, jnp.bfloat16
    tokens = dout.shape[0]
    table_rows = rows_o.shape[0] - tokens
    live = lax.broadcasted_iota(jnp.int32, (tokens, 1), 0) < length_ref[0]
    rows_o[pl.ds(0, tokens), :] = jnp.where(live, dout[...].astype(f32), 0.0).astype(bf16)
    lane = lax.broadcasted_iota(jnp.int32, (tokens, 128), 1)
    picked = jnp.zeros((tokens, 128), f32)
    for k in range(ids.shape[1]):
        picked = jnp.where(lane == ids[:, k:k + 1], 1.0, picked)
    picked = jnp.where(live, picked, 0.0).astype(bf16)
    earlier = lax.broadcasted_iota(jnp.int32, (tokens, tokens), 0)
    later = lax.broadcasted_iota(jnp.int32, (tokens, tokens), 1)
    before = jnp.where(earlier < later, 1.0, 0.0).astype(bf16)
    same = jnp.where(earlier == later, 1.0, 0.0).astype(bf16)
    rank = lax.dot_general(picked, before, TN, preferred_element_type=f32)
    hit = lax.dot_general(picked, same, TN, preferred_element_type=f32)
    table = jnp.where(hit > 0.5, rank, -1.0)[:table_rows].astype(bf16)
    rows_o[pl.ds(tokens, table_rows), pl.ds(0, tokens)] = table
    rows_o[pl.ds(tokens, table_rows), pl.ds(tokens, dout.shape[1] - tokens)] = jnp.zeros(
        (table_rows, dout.shape[1] - tokens), bf16
    )


def token_rows(lengths, expert_ids, dout, experts):
    return pl.pallas_call(
        token_kernel,
        in_specs=[
            pl.BlockSpec(memory_space=pltpu.SMEM),
            pl.BlockSpec(memory_space=pltpu.VMEM),
            pl.BlockSpec(memory_space=pltpu.VMEM),
        ],
        out_specs=pl.BlockSpec(memory_space=pltpu.VMEM),
        out_shape=jax.ShapeDtypeStruct((dout.shape[0] + experts, dout.shape[1]), jnp.bfloat16),
        cost_estimate=pl.CostEstimate(flops=0, bytes_accessed=0, transcendentals=0),
        name="token_rows",
    )(lengths, expert_ids, dout)


def store_grad(grad, cols, rows, mine, outs):
    low = jnp.bfloat16
    if not rows:
        outs[0][:, cols] = grad.astype(low)
        return
    for c in range(grad.shape[0] // (2 * rows)):
        first = grad[2 * c * rows : (2 * c + 1) * rows]
        second = grad[(2 * c + 1) * rows : (2 * c + 2) * rows]
        outs[0][pl.ds(c * rows, rows), cols] = jnp.where(mine, first, second).astype(low)
        outs[1][pl.ds(c * rows, rows), cols] = jnp.where(mine, second, first).astype(low)


def shared_kernel(rows, experts, core_ref, h2, cb, w_in, w_down, w_router, shared_out, grad_h2, probs, *rest):
    f32, bf16 = jnp.float32, jnp.bfloat16
    *grads, gu, hs, dgu = rest
    tokens, width = h2.shape
    hidden = w_down.shape[0]
    mine = core_ref[0] == 0
    own = pl.ds(0, tokens)

    logits = jnp.dot(h2[...], w_router[...], preferred_element_type=f32)
    column = lax.broadcasted_iota(jnp.int32, logits.shape, 1)
    logits = jnp.where(column < experts - 1, logits, MASK_VALUE)
    ex = jnp.exp(logits - jnp.max(logits, axis=1, keepdims=True))
    probs[...] = ex / jnp.sum(ex, axis=1, keepdims=True)
    for start in range(0, 2 * hidden, 256):
        t = pl.ds(start, 256)
        gu[:, t] = jnp.dot(h2[...], w_in[:, t], preferred_element_type=f32)
    for start in range(0, hidden, 128):
        ta, tb = pl.ds(start, 128), pl.ds(hidden + start, 128)
        a, b = gu[:, ta], gu[:, tb]
        sig = jax.nn.sigmoid(a)
        silu = a * sig
        hs[:, ta] = (silu * b).astype(bf16)
        gu[:, ta] = b * (sig * (1.0 + a * (1.0 - sig)))
        gu[:, tb] = silu
    for start in range(0, hidden, 256):
        n = min(256, hidden - start)
        dhs = lax.dot_general(cb[own, :], w_down[pl.ds(start, n), :], NT, preferred_element_type=f32)
        for t in (pl.ds(start, n), pl.ds(hidden + start, n)):
            dgu[:, t] = (dhs * gu[:, t]).astype(bf16)
    for start in range(0, width, 256):
        t = pl.ds(start, 256)
        shared_out[:, t] = jnp.dot(hs[...], w_down[:, t], preferred_element_type=f32)
        grad_h2[:, t] = lax.dot_general(dgu[...], w_in[t, :], NT, preferred_element_type=f32)
    for start in range(0, 2 * hidden, 256):
        t = pl.ds(start, 256)
        grad = lax.dot_general(h2[...], dgu[:, t], TN, preferred_element_type=f32)
        store_grad(grad, t, rows, mine, grads)
    for start in range(0, hidden, 256):
        n = min(256, hidden - start)
        grad = lax.dot_general(cb[own, :], hs[:, pl.ds(start, n)], TN, preferred_element_type=f32)
        store_grad(grad, pl.ds(2 * hidden + start, n), rows, mine, grads)


def shared_expert(core, h2, cb, w_in, w_down, w_router, rows, experts):
    tokens, width = h2.shape
    hidden = w_down.shape[0]
    f32, bf16 = jnp.float32, jnp.bfloat16
    sd = jax.ShapeDtypeStruct
    vmem = pl.BlockSpec(memory_space=pltpu.VMEM)
    grads = [sd((width // 2, 3 * hidden), bf16)] * 2 if rows else [sd((width, 3 * hidden), bf16)]
    outs = [sd((tokens, width), f32), sd((tokens, width), f32), sd((tokens, w_router.shape[1]), f32)] + grads
    return pl.pallas_call(
        lambda *r: shared_kernel(rows, experts, *r),
        in_specs=[pl.BlockSpec(memory_space=pltpu.SMEM)] + [vmem] * 5,
        out_specs=[vmem] * len(outs),
        out_shape=outs,
        scratch_shapes=[pltpu.VMEM((tokens, 2 * hidden), f32), pltpu.VMEM((tokens, hidden), bf16), pltpu.VMEM((tokens, 2 * hidden), bf16)],
        compiler_params=pltpu.CompilerParams(vmem_limit_bytes=48 * 2**20),
        cost_estimate=pl.CostEstimate(flops=0, bytes_accessed=0, transcendentals=0),
        name="shared_expert",
    )(core, h2, cb, w_in, w_down, w_router)


def middle_kernel(experts, length_ref, home_a, home_b, home_c, grad_shared, probs, h2, w_router, x_mid, dout, gain, digits, grad_mid, da, small):
    f32, bf16 = jnp.float32, jnp.bfloat16
    tokens = x_mid.shape[0]
    own, table = pl.ds(0, tokens), pl.ds(tokens, 2 * experts)
    total = lambda r, c: home_a[r, c].astype(f32) + home_b[r, c].astype(f32) + home_c[r, c].astype(f32)
    dots = total(table, own)
    dots = dots[:experts] + dots[experts:]
    grad_probs = jnp.concatenate([dots, jnp.zeros((128 - experts, tokens), f32)], axis=0).T
    p = probs[...]
    low = (p * (grad_probs - jnp.sum(grad_probs * p, axis=1, keepdims=True))).astype(bf16)
    incoming = total(own, slice(None)) + grad_shared[...]
    incoming += lax.dot_general(low, w_router[...], NT, preferred_element_type=f32)
    mid = x_mid[...]
    inverse = lax.rsqrt(jnp.mean(mid * mid, axis=-1, keepdims=True) + NORM_EPS)
    scaled = mid * inverse
    column = lax.broadcasted_iota(jnp.int32, (tokens, 128), 1)
    small[...] = digits[...]
    small[:, pl.ds(0, 128)] += lax.dot_general(h2[...], low, TN, preferred_element_type=f32) + lax.dot_general(
        incoming * scaled, jnp.where(column == experts, 1.0, 0.0), TN,
        precision=lax.Precision.HIGHEST, preferred_element_type=f32,
    )
    inner = incoming * gain[...]
    back = inverse * (inner - scaled * jnp.mean(inner * scaled, axis=-1, keepdims=True))
    grad = dout[...].astype(f32) + back
    grad_mid[...] = grad
    live = lax.broadcasted_iota(jnp.int32, (tokens, 1), 0) < length_ref[0]
    da[...] = jnp.where(live, grad, 0.0).astype(bf16)


def middle_back(lengths, home, grad_shared, probs, h2, w_router, x_mid, dout, gain, digits, experts):
    tokens, width = x_mid.shape
    f32 = jnp.float32
    sd = jax.ShapeDtypeStruct
    vmem = pl.BlockSpec(memory_space=pltpu.VMEM)
    return pl.pallas_call(
        lambda *r: middle_kernel(experts, *r),
        in_specs=[pl.BlockSpec(memory_space=pltpu.SMEM)] + [vmem] * 11,
        out_specs=[vmem] * 3,
        out_shape=[sd((tokens, width), f32), sd((tokens, width), jnp.bfloat16), sd(digits.shape, f32)],
        compiler_params=pltpu.CompilerParams(vmem_limit_bytes=48 * 2**20),
        cost_estimate=pl.CostEstimate(flops=0, bytes_accessed=0, transcendentals=0),
        name="middle_back",
    )(lengths, *home, grad_shared, probs, h2, w_router, x_mid, dout, gain, digits)


def weight_grad_kernel(parts, bit, index_ref, lhs, rhs, keep, away):
    f32, bf16 = jnp.float32, jnp.bfloat16
    grad = lax.dot_general(lhs[0], rhs[0], TN, preferred_element_type=f32)
    mine = ((index_ref[0] >> bit) & 1) == 0
    rows = grad.shape[0] // parts
    at = 0
    for c in range(parts):
        if (c >> bit) & 1:
            continue
        other = c | (1 << bit)
        first = grad[c * rows : (c + 1) * rows]
        second = grad[other * rows : (other + 1) * rows]
        keep[pl.ds(at, rows), :] = jnp.where(mine, first, second).astype(bf16)
        away[pl.ds(at, rows), :] = jnp.where(mine, second, first).astype(bf16)
        at += rows


def weight_grad(index, lhs, rhs, expert, parts, bit):
    _, rows, m = lhs.shape
    n = rhs.shape[2]
    tile = 256
    return pl.pallas_call(
        lambda *r: weight_grad_kernel(parts, bit, *r),
        grid=(n // tile,),
        in_specs=[
            pl.BlockSpec(memory_space=pltpu.SMEM),
            pl.BlockSpec((1, rows, m), lambda i: (expert, 0, 0)),
            pl.BlockSpec((1, rows, tile), lambda i: (expert, 0, i)),
        ],
        out_specs=[pl.BlockSpec((m // 2, tile), lambda i: (0, i))] * 2,
        out_shape=[jax.ShapeDtypeStruct((m // 2, n), jnp.bfloat16)] * 2,
        compiler_params=pltpu.CompilerParams(vmem_limit_bytes=48 * 2**20),
        cost_estimate=pl.CostEstimate(flops=0, bytes_accessed=0, transcendentals=0),
        name="weight_grad",
    )(index, lhs, rhs)


def rope_tables(seq_slots):
    half_dim = HEAD_DIM // 2
    inv_freq = 1.0 / 10000.0 ** (jnp.arange(half_dim, dtype=jnp.float32) * 2.0 / HEAD_DIM)
    angles = jnp.arange(seq_slots, dtype=jnp.float32)[:, None] * inv_freq[None, :]
    cosine, sine = jnp.cos(angles), jnp.sin(angles)
    return jnp.concatenate([cosine, cosine], axis=1), jnp.concatenate([-sine, sine], axis=1)


def assemble_kernel(wide, *refs):
    *pieces, qkv, out = refs
    pair, pairs = 0, out.shape[1] // wide
    for piece, count in zip(pieces, (pairs // 2, pairs // 2, pairs - 2 * (pairs // 2))):
        step = piece.shape[1] // count
        for at in range(count):
            for kind in range(4):
                block = piece[:, at * step + kind * wide : at * step + (kind + 1) * wide]
                if kind < 3:
                    qkv[:, pl.ds((kind * pairs + pair) * wide, wide)] = block
                else:
                    out[:, pl.ds(pair * wide, wide)] = block
            pair += 1


def assemble(pieces, width):
    rows = pieces[0].shape[0]
    vmem = pl.BlockSpec(memory_space=pltpu.VMEM)
    return pl.pallas_call(
        lambda *r: assemble_kernel(2 * HEAD_DIM, *r),
        in_specs=[vmem] * len(pieces),
        out_specs=[vmem] * 2,
        out_shape=[jax.ShapeDtypeStruct((rows, n), jnp.float32) for n in (3 * width, width)],
        cost_estimate=pl.CostEstimate(flops=0, bytes_accessed=0, transcendentals=0),
        name="assemble",
    )(*pieces)


def final_kernel(chosen_ref, *refs):
    *terms, out = refs
    for i in range(len(terms) // 3):
        keep, came, last = (term[...].astype(jnp.float32) for term in terms[3 * i : 3 * i + 3])
        out[i] = keep + came + last


def final_sums(chosen, groups):
    rows, n = groups[0][2].shape
    cut = rows // 4
    half = lambda i: pl.BlockSpec((cut, n), lambda c, chosen, i=i: (chosen[i] * 4 + c, 0))
    row = pl.BlockSpec((cut, n), lambda c, chosen: (c, 0))
    return pl.pallas_call(
        final_kernel,
        grid_spec=pltpu.PrefetchScalarGridSpec(
            num_scalar_prefetch=1,
            grid=(4,),
            in_specs=[spec for i in range(len(groups)) for spec in (half(i), half(i), row)],
            out_specs=pl.BlockSpec((len(groups), cut, n), lambda c, chosen: (0, c, 0)),
        ),
        out_shape=jax.ShapeDtypeStruct((len(groups), rows, n), jnp.float32),
        compiler_params=pltpu.CompilerParams(vmem_limit_bytes=24 * 2**20),
        cost_estimate=pl.CostEstimate(flops=0, bytes_accessed=0, transcendentals=0),
        name="final_sums",
    )(chosen, *[term for group in groups for term in group])


def expert_sums(scatters):
    flat = lambda term: term.reshape(-1, term.shape[-1])
    if any(len(scatter.choices[0]) != 1 for scatter in scatters):
        return jnp.stack([scatter.finish() for scatter in scatters])
    chosen = jnp.stack([scatter.choices[0][0][1] for scatter in scatters]).astype(jnp.int32)
    return final_sums(chosen, [[flat(term) for term in scatter.terms] for scatter in scatters])


def swap_cores(values_in):
    owners = lax.axis_size("expert")
    return lax.ppermute(values_in, "expert", [(i, i ^ 1) for i in range(owners)])


def next_chip(values_in):
    owners = lax.axis_size("expert")
    return lax.ppermute(values_in, "expert", [(i, (i + 2) % owners) for i in range(owners)])


def axis_bits(name):
    return [(name, bit) for bit in range(lax.axis_size(name).bit_length() - 1)]


def row_bits():
    return axis_bits("dp")[::-1] + axis_bits("expert")[::-1]


def sum_terms(parts):
    summed = parts[0].astype(jnp.float32)
    for term in parts[1:]:
        summed = summed + term.astype(jnp.float32)
    return summed


def after(values_in, *earlier):
    return lax.optimization_barrier((values_in, earlier))[0]


def picked(term, choices):
    for dim, index in choices:
        term = lax.dynamic_index_in_dim(term, index, dim, keepdims=False)
    return term


class Scatter:
    def __init__(self, terms, open_bits, order):
        self.terms, self.choices = list(terms), [[] for _ in terms]
        self.open_bits, self.order = list(open_bits), list(order)

    def advance(self, *earlier):
        name, bit = self.order.pop(0)
        dim = self.open_bits.index((name, bit))
        mine = (lax.axis_index(name) >> bit) & 1
        terms = after(self.terms, *earlier) if earlier else self.terms
        away = sum_terms(
            [picked(term, made + [(dim, 1 - mine)]) for term, made in zip(terms, self.choices)]
        ).astype(terms[0].dtype)
        came = lax.ppermute(
            away, name, [(i, i ^ (1 << bit)) for i in range(lax.axis_size(name))]
        )
        self.choices = [made + [(dim, mine)] for made in self.choices] + [[]]
        self.terms.append(came)
        self.open_bits.pop(dim)
        return away

    def finish(self):
        while self.order:
            self.advance()
        return sum_terms([picked(term, made) for term, made in zip(self.terms, self.choices)])


def split_rows(part, bits):
    rows = part.shape[0] >> len(bits)
    return part.reshape((2,) * len(bits) + (rows, part.shape[1]))


def scatter_orders():
    core, *line = axis_bits("expert")
    plane = axis_bits("dp")
    return ([core] + plane + line, [core] + plane[::-1] + line, [core] + plane + line)


def per_device(
    layer_input,
    lengths,
    expert_ids,
    norm1,
    w_qkv,
    w_out,
    norm2,
    w_router,
    w_shared_in,
    w_shared_down,
    w_expert_in,
    w_expert_down,
    dout,
):
    seq_slots, width = layer_input.shape
    top_k = expert_ids.shape[1]
    experts = w_router.shape[1]
    local_experts = w_expert_in.shape[0]
    hidden_units = w_shared_down.shape[0]
    capacity = (seq_slots * top_k // (experts - 1) // 8 + 1) * 8
    live_col = (jnp.arange(seq_slots, dtype=jnp.int32) < lengths[0]).astype(jnp.float32)[:, None]
    cosine, sine = rope_tables(seq_slots)

    bits = row_bits()
    rows = width >> len(bits)
    rows = rows if rows % 8 == 0 else 0
    core = (lax.axis_index("expert") & 1).astype(jnp.int32)[None]
    orders = scatter_orders()
    chips = experts // local_experts // 2
    first_expert = (lax.axis_index("expert") * local_experts).astype(jnp.int32)[None]
    router_t = w_router.T

    def start_scatter(grads, order):
        if rows:
            terms = [split_rows(grads[0], bits[:-1]), split_rows(swap_cores(grads[1]), bits[:-1])]
            return Scatter(terms, bits[:-1], order[1:])
        return Scatter([split_rows(grads[0], bits)], bits, order)

    def run_step(step, h2_pair, grad_pair, kept, *earlier):
        sums, kept = expert_step(
            first_expert, after(h2_pair[0], *earlier), h2_pair[1], grad_pair[0], grad_pair[1],
            router_t, w_expert_in, w_expert_down, step, chips, capacity, kept,
        )
        parts.append(sums)
        return kept, sums[0]

    parts = []
    router_wide = jnp.pad(w_router, ((0, 0), (0, 128 - experts)))
    grad_table = token_rows(lengths, expert_ids, dout, experts)
    grad_here = (grad_table, swap_cores(grad_table))
    grad_next = next_chip(grad_table)
    counts_here = jnp.sum((grad_table[seq_slots:, :seq_slots] >= 0).astype(jnp.int32), axis=1)
    places = jnp.minimum(jnp.arange(width >> len(bits), dtype=jnp.int32), 30)
    digits = ((counts_here[None, :] >> places[:, None]) & 1).astype(jnp.float32)
    small_columns = -(-(2 * experts + 2) // 128) * 128
    digits = jnp.pad(
        jnp.tile(digits, (1 << len(bits), 1)),
        ((0, 0), (experts + 2, small_columns - 2 * experts - 2)),
    )
    h1_low, queries, keys_in, values_in, attended_low, log_norm, x_mid, h2_low = attention_forward(
        lengths, after(layer_input, grad_table), norm1[None, :], w_qkv, cosine, sine, w_out,
        norm2[None, :],
    )
    h2_here = (h2_low, swap_cores(h2_low))
    h2_next = next_chip(h2_low)
    grad_next = after(grad_next, h2_low)
    grad_other = swap_cores(grad_next)
    grad_ahead = next_chip(grad_next)
    kept, done = run_step(0, h2_here, grad_here, None, grad_next)
    shared_out, grad_shared, router_probs, *shared_grads = shared_expert(
        core, after(h2_low, done), grad_table, w_shared_in, w_shared_down, router_wide, rows, experts
    )
    fence = shared_out
    shared_away = []
    swapped = []
    shared_scatter = None
    travelling = None
    for step in range(1, chips):
        h2_next, grad_next = after(h2_next, fence), after(grad_next, fence)
        pair_h2 = (h2_next, swap_cores(h2_next))
        pair_grad = (grad_next, grad_other)
        if shared_scatter is None:
            ready = (fence, grad_ahead, pair_h2[1], grad_other)
            shared_scatter = start_scatter(after(shared_grads, *ready), orders[0])
            swapped.append(swap_cores(after(parts[0][3], *ready)))
        earlier = [] if travelling is None else [travelling]
        earlier += shared_away
        if step + 1 < chips:
            h2_next = next_chip(h2_next)
            grad_next = after(grad_ahead, fence)
            grad_other = swap_cores(grad_next)
            if step + 2 < chips:
                grad_ahead = next_chip(grad_next)
        kept, fence = run_step(step, pair_h2, pair_grad, kept, *earlier)
        mine, theirs = parts[step][:2]
        if step + 1 < chips:
            theirs = after(theirs, h2_next, grad_ahead)
        theirs = after(theirs, *swapped)
        if step == 2:
            first_routed = parts[1][2].astype(jnp.float32) + swapped[1].astype(jnp.float32)
            first_routed = first_routed.astype(jnp.bfloat16)
            theirs = after(theirs, first_routed)
        swapped.append(swap_cores(after(parts[step][3], theirs)))
        if shared_away:
            theirs = after(theirs, shared_scatter.terms[-1])
        if shared_scatter.order[0][0] == "dp":
            shared_away = [shared_scatter.advance(fence)]
            theirs = after(theirs, *shared_away)
        if travelling is None:
            total = mine.astype(jnp.float32) + swap_cores(theirs).astype(jnp.float32)
        else:
            came = next_chip(travelling)
            total = (
                mine.astype(jnp.float32)
                + swap_cores(after(theirs, came)).astype(jnp.float32)
                + came.astype(jnp.float32)
            )
        travelling = total.astype(mine.dtype)

    home_hop = next_chip(travelling)
    rows_held, grad_result, expert_hidden, grad_expert_gu = kept

    plane = axis_bits("dp")
    plane_index = lax.axis_index("dp").astype(jnp.int32)[None]

    def expert_grads(lhs, rhs, expert):
        order = plane if expert % 2 == 0 else plane[::-1]
        return order, weight_grad(
            plane_index, lhs, rhs, expert, 1 << len(plane), order[0][1]
        )

    def plane_scatter(order, grads, *earlier):
        name, bit = order[0]
        keep, away = after(grads, *earlier) if earlier else grads
        came = lax.ppermute(
            away, name, [(i, i ^ (1 << bit)) for i in range(lax.axis_size(name))]
        )
        open_bits = [place for place in plane[::-1] if place != order[0]]
        terms = [split_rows(piece, open_bits) for piece in (keep, came)]
        return Scatter(terms, open_bits, order[1:])

    fence = [travelling, shared_scatter.terms[-1]]
    down_parts, in_parts = [], []
    for i in range(local_experts):
        down_parts.append(expert_grads(after(expert_hidden, *fence), grad_result, i))
        fence = down_parts[-1][1]
    down_scatters = [plane_scatter(*part) for part in down_parts]
    for i in range(local_experts):
        in_parts.append(expert_grads(after(rows_held, *fence), grad_expert_gu, i))
        fence = in_parts[-1][1]

    mine, theirs = parts[0][:2]
    own_home = (mine, swap_cores(after(theirs, travelling)))
    out_order = list(range(1, chips)) + [0]

    def add_routed(index, came, *earlier):
        mine, theirs = after((parts[out_order[index]][2], swapped[out_order[index]]), *earlier)
        total = mine.astype(jnp.float32) + theirs.astype(jnp.float32)
        return total if came is None else total + came.astype(jnp.float32)

    routed = first_routed if chips > 2 else add_routed(0, None, travelling).astype(jnp.bfloat16)
    landed = list(fence) + [home_hop, own_home[1], swapped[-1], routed]
    landed += [scatter.terms[-1] for scatter in down_scatters]
    in_scatters = [plane_scatter(*part, *landed) for part in in_parts]
    out_hop = next_chip(after(routed, *landed))
    fence = landed
    for scatter in down_scatters:
        fence = [scatter.advance(*fence)]
    home = after((*own_home, home_hop), *fence)
    grad_mid, grad_attn_branch, small = middle_back(
        lengths, home, grad_shared, router_probs, h2_low, router_wide, x_mid, dout, norm2[None, :],
        digits, experts,
    )

    pairs = width // (2 * HEAD_DIM)
    half = (pairs - 1) // 2
    cuts = (0, half, 2 * half, pairs)
    running = None
    columns = []
    fence = [grad_attn_branch]
    for index, (first, last) in enumerate(zip(cuts[:-1], cuts[1:])):
        tail = None
        if last == pairs:
            tail = (experts, (layer_input, norm1[None, :], grad_mid, small))
        *grads, running = attention_backward(
            lengths, core, after(grad_attn_branch, *fence), w_out, queries, keys_in, values_in,
            log_norm, cosine, sine, h1_low, attended_low, w_qkv, running, first, last - first, rows,
            tail,
        )
        fence = [running]
        columns.append(grads)
        if index == 0:
            routed = add_routed(1, out_hop, running).astype(jnp.bfloat16)
            out_hop = next_chip(routed)
            fence.append(routed)
    grad_input = running
    landed = [running, out_hop]
    landed += [scatter.terms[-1] for scatter in in_scatters + down_scatters]
    scatters = []
    fence = landed
    for grads, order in zip(columns, orders):
        scatters.append(start_scatter(after(grads, *landed, *fence), order))
    hops = 2
    first_cols, second_cols, third_cols = scatters
    plan = [first_cols, second_cols, None, third_cols, shared_scatter, first_cols, second_cols, third_cols, shared_scatter, None, first_cols, second_cols, third_cols, in_scatters[0], in_scatters[1], first_cols, second_cols, third_cols]
    for position, scatter in enumerate(plan):
        if position == 5:
            for held in down_scatters:
                held.terms = after(held.terms, *fence)
            expert_down_sum = expert_sums(down_scatters)
            fence = fence + [expert_down_sum]
        if scatter is not None:
            if scatter.order:
                fence = [scatter.advance(*fence)]
        elif hops < chips:
            routed = add_routed(hops, out_hop, *fence)
            hops += 1
            if hops < chips:
                out_hop = next_chip(routed.astype(jnp.bfloat16))
            fence = [routed]
    for hops in range(hops, chips):
        routed = add_routed(hops, out_hop, *fence)
        out_hop = next_chip(routed.astype(jnp.bfloat16))
    for scatter in in_scatters + [shared_scatter]:
        scatter.terms = after(scatter.terms, *fence)
    result = (x_mid + live_col * (shared_out + routed)).astype(jnp.bfloat16)
    shared_sum = shared_scatter.finish()
    expert_in_sum = expert_sums(in_scatters)
    pieces = [scatter.finish() for scatter in scatters]
    qkv_sum, out_sum = assemble(pieces, width)
    small_sum = pieces[-1][:, 8 * HEAD_DIM :]
    counts = jnp.sum(
        small_sum[:, experts + 2 : 2 * experts + 2] * (1 << places).astype(jnp.float32)[:, None],
        axis=0,
    )
    return (
        result,
        grad_input,
        small_sum[:, experts + 1],
        qkv_sum,
        out_sum,
        small_sum[:, experts],
        small_sum[:, :experts],
        shared_sum[:, : 2 * hidden_units],
        shared_sum[:, 2 * hidden_units :].T,
        expert_in_sum,
        expert_down_sum,
        counts.astype(jnp.int32),
    )


def solution(mesh):
    return jax.shard_map(
        per_device,
        mesh=mesh,
        in_specs=(
            P(("dp", "expert"), None),
            P(("dp", "expert")),
            P(("dp", "expert"), None),
            P(),
            P(),
            P(),
            P(),
            P(),
            P(),
            P(),
            P("expert", None, None),
            P("expert", None, None),
            P(("dp", "expert"), None),
        ),
        out_specs=(
            P(("dp", "expert"), None),
            P(("dp", "expert"), None),
            P(("dp", "expert")),
            P(("dp", "expert"), None),
            P(("dp", "expert"), None),
            P(("dp", "expert")),
            P(("dp", "expert"), None),
            P(("dp", "expert"), None),
            P(None, ("dp", "expert")),
            P("expert", "dp", None),
            P("expert", "dp", None),
            P(),
        ),
        check_vma=False,
    )
```
